32 devices in a mesh: ulysses: 4 (over y, x), blk: 8 (over z, core).
Axes of the slice: x: 2, y: 2, z: 4, core: 2. Of those that a mesh axis runs over, the one named last changes fastest.
Arguments:
- inputs: bfloat16 [2, 2048, 1024], P(None, ('blk', 'ulysses')), may hold values from -16 to 16
- v_first: bfloat16 [2, 2048, 1024], P(None, ('blk', 'ulysses')), may hold values from -6 to 6
- grad_out: bfloat16 [2, 2048, 1024], P(None, ('blk', 'ulysses')), may hold values from -6 to 6
- positions: int32 [2, 2048], P(None, ('blk', 'ulysses')), may hold values from 0 to 2047, as said below
- segments: int32 [2, 2048], replicated, may hold values from 0 to 1, as said below
- w_query: bfloat16 [1024, 1024], P(('ulysses', 'blk')), may hold values from -0.1875 to 0.1875
- w_key: bfloat16 [1024, 1024], P(('ulysses', 'blk')), may hold values from -0.1875 to 0.1875
- w_value: bfloat16 [1024, 1024], P(('ulysses', 'blk')), may hold values from -0.1875 to 0.1875
- w_out: bfloat16 [1024, 1024], P(('ulysses', 'blk')), may hold values from -1.5 to 1.5
- w_gate: bfloat16 [1024, 2816], P(('ulysses', 'blk')), may hold values from -0.1875 to 0.1875
- w_up: bfloat16 [1024, 2816], P(('ulysses', 'blk')), may hold values from -0.1875 to 0.1875
- w_down: bfloat16 [2816, 1024], P(('ulysses', 'blk')), may hold values from -0.109375 to 0.109375
- gain_attn: bfloat16 [1024], P(('ulysses', 'blk')), may hold values from 0.5 to 1.5
- gain_ffn: bfloat16 [1024], P(('ulysses', 'blk')), may hold values from 0.5 to 1.5
Outputs:
- output: bfloat16 [2, 2048, 1024], P(None, ('blk', 'ulysses'))
- grad_inputs: bfloat16 [2, 2048, 1024], P(None, ('blk', 'ulysses'))
- grad_v_first: bfloat16 [2, 2048, 1024], P(None, ('blk', 'ulysses'))
- grad_w_query: float32 [1024, 1024], P(('ulysses', 'blk'))
- grad_w_key: float32 [1024, 1024], P(('ulysses', 'blk'))
- grad_w_value: float32 [1024, 1024], P(('ulysses', 'blk'))
- grad_w_out: float32 [1024, 1024], P(('ulysses', 'blk'))
- grad_w_gate: float32 [1024, 2816], P(('ulysses', 'blk'))
- grad_w_up: float32 [1024, 2816], P(('ulysses', 'blk'))
- grad_w_down: float32 [2816, 1024], P(('ulysses', 'blk'))
- grad_gain_attn: float32 [1024], P(('ulysses', 'blk'))
- grad_gain_ffn: float32 [1024], P(('ulysses', 'blk'))
- stats: float32 [3], replicated
The draws below stay inside these ranges and needn't reach their ends.
Inputs may be any that keep to these rules, and one draw needn't show every extreme that they name: `segments`: each sequence holds one document of 2048 tokens or two, the second starting between 512 and 1536; some sequence holds one. `positions`: the token's distance from the first token of its document.
All inputs are finite; a program needn't handle non-finite values.
Results may differ from the reference program's by a relative error of at most 0.017.
Values may be sent and summed in bfloat16 or wider, within the bound.
A program may use at most 192 MiB of HBM per device.

```python
import math
import jax
import jax.numpy as jnp
from jax import lax

D = 1024
HEADS = 16
HD = 64
FF = 2816
NSEQ = 2
SEQ_DEV = 64
SEQ = 2048
N_ULYSSES = 4


def layout_docs(key):
    whole_key = jax.random.fold_in(key, 11)
    split_key = jax.random.fold_in(key, 12)
    whole_row = jax.random.randint(whole_key, (), 0, NSEQ)
    cut_points = jax.random.randint(split_key, (NSEQ,), SEQ // 4, 3 * SEQ // 4)
    places = jnp.arange(SEQ, dtype=jnp.int32)[None, :]
    row_index = jnp.arange(NSEQ, dtype=jnp.int32)[:, None]
    cut_points = jnp.where(row_index == whole_row, SEQ, cut_points[:, None])
    segment_ids = (places >= cut_points).astype(jnp.int32)
    offsets = jnp.where(segment_ids == 1, cut_points, 0)
    return (segment_ids, places - offsets)


def draw_segments(key, part):
    return layout_docs(key)[0]


def draw_positions(key, part):
    return layout_docs(key)[1]


def draw_inputs(key, part):
    noise_key = jax.random.fold_in(key, 21)
    group = jnp.arange(SEQ, dtype=jnp.int32) // SEQ_DEV
    lane = (group % N_ULYSSES).astype(jnp.float32) / (N_ULYSSES - 1)
    lane = lane[None, :, None]
    noise = jnp.clip(jax.random.normal(noise_key, (NSEQ, SEQ, D), jnp.float32), -4.0, 4.0)
    return (noise * (1.0 + 3.0 * lane)).astype(jnp.bfloat16)


def shard_levels(rng, shape, shards, low, largest):
    loudness, own = 1.0, jax.random.fold_in(rng, 6)
    for position, blocks in shards:
        draws = jnp.exp(jax.random.uniform(jax.random.fold_in(own, position), (blocks,), jnp.float32, low / len(shards), largest / len(shards)))
        loudness = loudness * jnp.repeat(draws, shape[position] // blocks).reshape([-1 if axis == position else 1 for axis in range(len(shape))])
    return loudness


def gaussian(own_key, dims, scale, reach, cuts=(), kind=jnp.bfloat16):
    factor_of = shard_levels(own_key, dims, cuts, -0.22, 0.18) if cuts else 1.0
    entries = jax.random.normal(own_key, dims, jnp.float32) * scale * factor_of
    return jnp.minimum(jnp.maximum(entries, -reach), reach).astype(kind)


def setup_inputs(seed: int = 0) -> dict:
    splits = jax.random.split(jax.random.key(seed), 15)
    inputs = draw_inputs(jax.random.fold_in(splits[14], 71), 0)
    v_first = gaussian(splits[1], (NSEQ, SEQ, D), 1.0, 6.0, ((1, 32),))
    grad_out = gaussian(splits[2], (NSEQ, SEQ, D), 1.0, 6.0, ((1, 32),))
    positions = draw_positions(jax.random.fold_in(splits[14], 71), 0)
    segments = draw_segments(jax.random.fold_in(splits[14], 71), 0)
    w_query = gaussian(splits[5], (D, D), D ** -0.5, 0.1875, ((0, 32),))
    w_key = gaussian(splits[6], (D, D), D ** -0.5, 0.1875, ((0, 32),))
    w_value = gaussian(splits[7], (D, D), D ** -0.5, 0.1875, ((0, 32),))
    w_out = gaussian(splits[8], (D, D), (D // 64) ** -0.5, 1.5, ((0, 32),))
    w_gate = gaussian(splits[9], (D, FF), D ** -0.5, 0.1875, ((0, 32),))
    w_up = gaussian(splits[10], (D, FF), D ** -0.5, 0.1875, ((0, 32),))
    w_down = gaussian(splits[11], (FF, D), FF ** -0.5, 0.109375, ((0, 32),))
    gain_attn = jnp.clip(1.0 + 0.1 * jax.random.normal(splits[12], (D,), jnp.float32), 0.5, 1.5).astype(jnp.bfloat16)
    gain_ffn = jnp.clip(1.0 + 0.1 * jax.random.normal(splits[13], (D,), jnp.float32), 0.5, 1.5).astype(jnp.bfloat16)
    return dict(inputs=inputs, v_first=v_first, grad_out=grad_out, positions=positions, segments=segments, w_query=w_query, w_key=w_key, w_value=w_value, w_out=w_out, w_gate=w_gate, w_up=w_up, w_down=w_down, gain_attn=gain_attn, gain_ffn=gain_ffn)


@jax.custom_vjp
def low(v):
    return lax.optimization_barrier(v.astype(jnp.bfloat16)).astype(jnp.float32)

@jax.custom_vjp
def low_back(v):
    return v

def low_keep(v):
    return (low(v), None)

def low_pass(kept, grad):
    return (grad,)

def back_keep(v):
    return (v, None)

def back_low(kept, grad):
    return (low(grad),)
low.defvjp(low_keep, low_pass)
low_back.defvjp(back_keep, back_low)
epsilon = 1e-06
rope_base = 10000.0
neg_big = -1e+30

def matmul_high(left, right):
    return jnp.dot(left, right, precision=lax.Precision.HIGHEST, preferred_element_type=jnp.float32)

def norm_rows(values, gain):
    return values * lax.rsqrt(lax.optimization_barrier(jnp.mean(values * values, axis=-1, keepdims=True)) + epsilon) * gain

def rotate(values, positions):
    half_dim = HD // 2
    inverse = rope_base ** (-2.0 * jnp.arange(half_dim, dtype=jnp.float32) / HD)
    angles = positions.astype(jnp.float32)[:, :, None] * inverse
    cosine = jnp.cos(angles)[:, :, None, :]
    sine = jnp.sin(angles)[:, :, None, :]
    first = values[..., :half_dim]
    second = values[..., half_dim:]
    return jnp.concatenate([first * cosine - second * sine, second * cosine + first * sine], axis=-1)

def attend_sequence(query, key_all, value_all, seg_row):
    block_rows = math.gcd(SEQ, 512)
    block_count = SEQ // block_rows
    blocks = query.reshape(block_count, block_rows, HEADS, HD)
    starts = jnp.arange(block_count, dtype=jnp.int32) * block_rows
    key_place = jnp.arange(SEQ, dtype=jnp.int32)
    score_scale = HD ** (-0.5)

    @jax.checkpoint
    def attend_block(entry):
        query_block, first_row = entry
        scores = low_back(jnp.einsum('qhd,khd->hqk', query_block, key_all, precision=lax.Precision.HIGHEST) * score_scale)
        query_place = first_row + jnp.arange(block_rows, dtype=jnp.int32)
        seg_query = lax.dynamic_slice_in_dim(seg_row, first_row, block_rows, 0)
        allowed = (key_place[None, :] <= query_place[:, None]) & (seg_query[:, None] == seg_row[None, :])
        masked = jnp.where(allowed[None], scores, neg_big)
        shifted = jnp.exp(masked - lax.optimization_barrier(jnp.max(masked, axis=-1, keepdims=True)))
        probs = shifted / lax.optimization_barrier(jnp.sum(shifted, axis=-1, keepdims=True))
        return jnp.einsum('hqk,khd->qhd', low(probs), value_all, precision=lax.Precision.HIGHEST)
    mixed = lax.map(attend_block, (blocks, starts))
    return mixed.reshape(SEQ, HEADS, HD)

def attend_item(entry):
    return attend_sequence(entry[0], entry[1], entry[2], entry[3])

def root_mean(values):
    return jnp.sqrt(jnp.mean(values * values))

def layer_forward(inputs, v_first, w_query, w_key, w_value, w_out, w_gate, w_up, w_down, gain_attn, gain_ffn, positions, segments):
    flat = inputs.reshape(NSEQ * SEQ, D)
    normed = low(norm_rows(flat, gain_attn))
    query_raw = low_back(matmul_high(normed, w_query)).reshape(NSEQ, SEQ, HEADS, HD)
    query = low_back(low(rotate(query_raw, positions)))
    key_raw = low_back(matmul_high(normed, w_key)).reshape(NSEQ, SEQ, HEADS, HD)
    key = low_back(low(rotate(key_raw, positions)))
    value_mix = 0.5 * matmul_high(normed, w_value) + 0.5 * v_first.reshape(NSEQ * SEQ, D)
    value = low_back(low(value_mix)).reshape(NSEQ, SEQ, HEADS, HD)
    attended = lax.map(attend_item, (query, key, value, segments))
    mixed = low_back(low(attended.reshape(NSEQ * SEQ, D)))
    attn_branch = low_back(matmul_high(mixed, w_out))
    hidden = flat + attn_branch
    normed_ffn = low(norm_rows(hidden, gain_ffn))
    gate = low_back(matmul_high(normed_ffn, w_gate))
    up_proj = low_back(matmul_high(normed_ffn, w_up))
    act = low(gate / (1.0 + jnp.exp(-gate)) * up_proj)
    ffn_branch = low_back(matmul_high(act, w_down))
    output = hidden + ffn_branch
    statistics = jnp.stack([root_mean(flat), root_mean(attn_branch), root_mean(output)])
    return (output.reshape(NSEQ, SEQ, D), statistics)

def reference(inputs, v_first, grad_out, positions, segments, w_query, w_key, w_value, w_out, w_gate, w_up, w_down, gain_attn, gain_ffn):
    floats = tuple((member.astype(jnp.float32) for member in (inputs, v_first, w_query, w_key, w_value, w_out, w_gate, w_up, w_down, gain_attn, gain_ffn)))

    def wrapped(inputs_f, v_first_f, query_f, key_f, value_f, out_f, gate_f, up_f, down_f, gain_a, gain_f):
        return layer_forward(inputs_f, v_first_f, query_f, key_f, value_f, out_f, gate_f, up_f, down_f, gain_a, gain_f, positions, segments)
    output, pullback, statistics = jax.vjp(wrapped, *floats, has_aux=True)
    gradients = pullback(grad_out.astype(jnp.float32))
    return (output.astype(jnp.bfloat16), gradients[0].astype(jnp.bfloat16), gradients[1].astype(jnp.bfloat16), gradients[2], gradients[3], gradients[4], gradients[5], gradients[6], gradients[7], gradients[8], gradients[9], gradients[10], statistics)
```

```python
import functools

import jax
import jax.numpy as jnp
from jax import lax
from jax.experimental import pallas as pl
from jax.experimental.pallas import tpu as pltpu
from jax.sharding import PartitionSpec as P

HEADS = 16
HD = 64


epsilon = 1e-06
rope_base = 10000.0
neg_big = -1e30


def norm_rows(values, gain):
    factor = lax.rsqrt(jnp.mean(values * values, axis=-1, keepdims=True) + epsilon)
    hatted = values * factor
    return (hatted * gain, hatted, factor)


def norm_back(grad_normed, hatted, factor, gain):
    scaled = grad_normed * gain
    inner = jnp.mean(scaled * hatted, axis=-1, keepdims=True)
    return (factor * (scaled - hatted * inner), jnp.sum(grad_normed * hatted, axis=(0, 1)))


def rope_tables(positions):
    half_dim = HD // 2
    inverse = rope_base ** (-2.0 * jnp.arange(half_dim, dtype=jnp.float32) / HD)
    angles = positions.astype(jnp.float32)[:, :, None] * inverse
    return (jnp.cos(angles)[:, :, None, :], jnp.sin(angles)[:, :, None, :])


def rotate(values, cosine, sine, forward_turn):
    shaped = values.reshape(values.shape[0], values.shape[1], HEADS, HD)
    half_dim = HD // 2
    first = shaped[..., :half_dim]
    second = shaped[..., half_dim:]
    if forward_turn:
        turned = jnp.concatenate(
            [first * cosine - second * sine, second * cosine + first * sine], axis=-1
        )
    else:
        turned = jnp.concatenate(
            [first * cosine + second * sine, second * cosine - first * sine], axis=-1
        )
    return turned.reshape(values.shape)


def project(activations, weight):
    return jnp.einsum("std,de->ste", activations, weight, preferred_element_type=jnp.float32)


def project_back(gradient, weight):
    return jnp.einsum("ste,de->std", gradient, weight, preferred_element_type=jnp.float32)


def weight_grad(activations, gradient):
    return jnp.einsum("std,ste->de", activations, gradient, preferred_element_type=jnp.float32)


def allowed_mask(segments, query_first, query_count, key_first, key_count):
    seg_query = lax.dynamic_slice_in_dim(segments, query_first, query_count, 1)
    seg_key = lax.dynamic_slice_in_dim(segments, key_first, key_count, 1)
    query_place = query_first + jnp.arange(query_count, dtype=jnp.int32)
    key_place = key_first + jnp.arange(key_count, dtype=jnp.int32)
    causal = key_place[None, :] <= query_place[:, None]
    same_doc = seg_query[:, :, None] == seg_key[:, None, :]
    return (causal[None] & same_doc)[:, :, None, :]


def over_blocks(step_fn, running, pieces, block_rows):
    row_count = pieces[0].shape[1]
    block_count = row_count // block_rows
    stacked = tuple(
        (
            jnp.moveaxis(
                member.reshape((member.shape[0], block_count, block_rows) + member.shape[2:]), 1, 0
            )
            for member in pieces
        )
    )
    offsets = block_rows * jnp.arange(block_count, dtype=jnp.int32)

    def advance(current, scan_entry):
        return (step_fn(current, scan_entry[:-1], scan_entry[-1]), None)

    running, unused = lax.scan(advance, running, stacked + (offsets,))
    return running


def add_rows(buffer, update, first_row):
    current = lax.dynamic_slice_in_dim(buffer, first_row, update.shape[1], 1)
    return lax.dynamic_update_slice_in_dim(buffer, current + update, first_row, 1)


def unchanged(running):
    return running


def local(
    inputs,
    v_first,
    grad_out,
    positions,
    segments,
    w_query,
    w_key,
    w_value,
    w_out,
    w_gate,
    w_up,
    w_down,
    gain_attn,
    gain_ffn,
):
    gathered = (
        lax.all_gather(w_query, ("ulysses", "blk"), axis=0, tiled=True),
        lax.all_gather(w_key, ("ulysses", "blk"), axis=0, tiled=True),
        lax.all_gather(w_value, ("ulysses", "blk"), axis=0, tiled=True),
        lax.all_gather(w_out, ("ulysses", "blk"), axis=0, tiled=True),
        lax.all_gather(w_gate, ("ulysses", "blk"), axis=0, tiled=True),
        lax.all_gather(w_up, ("ulysses", "blk"), axis=0, tiled=True),
        lax.all_gather(w_down, ("ulysses", "blk"), axis=0, tiled=True),
        lax.all_gather(gain_attn, ("ulysses", "blk"), axis=0, tiled=True),
        lax.all_gather(gain_ffn, ("ulysses", "blk"), axis=0, tiled=True),
    )
    (
        full_query,
        full_key,
        full_value,
        full_out,
        full_gate,
        full_up,
        full_down,
        full_gain_attn,
        full_gain_ffn,
    ) = gathered
    score_scale = HD ** (-0.5)
    residual = inputs.astype(jnp.float32)
    normed_f, hatted_attn, factor_attn = norm_rows(residual, full_gain_attn.astype(jnp.float32))
    normed = normed_f.astype(jnp.bfloat16)
    cosine, sine = rope_tables(positions)
    query_tok = rotate(project(normed, full_query), cosine, sine, True).astype(jnp.bfloat16)
    key_tok = rotate(project(normed, full_key), cosine, sine, True).astype(jnp.bfloat16)
    value_tok = (0.5 * project(normed, full_value) + 0.5 * v_first.astype(jnp.float32)).astype(
        jnp.bfloat16
    )
    query_head, key_head, value_head = (
        lax.all_to_all(query_tok, "ulysses", split_axis=2, concat_axis=1, tiled=True),
        lax.all_to_all(key_tok, "ulysses", split_axis=2, concat_axis=1, tiled=True),
        lax.all_to_all(value_tok, "ulysses", split_axis=2, concat_axis=1, tiled=True),
    )
    seq_count, block_rows, width = query_head.shape
    heads_local = width // HD
    query_start = lax.axis_index("blk") * block_rows
    full_rows = block_rows * lax.axis_size("blk")

    def split_heads(values):
        return values.reshape(values.shape[0], values.shape[1], heads_local, HD)

    query_four = split_heads(query_head)

    def attend_rows(running, pieces, first_row):
        key_rows, value_rows = pieces
        key_count = key_rows.shape[1]

        def attend_compute(current):
            best, total, accum = current
            allowed = allowed_mask(segments, query_start, block_rows, first_row, key_count)
            scores = (
                jnp.einsum(
                    "sqhd,skhd->sqhk",
                    query_four,
                    split_heads(key_rows),
                    preferred_element_type=jnp.float32,
                )
                * score_scale
            )
            masked = jnp.where(allowed, scores, neg_big)
            new_best = jnp.maximum(best, jnp.max(masked, axis=-1))
            weights = jnp.where(allowed, jnp.exp(masked - new_best[..., None]), 0.0)
            rescale = jnp.exp(best - new_best)
            total = total * rescale + jnp.sum(weights, axis=-1)
            accum = accum * rescale[..., None] + jnp.einsum(
                "sqhk,skhd->sqhd",
                weights.astype(jnp.bfloat16),
                split_heads(value_rows),
                preferred_element_type=jnp.float32,
            )
            return (new_best, total, accum)

        return lax.cond(
            first_row <= query_start + block_rows - 1, attend_compute, unchanged, running
        )

    stat_zeros = jnp.zeros((seq_count, block_rows, heads_local), jnp.float32)
    head_zeros = jnp.zeros((seq_count, block_rows, heads_local, HD), jnp.float32)
    initial = (
        jnp.full((seq_count, block_rows, heads_local), neg_big, jnp.float32),
        stat_zeros,
        head_zeros,
    )
    best, total, accum = over_blocks(
        attend_rows,
        initial,
        (
            lax.all_gather(key_head, "blk", axis=1, tiled=True),
            lax.all_gather(value_head, "blk", axis=1, tiled=True),
        ),
        block_rows,
    )
    log_total = best + jnp.log(total)
    attn_heads = accum / total[..., None]
    attn_low = attn_heads.reshape(seq_count, block_rows, width).astype(jnp.bfloat16)
    mixed = lax.all_to_all(attn_low, "ulysses", split_axis=1, concat_axis=2, tiled=True)
    attn_branch = project(mixed, full_out)
    hidden = residual + attn_branch
    normed_ffn_f, hatted_ffn, factor_ffn = norm_rows(hidden, full_gain_ffn.astype(jnp.float32))
    normed_ffn = normed_ffn_f.astype(jnp.bfloat16)
    gate = project(normed_ffn, full_gate)
    up_proj = project(normed_ffn, full_up)
    sigmoid_gate = jax.nn.sigmoid(gate)
    silu_gate = gate * sigmoid_gate
    act = (silu_gate * up_proj).astype(jnp.bfloat16)
    ffn_branch = project(act, full_down)
    output_f = hidden + ffn_branch
    output = output_f.astype(jnp.bfloat16)
    squares = lax.psum(
        (
            jnp.sum(residual * residual),
            jnp.sum(attn_branch * attn_branch),
            jnp.sum(output_f * output_f),
        ),
        ("ulysses", "blk"),
    )
    entry_count = residual.size * lax.axis_size("ulysses") * lax.axis_size("blk")
    statistics = jnp.sqrt(jnp.stack(squares) / entry_count)
    again = (
        lax.all_gather(w_query, ("ulysses", "blk"), axis=0, tiled=True),
        lax.all_gather(w_key, ("ulysses", "blk"), axis=0, tiled=True),
        lax.all_gather(w_value, ("ulysses", "blk"), axis=0, tiled=True),
        lax.all_gather(w_out, ("ulysses", "blk"), axis=0, tiled=True),
        lax.all_gather(w_gate, ("ulysses", "blk"), axis=0, tiled=True),
        lax.all_gather(w_up, ("ulysses", "blk"), axis=0, tiled=True),
        lax.all_gather(w_down, ("ulysses", "blk"), axis=0, tiled=True),
        lax.all_gather(gain_attn, ("ulysses", "blk"), axis=0, tiled=True),
        lax.all_gather(gain_ffn, ("ulysses", "blk"), axis=0, tiled=True),
    )
    (
        back_query,
        back_key,
        back_value,
        back_out,
        back_gate,
        back_up,
        back_down,
        back_gain_attn,
        back_gain_ffn,
    ) = again
    grad_act = project_back(grad_out, back_down)
    grad_gate = (grad_act * up_proj * sigmoid_gate * (1.0 + gate * (1.0 - sigmoid_gate))).astype(
        jnp.bfloat16
    )
    grad_up = (grad_act * silu_gate).astype(jnp.bfloat16)
    grad_normed_ffn = project_back(grad_gate, back_gate) + project_back(grad_up, back_up)
    grad_ffn_norm, grad_gain_ffn = norm_back(
        grad_normed_ffn, hatted_ffn, factor_ffn, back_gain_ffn.astype(jnp.float32)
    )
    grad_hidden = grad_out.astype(jnp.float32) + grad_ffn_norm
    grad_branch = grad_hidden.astype(jnp.bfloat16)
    grad_mixed = project_back(grad_branch, back_out).astype(jnp.bfloat16)
    dout_head = lax.all_to_all(grad_mixed, "ulysses", split_axis=2, concat_axis=1, tiled=True)
    dout_four = split_heads(dout_head)
    row_dot = jnp.sum(dout_four.astype(jnp.float32) * attn_heads, axis=-1)

    def grad_rows(running, pieces, first_row):
        key_rows, value_rows = pieces
        key_count = key_rows.shape[1]

        def grad_compute(current):
            grad_query, grad_keys, grad_values = current
            key_part = split_heads(key_rows)
            allowed = allowed_mask(segments, query_start, block_rows, first_row, key_count)
            scores = (
                jnp.einsum(
                    "sqhd,skhd->sqhk", query_four, key_part, preferred_element_type=jnp.float32
                )
                * score_scale
            )
            probs = jnp.where(allowed, jnp.exp(scores - log_total[..., None]), 0.0)
            prob_grad = jnp.einsum(
                "sqhd,skhd->sqhk",
                dout_four,
                split_heads(value_rows),
                preferred_element_type=jnp.float32,
            )
            score_grad = (probs * (prob_grad - row_dot[..., None])).astype(jnp.bfloat16)
            grad_query = (
                grad_query
                + jnp.einsum(
                    "sqhk,skhd->sqhd", score_grad, key_part, preferred_element_type=jnp.float32
                )
                * score_scale
            )
            key_term = (
                jnp.einsum(
                    "sqhk,sqhd->skhd", score_grad, query_four, preferred_element_type=jnp.float32
                )
                * score_scale
            )
            value_term = jnp.einsum(
                "sqhk,sqhd->skhd",
                probs.astype(jnp.bfloat16),
                dout_four,
                preferred_element_type=jnp.float32,
            )
            return (
                grad_query,
                add_rows(grad_keys, key_term, first_row),
                add_rows(grad_values, value_term, first_row),
            )

        return lax.cond(first_row <= query_start + block_rows - 1, grad_compute, unchanged, running)

    full_zeros = jnp.zeros((seq_count, full_rows, heads_local, HD), jnp.float32)
    grad_query_own, grad_keys_all, grad_values_all = over_blocks(
        grad_rows,
        (head_zeros, full_zeros, full_zeros),
        (
            lax.all_gather(key_head, "blk", axis=1, tiled=True),
            lax.all_gather(value_head, "blk", axis=1, tiled=True),
        ),
        block_rows,
    )
    grad_key_own, grad_value_own = (
        lax.psum_scatter(
            grad_keys_all.reshape(seq_count, full_rows, width).astype(jnp.bfloat16),
            "blk",
            scatter_dimension=1,
            tiled=True,
        ).astype(jnp.float32),
        lax.psum_scatter(
            grad_values_all.reshape(seq_count, full_rows, width).astype(jnp.bfloat16),
            "blk",
            scatter_dimension=1,
            tiled=True,
        ).astype(jnp.float32),
    )
    grad_query_own = grad_query_own.reshape(seq_count, block_rows, width)
    grad_query_tok, grad_key_tok, grad_value_tok = (
        lax.all_to_all(
            grad_query_own.astype(jnp.bfloat16), "ulysses", split_axis=1, concat_axis=2, tiled=True
        ),
        lax.all_to_all(
            grad_key_own.astype(jnp.bfloat16), "ulysses", split_axis=1, concat_axis=2, tiled=True
        ),
        lax.all_to_all(
            grad_value_own.astype(jnp.bfloat16), "ulysses", split_axis=1, concat_axis=2, tiled=True
        ),
    )
    grad_query_raw = rotate(grad_query_tok.astype(jnp.float32), cosine, sine, False).astype(
        jnp.bfloat16
    )
    grad_key_raw = rotate(grad_key_tok.astype(jnp.float32), cosine, sine, False).astype(
        jnp.bfloat16
    )
    grad_v_first = grad_value_tok * 0.5
    grad_normed = (
        project_back(grad_query_raw, back_query)
        + project_back(grad_key_raw, back_key)
        + project_back(grad_v_first, back_value)
    )
    grad_attn_norm, grad_gain_attn = norm_back(
        grad_normed, hatted_attn, factor_attn, back_gain_attn.astype(jnp.float32)
    )
    grad_inputs = (grad_hidden + grad_attn_norm).astype(jnp.bfloat16)
    model_width = w_query.shape[1]
    hidden_width = w_gate.shape[1]
    owned = lax.psum_scatter(
        jnp.concatenate(
            [
                weight_grad(normed, grad_query_raw),
                weight_grad(normed, grad_key_raw),
                weight_grad(normed, grad_v_first),
                weight_grad(mixed, grad_branch),
                weight_grad(normed_ffn, grad_gate),
                weight_grad(normed_ffn, grad_up),
                grad_gain_attn[:, None],
                grad_gain_ffn[:, None],
            ],
            axis=1,
        ),
        ("ulysses", "blk"),
        scatter_dimension=0,
        tiled=True,
    )
    grad_w_down = lax.psum_scatter(
        weight_grad(act, grad_out), ("ulysses", "blk"), scatter_dimension=0, tiled=True
    )
    column = 0
    pieces = []
    for span in (model_width, model_width, model_width, model_width, hidden_width, hidden_width):
        pieces.append(owned[:, column : column + span])
        column = column + span
    grad_gain_attn_own = owned[:, column]
    grad_gain_ffn_own = owned[:, column + 1]
    return (
        output,
        grad_inputs,
        grad_v_first,
        pieces[0],
        pieces[1],
        pieces[2],
        pieces[3],
        pieces[4],
        pieces[5],
        grad_w_down,
        grad_gain_attn_own,
        grad_gain_ffn_own,
        statistics,
    )


MESH = pl.DeviceIdType.MESH
LANES = 128
VMEM_BYTES = 58 << 20
f32 = jnp.float32
bf16 = jnp.bfloat16


class Net:
    def __init__(self, send_sems, recv_sems):
        self.send_sems, self.recv_sems = send_sems, recv_sems
        self.count, self.open = 0, []

    def push(self, src, dst, u, b):
        at = self.count
        self.count += 1
        copy = pltpu.make_async_remote_copy(
            src_ref=src,
            dst_ref=dst,
            send_sem=self.send_sems.at[at],
            recv_sem=self.recv_sems.at[at],
            device_id=(u, b),
            device_id_type=MESH,
        )
        copy.start()
        self.open.append(copy)
        return copy

    def drain(self):
        for copy in self.open:
            copy.wait_send()
        self.open = []


def arrive(copies):
    for copy in copies:
        copy.wait_recv()


def here():
    return lax.axis_index("ulysses"), lax.axis_index("blk")


def greet(u, b, n_u, n_b):
    barrier = pltpu.get_barrier_semaphore()
    for off in range(1, n_u):
        pl.semaphore_signal(barrier, inc=1, device_id=(u ^ off, b), device_id_type=MESH)
    for off in range(1, n_b):
        pl.semaphore_signal(barrier, inc=1, device_id=(u, b ^ off), device_id_type=MESH)
    pl.semaphore_wait(barrier, n_u - 1 + n_b - 1)


def dot(left, right):
    return jnp.dot(left, right, preferred_element_type=f32)


def dot_nt(left, right):
    return lax.dot_general(left, right, (((1,), (1,)), ((), ())), preferred_element_type=f32)


def dot_tn(left, right):
    return lax.dot_general(left, right, (((0,), (0,)), ((), ())), preferred_element_type=f32)


def lane_of(shape):
    return lax.broadcasted_iota(jnp.int32, shape, len(shape) - 1)


def swap_halves(tile):
    return pltpu.roll(tile, HD, tile.ndim - 1)


def partner(tile):
    low = lane_of(tile.shape) % HD < HD // 2
    return jnp.where(low, pltpu.roll(tile, LANES - HD // 2, 1), pltpu.roll(tile, HD // 2, 1))


def pack_rows(rows):
    half = rows.shape[0] // 2
    low = lane_of((half, LANES)) < HD
    return jnp.where(low, rows[:half], swap_halves(rows[half:]))


def unpack_rows(packed):
    return jnp.concatenate([packed, swap_halves(packed)], axis=0)


class Gather:
    def __init__(self, net, slot, u, b, n_b):
        self.net, self.slot, self.u, self.b, self.n_b = net, slot, u, b, n_b
        mine = slot(b)
        self.along = [net.push(mine, mine, u, b ^ (2 * k)) for k in range(1, n_b // 2)]
        self.side = [net.push(mine, mine, u, b ^ 1)]

    def relay(self):
        for k in range(1, self.n_b // 2):
            self.along[k - 1].wait_recv()
            got = self.slot(self.b ^ (2 * k))
            self.side.append(self.net.push(got, got, self.u, self.b ^ 1))

    def finish(self):
        arrive(self.side)


def kernel_project(dims, x, vf, go, wqkv, wgu, gains, cosr, sinr, units, normed, wq, gog, wg1, gain,
                   xg, vfg, stage, gbuf, send_sems, recv_sems):
    n_u, n_b, seqs, td, rows, heads = dims
    tb = n_u * td
    u, b = here()
    net = Net(send_sems, recv_sems)
    mine = pl.ds(pl.multiple_of(b * rows, rows), rows)
    slab = pl.ds(pl.multiple_of(u * td, td), td)
    greet(u, b, n_u, n_b)
    others = [u ^ off for off in range(1, n_u)]
    got_w = [net.push(wqkv.at[v], wq.at[u, mine], v, b) for v in others]
    got_g = [net.push(gains, gbuf.at[b, u], v, b) for v in others]
    got_x = [net.push(x, xg.at[:, slab], v, b) for v in others]
    got_v = [net.push(vf.at[v], vfg.at[:, slab], v, b) for v in others]
    wq[u, mine] = wqkv[u]
    gbuf[b, u] = gains[...]
    xg[:, slab] = x[...]
    vfg[:, slab] = vf[u]
    gog[:, slab] = go[...]
    wg1[u] = wgu[u]
    arrive(got_w)
    weights = Gather(net, lambda c: wq.at[:, pl.ds(pl.multiple_of(c * rows, rows), rows)], u, b, n_b)
    arrive(got_g)
    got_g = [net.push(gbuf.at[b], gbuf.at[b], u, b ^ off) for off in range(1, n_b)]
    got_o = [net.push(go, gog.at[:, slab], v, b) for v in others]
    got_o += [net.push(wgu.at[v], wg1.at[u], v, b) for v in others]
    arrive(got_g)
    per_tile = LANES // rows
    for tile in range(n_u * n_b // per_tile):
        total = None
        for index in range(tile * per_tile, (tile + 1) * per_tile):
            term = gbuf[index % n_b, index // n_b]
            total = term if total is None else total + term
        gain[:, tile * LANES : (tile + 1) * LANES] = total
    arrive(got_x)

    def norm(step, carry):
        s, part = step // 2, step % 2
        place = pl.ds(pl.multiple_of(part * (tb // 2), tb // 2), tb // 2)
        values = xg[s, place].astype(f32)
        factor = lax.rsqrt(jnp.mean(values * values, axis=-1, keepdims=True) + epsilon)
        normed[s, place] = (values * factor * gain[0:1, :]).astype(bf16)
        return carry

    lax.fori_loop(0, 2 * seqs, norm, 0)
    arrive(got_v)
    weights.relay()
    weights.finish()

    depth = wq.shape[0] * wq.shape[1]
    for s in range(seqs):
        left = normed[s]
        for n in range(heads // 2):
            found = dot(left, wq[:, :, n * 256 : (n + 1) * 256].reshape(depth, 256))
            for i in range(2):
                tile = found[:, i * LANES : (i + 1) * LANES]
                turned = tile * cosr[s] + partner(tile) * sinr[s]
                stage[s * heads + 2 * n + i, 0:tb] = turned.astype(bf16)
        for n in range(heads // 4):
            at = heads * LANES + n * 256
            found = dot(left, wq[:, :, at : at + 256].reshape(depth, 256))
            for i in range(2):
                first = vfg[s, :, n * 256 + i * LANES : n * 256 + (i + 1) * LANES].astype(f32)
                value = 0.5 * found[:, i * LANES : (i + 1) * LANES] + 0.5 * first
                unit = s * heads + 4 * n + 2 * i
                stage[unit, tb:] = pack_rows(value).astype(bf16)
                stage[unit + 1, tb:] = pack_rows(swap_halves(value)).astype(bf16)
    got = [net.push(stage.at[b ^ off], units.at[b], u, b ^ off) for off in range(1, n_b)]
    units[b] = stage[b]
    arrive(got)
    arrive(got_o)
    net.drain()


def fill_units(units, tb, store):
    def one(block, carry):
        low = lane_of((tb, LANES)) < HD
        tile = units[block, 0:tb].astype(f32)
        query = jnp.where(low, tile * HD ** (-0.5), 0.0)
        key = jnp.where(low, swap_halves(tile), 0.0)
        value = jnp.where(low, unpack_rows(units[block, tb:].astype(f32)), 0.0)
        store(block, query, key, value)
        return carry

    lax.fori_loop(0, units.shape[0], one, 0)


QB, KB = 512, 256


def allowed_block(first_key, first_query, low_row):
    key_place = first_key + lax.broadcasted_iota(jnp.int32, (KB, QB), 0)
    query_place = first_query + lax.broadcasted_iota(jnp.int32, (KB, QB), 1)
    return (key_place <= query_place) & (key_place >= low_row)


def kernel_attend(dims, units, low, x, wout, wg1, wd, gain, hidden, nf, wg, wdg, wo, mix, heads_t, lse, sums,
                  keys, query_t, value_t, acc, stage, parts, branch, branch_low, landed, nf_own,
                  send_sems, recv_sems):
    n_u, n_b, seqs, td, rows, heads = dims
    tb = n_u * td
    u, b = here()
    net = Net(send_sems, recv_sems)
    slab = pl.ds(pl.multiple_of(u * td, td), td)
    ff_rows = wd.shape[0]
    greet(u, b, n_u, n_b)

    def slot(ref, size):
        return lambda c: ref.at[pl.ds(pl.multiple_of(c * size, size), size)]

    wo[pl.ds(pl.multiple_of(b * rows, rows), rows)] = wout[...]
    g_out = Gather(net, slot(wo, rows), u, b, n_b)
    wdg[pl.ds(pl.multiple_of(b * ff_rows, ff_rows), ff_rows)] = wd[...]
    g_down = Gather(net, slot(wdg, ff_rows), u, b, n_b)
    wg[:, pl.ds(pl.multiple_of(b * rows, rows), rows)] = wg1[...]
    g_gate = Gather(net, lambda c: wg.at[:, pl.ds(pl.multiple_of(c * rows, rows), rows)], u, b, n_b)

    def store(block, query, key, value):
        place = pl.ds(pl.multiple_of(block * tb, tb), tb)
        keys[place] = key.astype(bf16)
        query_t[:, place] = jnp.transpose(query).astype(bf16)
        value_t[:, place] = jnp.transpose(value)[:HD].astype(bf16)

    fill_units(units, tb, store)
    seq = n_b * tb

    def attend(qb, carry):
        q_at = pl.ds(pl.multiple_of(qb * QB, QB), QB)
        query = query_t[:, q_at]
        low_row = low[0:1, q_at]
        acc[...] = jnp.zeros_like(acc)

        def inner(kb, state):
            best, total = state
            k_at = pl.ds(pl.multiple_of(kb * KB, KB), KB)
            scores = dot(keys[k_at], query)
            scores = jnp.where(allowed_block(kb * KB, qb * QB, low_row), scores, neg_big)
            new_best = jnp.maximum(best, jnp.max(scores, axis=0, keepdims=True))
            weights = jnp.exp(scores - new_best)
            rescale = jnp.exp(best - new_best)
            total = total * rescale + jnp.sum(weights, axis=0, keepdims=True)
            acc[...] = acc[...] * rescale + dot(value_t[:, k_at], weights.astype(bf16))
            return new_best, total

        start = (jnp.full((1, QB), neg_big, f32), jnp.zeros((1, QB), f32))
        best, total = lax.fori_loop(0, (qb + 1) * (QB // KB), inner, start)
        out = acc[...] / total
        heads_t[:, q_at] = out
        lse[:, q_at] = jnp.broadcast_to(best + jnp.log(total), (8, QB))
        turned = jnp.transpose(jnp.concatenate([out, jnp.zeros_like(out)], axis=0))
        for i in range(QB // tb):
            stage[qb * (QB // tb) + i] = pack_rows(turned[i * tb : (i + 1) * tb]).astype(bf16)
        return carry

    lax.fori_loop(0, seq // QB, attend, 0)
    got = [net.push(stage.at[b ^ off], parts.at[b], u, b ^ off) for off in range(1, n_b)]
    parts[b] = stage[b]
    g_out.relay()
    arrive(got)
    half = tb // 2
    for s in range(seqs):
        for pair in range(heads // 2):
            one = parts[s * heads + 2 * pair].astype(f32)
            two = parts[s * heads + 2 * pair + 1].astype(f32)
            low_lane = lane_of(one.shape) < HD
            lanes = slice(pair * LANES, (pair + 1) * LANES)
            mix[s, :half, lanes] = jnp.where(low_lane, one, swap_halves(two)).astype(bf16)
            mix[s, half:, lanes] = jnp.where(low_lane, swap_halves(one), two).astype(bf16)
    g_out.finish()
    others = [u ^ off for off in range(1, n_u)]

    def project_out(s, carry):
        found = dot(mix[s], wo[...])
        branch[s] = found
        branch_low[s] = found.astype(bf16)
        return carry

    lax.fori_loop(0, seqs, project_out, 0)

    def part(v):
        return pl.ds(pl.multiple_of(v * td, td), td)

    got = [net.push(branch_low.at[:, part(v)], landed.at[u], v, b) for v in others]
    arrive(got)
    for s in range(seqs):
        total = branch[s, slab]
        for v in others:
            total = total + landed[v, s].astype(f32)
        own = x[s].astype(f32)
        hid = own + total
        hidden[s] = hid
        factor = lax.rsqrt(jnp.mean(hid * hid, axis=-1, keepdims=True) + epsilon)
        nf_own[s] = (hid * factor * gain[1:2, :]).astype(bf16)
        squares = [jnp.sum(own * own, axis=0, keepdims=True), jnp.sum(total * total, axis=0, keepdims=True)]
        if s == 0:
            sums[...] = jnp.zeros_like(sums)
        for i, square in enumerate(squares):
            sums[i : i + 1] = sums[i : i + 1] + square
    got = [net.push(nf_own, nf.at[:, slab], v, b) for v in others]
    nf[:, slab] = nf_own[...]
    g_down.relay()
    g_gate.relay()
    g_down.finish()
    g_gate.finish()
    arrive(got)
    net.drain()


class Scatter:
    def __init__(self, net, u, b, n_b, mine, paired, summed, landed):
        self.net, self.u, self.b, self.n_z = net, u, b, n_b // 2
        self.mine, self.paired, self.summed, self.landed = mine, paired, summed, landed
        core = b % 2
        self.swap = [net.push(mine(z, 1 - core), paired(z), u, b ^ 1) for z in range(self.n_z)]

    def middle(self):
        z_own, core = self.b // 2, self.b % 2
        self.along = []
        for k in range(self.n_z):
            if k == 0:
                arrive(self.swap)
            z = z_own ^ ((k + 1) % self.n_z)
            self.summed[z] = (
                self.mine(z, core)[...].astype(f32) + self.paired(z)[...].astype(f32)
            ).astype(bf16)
            if k + 1 < self.n_z:
                self.along.append(
                    self.net.push(
                        self.summed.at[z], self.landed.at[k], self.u, self.b ^ (2 * (k + 1))
                    )
                )

    def finish(self):
        arrive(self.along)
        total = self.summed[self.b // 2].astype(f32)
        for k in range(self.n_z - 1):
            total = total + self.landed[k].astype(f32)
        return total


def kernel_feed(dims, nf, gog, wg, wdg, wo, mix, hidden, gain, sums_in, out, ghid, units, dwd, dwgu, dwo, sums,
                act, dgu, d_part, d_low, f_part, f_low, landed_d, landed_f, gb_own, gb, stage,
                wd_buf, wd_pair, wd_sum, wd_land, wg_buf, wg_pair, wg_sum, wg_land, wg_low,
                send_sems, recv_sems):
    n_u, n_b, seqs, td, rows, heads = dims
    tb = n_u * td
    n_z = n_b // 2
    u, b = here()
    net = Net(send_sems, recv_sems)
    slab = pl.ds(pl.multiple_of(u * td, td), td)
    greet(u, b, n_u, n_b)
    others = [u ^ off for off in range(1, n_u)]
    depth = wg.shape[0] * wg.shape[1]
    units_ff = wdg.shape[0]
    ff_rows = units_ff // n_b

    def part(v):
        return pl.ds(pl.multiple_of(v * td, td), td)

    def hidden_units(s, carry):
        left = nf[s]
        grad = gog[s]
        for n in range(units_ff // 256):
            span = slice(n * 256, (n + 1) * 256)
            up_span = slice(units_ff + n * 256, units_ff + (n + 1) * 256)
            gate = dot(left, wg[:, :, span].reshape(depth, 256))
            up = dot(left, wg[:, :, up_span].reshape(depth, 256))
            grad_act = dot_nt(grad, wdg[span])
            sig = 1.0 / (1.0 + jnp.exp(-gate))
            silu = gate * sig
            act[s, :, span] = (silu * up).astype(bf16)
            dgu[s, :, span] = (grad_act * up * sig * (1.0 + gate * (1.0 - sig))).astype(bf16)
            dgu[s, :, up_span] = (grad_act * silu).astype(bf16)
        return carry

    lax.fori_loop(0, seqs, hidden_units, 0)

    def back(s, carry):
        left = dgu[s]
        for v in range(n_u):
            lanes = slice(v * 256, (v + 1) * 256)
            found = dot_nt(left, wg[v])
            d_part[s, :, lanes] = found
            d_low[s, :, lanes] = found.astype(bf16)
        return carry

    lax.fori_loop(0, seqs, back, 0)
    got_d = [net.push(d_low.at[:, part(v)], landed_d.at[u], v, b) for v in others]

    width = wdg.shape[1]
    half_units = units_ff // 2
    for n in range(2):
        span = slice(n * half_units, (n + 1) * half_units)
        found = dot_tn(act[:, :, span].reshape(seqs * tb, half_units), gog[...].reshape(seqs * tb, width))
        wd_buf[n * (n_z // 2) : (n + 1) * (n_z // 2)] = found.astype(bf16).reshape(
            n_z // 2, 2, ff_rows, width
        )
    s_down = Scatter(net, u, b, n_b, lambda z, c: wd_buf.at[z, c], lambda z: wd_pair.at[z], wd_sum, wd_land)
    for v in range(n_u):
        left = nf[:, :, v * 256 : (v + 1) * 256].reshape(seqs * tb, 256)
        found = dot_tn(left, dgu[...].reshape(seqs * tb, 2 * units_ff))
        wg_buf[:, :, v] = found.astype(bf16).reshape(n_z, 2, rows, 2 * units_ff)
    s_gate = Scatter(net, u, b, n_b, lambda z, c: wg_buf.at[z, c], lambda z: wg_pair.at[z], wg_sum, wg_land)

    s_down.middle()
    s_gate.middle()

    arrive(got_d)
    sums[...] = sums_in[...]
    for s in range(seqs):
        grad_normed = d_part[s, slab]
        for v in others:
            grad_normed = grad_normed + landed_d[v, s].astype(f32)
        hid = hidden[s]
        factor = lax.rsqrt(jnp.mean(hid * hid, axis=-1, keepdims=True) + epsilon)
        hat = hid * factor
        scaled = grad_normed * gain[1:2, :]
        inner = jnp.mean(scaled * hat, axis=-1, keepdims=True)
        total = gog[s, slab].astype(f32) + factor * (scaled - hat * inner)
        ghid[s] = total
        gb_own[s] = total.astype(bf16)
        sums[4:5] = sums[4:5] + jnp.sum(grad_normed * hat, axis=0, keepdims=True)
    got_b = [net.push(gb_own, gb.at[:, slab], v, b) for v in others]
    gb[:, slab] = gb_own[...]

    def forward(s, carry):
        found = dot(act[s], wdg[...])
        f_part[s] = found
        f_low[s] = found.astype(bf16)
        return carry

    lax.fori_loop(0, seqs, forward, 0)
    arrive(got_b)
    for s in range(seqs):
        for pair in range(heads // 2):
            found = dot_nt(gb[s], wo[pair * LANES : (pair + 1) * LANES])
            stage[s * heads + 2 * pair] = pack_rows(found).astype(bf16)
            stage[s * heads + 2 * pair + 1] = pack_rows(swap_halves(found)).astype(bf16)
    got_u = [net.push(stage.at[b ^ off], units.at[b], u, b ^ off) for off in range(1, n_b)]
    units[b] = stage[b]
    got_f = [net.push(f_low.at[:, part(v)], landed_f.at[u], v, b) for v in others]
    found = dot_tn(mix[...].reshape(seqs * tb, mix.shape[2]), gb[...].reshape(seqs * tb, width))
    dwo[...] = found.astype(bf16).reshape(dwo.shape)

    arrive(got_f)
    for s in range(seqs):
        total = hidden[s] + f_part[s, slab]
        for v in others:
            total = total + landed_f[v, s].astype(f32)
        out[s] = total.astype(bf16)
        sums[2:3] = sums[2:3] + jnp.sum(total * total, axis=0, keepdims=True)

    dwd[...] = s_down.finish()
    wg_low[...] = s_gate.finish().astype(bf16)
    got = [net.push(wg_low.at[v], dwgu.at[u], v, b) for v in others]
    dwgu[u] = wg_low[u]
    arrive(got_u)
    arrive(got)
    net.drain()


def kernel_back(dims, units, grads, heads_t, lse, low, normed, wq, cosr, sinr, ghid, x, gain, dwo_in, sums_in,
                gin, gvf, dwq, dwo, sums,
                keys, key_t, query, query_t, value, grad, grad_t, row_dot, dq_t, dk, dv, stage, returned, raw,
                gin_part, gin_low, landed, gv, wq_buf, wq_pair, wq_sum, wq_land, wq_low,
                wo_pair, wo_sum, wo_land, sums_own, sums_u, sums_ub, sums_b, send_sems, recv_sems):
    n_u, n_b, seqs, td, rows, heads = dims
    tb = n_u * td
    n_z = n_b // 2
    seq = n_b * tb
    u, b = here()
    net = Net(send_sems, recv_sems)
    slab = pl.ds(pl.multiple_of(u * td, td), td)
    greet(u, b, n_u, n_b)
    others = [u ^ off for off in range(1, n_u)]
    s_out = Scatter(net, u, b, n_b, lambda z, c: dwo_in.at[z, c], lambda z: wo_pair.at[z], wo_sum, wo_land)

    def part(v):
        return pl.ds(pl.multiple_of(v * td, td), td)

    def store(block, q, k, v):
        place = pl.ds(pl.multiple_of(block * tb, tb), tb)
        keys[place] = k.astype(bf16)
        key_t[:, place] = jnp.transpose(k)[:HD].astype(bf16)
        query[place] = q.astype(bf16)
        query_t[:, place] = jnp.transpose(q).astype(bf16)
        value[place] = v.astype(bf16)
        g = unpack_rows(grads[block].astype(f32))
        g = jnp.where(lane_of(g.shape) < HD, g, 0.0)
        grad[place] = g.astype(bf16)
        turned = jnp.transpose(g)
        grad_t[:, place] = turned.astype(bf16)
        total = jnp.sum(turned[:HD] * heads_t[:, place], axis=0, keepdims=True)
        row_dot[:, place] = jnp.broadcast_to(total, (8, tb))

    fill_units(units, tb, store)
    s_out.middle()
    dq_t[...] = jnp.zeros_like(dq_t)

    def outer(kb, carry):
        k_at = pl.ds(pl.multiple_of(kb * KB, KB), KB)
        dk[...] = jnp.zeros_like(dk)
        dv[...] = jnp.zeros_like(dv)

        def inner(qb, carry):
            q_at = pl.ds(pl.multiple_of(qb * QB, QB), QB)
            scores = dot(keys[k_at], query_t[:, q_at])
            seen = allowed_block(kb * KB, qb * QB, low[0:1, q_at])
            probs = jnp.where(seen, jnp.exp(scores - lse[0:1, q_at]), 0.0)
            prob_grad = dot(value[k_at], grad_t[:, q_at])
            score_grad = (probs * (prob_grad - row_dot[0:1, q_at])).astype(bf16)
            dv[...] += dot(probs.astype(bf16), grad[q_at])
            dk[...] += dot(score_grad, query[q_at])
            dq_t[:, q_at] += dot(key_t[:, k_at], score_grad)
            return carry

        lax.fori_loop(kb // (QB // KB), seq // QB, inner, 0)
        low_lane = lane_of((KB, LANES)) < HD
        stage[kb, 0:tb] = jnp.where(low_lane, 0.0, swap_halves(dk[...])).astype(bf16)
        stage[kb, tb:] = pack_rows(dv[...]).astype(bf16)
        return carry

    lax.fori_loop(0, seq // KB, outer, 0)

    def turn_query(block, carry):
        place = pl.ds(pl.multiple_of(block * tb, tb), tb)
        columns = dq_t[:, place] * HD ** (-0.5)
        turned = jnp.transpose(jnp.concatenate([columns, jnp.zeros_like(columns)], axis=0))
        low_lane = lane_of(turned.shape) < HD
        stage[block, 0:tb] = jnp.where(low_lane, turned, stage[block, 0:tb].astype(f32)).astype(bf16)
        return carry

    lax.fori_loop(0, n_b, turn_query, 0)
    got = [net.push(stage.at[b ^ off], returned.at[b], u, b ^ off) for off in range(1, n_b)]
    returned[b] = stage[b]
    dwo[...] = s_out.finish()
    arrive(got)

    wide = heads * LANES
    for s in range(seqs):
        for head in range(heads):
            tile = returned[s * heads + head, 0:tb].astype(f32)
            turned = tile * cosr[s] - partner(tile) * sinr[s]
            raw[s, :, head * LANES : (head + 1) * LANES] = turned.astype(bf16)
        for pair in range(heads // 2):
            one = unpack_rows(returned[s * heads + 2 * pair, tb:].astype(f32))
            two = unpack_rows(returned[s * heads + 2 * pair + 1, tb:].astype(f32))
            both = 0.5 * jnp.where(lane_of(one.shape) < HD, one, swap_halves(two))
            raw[s, :, wide + pair * LANES : wide + (pair + 1) * LANES] = both.astype(bf16)
    got_v = [net.push(raw.at[:, part(v), pl.ds(wide, gv.shape[3])], gv.at[u], v, b) for v in others]
    gv[u] = raw[:, slab, wide:]

    def back(s, carry):
        left = raw[s]
        for v in range(n_u):
            lanes = slice(v * 256, (v + 1) * 256)
            found = dot_nt(left, wq[v])
            gin_part[s, :, lanes] = found
            gin_low[s, :, lanes] = found.astype(bf16)
        return carry

    lax.fori_loop(0, seqs, back, 0)
    got_g = [net.push(gin_low.at[:, part(v)], landed.at[u], v, b) for v in others]
    columns = raw.shape[2]
    for v in range(n_u):
        left = normed[:, :, v * 256 : (v + 1) * 256].reshape(seqs * tb, 256)
        found = dot_tn(left, raw[...].reshape(seqs * tb, columns))
        wq_buf[:, :, v] = found.astype(bf16).reshape(n_z, 2, rows, columns)
    s_qkv = Scatter(net, u, b, n_b, lambda z, c: wq_buf.at[z, c], lambda z: wq_pair.at[z], wq_sum, wq_land)
    s_qkv.middle()

    arrive(got_g)
    sums_own[...] = sums_in[...]
    for s in range(seqs):
        grad_normed = gin_part[s, slab]
        for v in others:
            grad_normed = grad_normed + landed[v, s].astype(f32)
        own = x[s].astype(f32)
        factor = lax.rsqrt(jnp.mean(own * own, axis=-1, keepdims=True) + epsilon)
        hat = own * factor
        scaled = grad_normed * gain[0:1, :]
        inner = jnp.mean(scaled * hat, axis=-1, keepdims=True)
        gin[s] = (ghid[s] + factor * (scaled - hat * inner)).astype(bf16)
        sums_own[3:4] = sums_own[3:4] + jnp.sum(grad_normed * hat, axis=0, keepdims=True)
    got_s = [net.push(sums_own, sums_u.at[u], v, b) for v in others]
    arrive(got_s)
    total = sums_own[...]
    for v in others:
        total = total + sums_u[v]
    sums_ub[...] = total
    got_s = [net.push(sums_ub, sums_b.at[b], u, b ^ off) for off in range(1, n_b)]
    arrive(got_s)
    for off in range(1, n_b):
        total = total + sums_b[b ^ off]
    sums[...] = total
    arrive(got_v)
    for v in range(n_u):
        gvf[:, :, v * 256 : (v + 1) * 256] = gv[v]
    wq_low[...] = s_qkv.finish().astype(bf16)
    got = [net.push(wq_low.at[v], dwq.at[u], v, b) for v in others]
    dwq[u] = wq_low[u]
    arrive(got)
    net.drain()


def call(kernel, dims, name, collective_id, outs, scratch, copies, inputs):
    vmem = pl.BlockSpec(memory_space=pltpu.VMEM)
    return pl.pallas_call(
        functools.partial(kernel, dims),
        out_shape=[jax.ShapeDtypeStruct(shape, dtype) for shape, dtype in outs],
        in_specs=[vmem] * len(inputs),
        out_specs=[vmem] * len(outs),
        scratch_shapes=[pltpu.VMEM(shape, dtype) for shape, dtype in scratch]
        + [pltpu.SemaphoreType.DMA((copies,))] * 2,
        compiler_params=pltpu.CompilerParams(
            collective_id=collective_id, has_side_effects=True, vmem_limit_bytes=VMEM_BYTES
        ),
        name=name,
    )(*inputs)


def pad_to(values, axis, size):
    widths = [(0, 0)] * values.ndim
    widths[axis] = (0, size - values.shape[axis])
    return jnp.pad(values, widths)


def local_units(
    inputs, v_first, grad_out, positions, segments,
    w_query, w_key, w_value, w_out, w_gate, w_up, w_down, gain_attn, gain_ffn,
    debug=None,
):
    n_u, n_b = lax.axis_size("ulysses"), lax.axis_size("blk")
    u, b = here()
    seqs, td, width = inputs.shape
    rows = w_query.shape[0]
    heads = HEADS // n_u
    tb = n_u * td
    seq = n_b * tb
    ff_own = w_down.shape[0]
    ff_pad = -(-ff_own // 32) * 32
    ff = ff_pad * n_b
    dims = (n_u, n_b, seqs, td, rows, heads)

    place = jnp.arange(seq, dtype=jnp.int32)
    cut = jnp.sum(1 - segments, axis=1, keepdims=True)
    first = jnp.where(segments == 1, cut, 0)
    low = lax.dynamic_slice_in_dim(first, b // heads, 1, 0)
    low = jnp.broadcast_to(low, (8, seq))
    local_place = (place[None, :] - first).astype(f32)
    angle_rows = lax.dynamic_slice_in_dim(local_place, b * tb, tb, 1)
    inverse = rope_base ** (-2.0 * jnp.arange(HD // 2, dtype=f32) / HD)
    angles = angle_rows[:, :, None] * inverse
    cosine, sine = jnp.cos(angles), jnp.sin(angles)
    cosr = jnp.concatenate([cosine] * 4, axis=-1)
    sinr = jnp.concatenate([-sine, sine] * 2, axis=-1)

    qk = jnp.stack([w_query.reshape(rows, n_u, heads, HD), w_key.reshape(rows, n_u, heads, HD)], axis=3)
    wqkv = jnp.concatenate(
        [qk.reshape(rows, n_u, heads * 2 * HD), w_value.reshape(rows, n_u, heads * HD)], axis=2
    )
    wqkv = jnp.moveaxis(wqkv, 1, 0)

    def hidden_columns(weight):
        parted = pad_to(weight.reshape(rows, n_u, n_b, ff_own), 3, ff_pad)
        return parted.reshape(rows, n_u, ff)

    wgu = jnp.moveaxis(
        jnp.concatenate([hidden_columns(w_gate), hidden_columns(w_up)], axis=2), 1, 0
    )
    wd = pad_to(w_down, 0, ff_pad)
    vf = jnp.moveaxis(v_first.reshape(seqs, td, n_u, heads * HD), 2, 0)
    pair = jnp.stack([gain_attn, gain_ffn]).astype(f32)
    lane = (jnp.arange(LANES) // rows) == (u * n_b + b) % (LANES // rows)
    gains = pad_to(jnp.where(lane[None, :], jnp.tile(pair, (1, LANES // rows)), 0.0), 0, 8)

    columns = 3 * heads * HD
    units, normed, wq, gog, wg1, gain = call(
        kernel_project, dims, "project", 1,
        [((n_b, tb + tb // 2, LANES), bf16), ((seqs, tb, width), bf16), ((n_u, n_b * rows, columns), bf16),
         ((seqs, tb, width), bf16), ((n_u, rows, 2 * ff), bf16), ((8, width), f32)],
        [((seqs, tb, width), bf16), ((seqs, tb, heads * HD), bf16), ((n_b, tb + tb // 2, LANES), bf16),
         ((n_b, n_u, 8, LANES), f32)],
        48,
        [inputs, vf, grad_out, wqkv, wgu, gains, cosr, sinr],
    )
    hidden, nf, wg, wdg, wo, mix, heads_t, lse, sums = call(
        kernel_attend, dims, "attend", 2,
        [((seqs, td, width), f32), ((seqs, tb, width), bf16), ((n_u, n_b * rows, 2 * ff), bf16),
         ((ff, width), bf16), ((n_b * rows, width), bf16), ((seqs, tb, heads * HD), bf16),
         ((HD, seq), f32), ((8, seq), f32), ((8, width), f32)],
        [((seq, LANES), bf16), ((LANES, seq), bf16), ((HD, seq), bf16), ((HD, QB), f32),
         ((n_b, tb // 2, LANES), bf16), ((n_b, tb // 2, LANES), bf16), ((seqs, tb, width), f32),
         ((seqs, tb, width), bf16), ((n_u, seqs, td, width), bf16), ((seqs, td, width), bf16)],
        48,
        [units, low, inputs, w_out, wg1, wd, gain],
    )
    n_z = n_b // 2
    out, ghid, grads, dwd, dwgu, dwo_part, sums = call(
        kernel_feed, dims, "feed", 3,
        [((seqs, td, width), bf16), ((seqs, td, width), f32), ((n_b, tb // 2, LANES), bf16),
         ((ff_pad, width), f32), ((n_u, rows, 2 * ff), bf16), ((n_z, 2, rows, width), bf16), ((8, width), f32)],
        [((seqs, tb, ff), bf16), ((seqs, tb, 2 * ff), bf16),
         ((seqs, tb, width), f32), ((seqs, tb, width), bf16), ((seqs, tb, width), f32), ((seqs, tb, width), bf16),
         ((n_u, seqs, td, width), bf16), ((n_u, seqs, td, width), bf16),
         ((seqs, td, width), bf16), ((seqs, tb, width), bf16), ((n_b, tb // 2, LANES), bf16),
         ((n_z, 2, ff_pad, width), bf16), ((n_z, ff_pad, width), bf16), ((n_z, ff_pad, width), bf16),
         ((n_z - 1, ff_pad, width), bf16),
         ((n_z, 2, n_u, rows, 2 * ff), bf16), ((n_z, n_u, rows, 2 * ff), bf16), ((n_z, n_u, rows, 2 * ff), bf16),
         ((n_z - 1, n_u, rows, 2 * ff), bf16), ((n_u, rows, 2 * ff), bf16)],
        48,
        [nf, gog, wg, wdg, wo, mix, hidden, gain, sums],
    )
    gin, gvf, dwq, dwo, sums = call(
        kernel_back, dims, "back", 4,
        [((seqs, td, width), bf16), ((seqs, td, width), bf16), ((n_u, rows, columns), bf16),
         ((rows, width), f32), ((8, width), f32)],
        [((seq, LANES), bf16), ((HD, seq), bf16), ((seq, LANES), bf16), ((LANES, seq), bf16),
         ((seq, LANES), bf16), ((seq, LANES), bf16), ((LANES, seq), bf16), ((8, seq), f32), ((HD, seq), f32),
         ((KB, LANES), f32), ((KB, LANES), f32), ((n_b, tb + tb // 2, LANES), bf16),
         ((n_b, tb + tb // 2, LANES), bf16), ((seqs, tb, columns), bf16),
         ((seqs, tb, width), f32), ((seqs, tb, width), bf16), ((n_u, seqs, td, width), bf16),
         ((n_u, seqs, td, heads * HD), bf16),
         ((n_z, 2, n_u, rows, columns), bf16), ((n_z, n_u, rows, columns), bf16),
         ((n_z, n_u, rows, columns), bf16), ((n_z - 1, n_u, rows, columns), bf16), ((n_u, rows, columns), bf16),
         ((n_z, rows, width), bf16), ((n_z, rows, width), bf16), ((n_z - 1, rows, width), bf16),
         ((8, width), f32), ((n_u, 8, width), f32), ((8, width), f32), ((n_b, 8, width), f32)],
        64,
        [units, grads, heads_t, lse, low, normed, wq, cosr, sinr, ghid, inputs, gain, dwo_part, sums],
    )
    dwq = jnp.moveaxis(dwq.astype(f32), 0, 1)
    dqk = dwq[:, :, : heads * 2 * HD].reshape(rows, n_u, heads, 2, HD)
    grad_w_query = dqk[:, :, :, 0].reshape(rows, width)
    grad_w_key = dqk[:, :, :, 1].reshape(rows, width)
    grad_w_value = dwq[:, :, heads * 2 * HD :].reshape(rows, width)
    dwgu = jnp.moveaxis(dwgu.astype(f32), 0, 1).reshape(rows, n_u, 2, n_b, ff_pad)[..., :ff_own]
    grad_w_gate = dwgu[:, :, 0].reshape(rows, w_gate.shape[1])
    grad_w_up = dwgu[:, :, 1].reshape(rows, w_gate.shape[1])
    grad_w_down = dwd[:ff_own]
    gain_at = (u * n_b + b) * rows
    grad_gain_attn = lax.dynamic_slice_in_dim(sums[3], gain_at, rows, 0)
    grad_gain_ffn = lax.dynamic_slice_in_dim(sums[4], gain_at, rows, 0)
    statistics = jnp.sqrt(jnp.sum(sums[:3], axis=1) / (seqs * seq * width))
    return (
        out, gin, gvf, grad_w_query, grad_w_key, grad_w_value, dwo, grad_w_gate, grad_w_up, grad_w_down,
        grad_gain_attn, grad_gain_ffn, statistics,
    )


def fits_units(mesh):
    n_u, n_b = mesh.shape["ulysses"], mesh.shape["blk"]
    return n_u == 4 and n_b == 8


def solution(mesh):
    in_specs = (
        P(None, ("blk", "ulysses"), None),
        P(None, ("blk", "ulysses"), None),
        P(None, ("blk", "ulysses"), None),
        P(None, ("blk", "ulysses")),
        P(),
        P(("ulysses", "blk"), None),
        P(("ulysses", "blk"), None),
        P(("ulysses", "blk"), None),
        P(("ulysses", "blk"), None),
        P(("ulysses", "blk"), None),
        P(("ulysses", "blk"), None),
        P(("ulysses", "blk"), None),
        P(("ulysses", "blk")),
        P(("ulysses", "blk")),
    )
    out_specs = (
        P(None, ("blk", "ulysses"), None),
        P(None, ("blk", "ulysses"), None),
        P(None, ("blk", "ulysses"), None),
        P(("ulysses", "blk"), None),
        P(("ulysses", "blk"), None),
        P(("ulysses", "blk"), None),
        P(("ulysses", "blk"), None),
        P(("ulysses", "blk"), None),
        P(("ulysses", "blk"), None),
        P(("ulysses", "blk"), None),
        P(("ulysses", "blk")),
        P(("ulysses", "blk")),
        P(),
    )
    path = local_units if fits_units(mesh) else local
    return jax.shard_map(path, mesh=mesh, in_specs=in_specs, out_specs=out_specs, check_vma=False)
```

```python
import functools
import types

import jax
import jax.numpy as jnp
from jax import lax
from jax.experimental import pallas as pl
from jax.experimental.pallas import tpu as pltpu
from jax.sharding import PartitionSpec as P

HEADS = 16
HD = 64


epsilon = 1e-06
rope_base = 10000.0
neg_big = -1e30


def norm_rows(values, gain):
    factor = lax.rsqrt(jnp.mean(values * values, axis=-1, keepdims=True) + epsilon)
    hatted = values * factor
    return (hatted * gain, hatted, factor)


def norm_back(grad_normed, hatted, factor, gain):
    scaled = grad_normed * gain
    inner = jnp.mean(scaled * hatted, axis=-1, keepdims=True)
    return (factor * (scaled - hatted * inner), jnp.sum(grad_normed * hatted, axis=(0, 1)))


def rope_tables(positions):
    half_dim = HD // 2
    inverse = rope_base ** (-2.0 * jnp.arange(half_dim, dtype=jnp.float32) / HD)
    angles = positions.astype(jnp.float32)[:, :, None] * inverse
    return (jnp.cos(angles)[:, :, None, :], jnp.sin(angles)[:, :, None, :])


def rotate(values, cosine, sine, forward_turn):
    shaped = values.reshape(values.shape[0], values.shape[1], HEADS, HD)
    half_dim = HD // 2
    first = shaped[..., :half_dim]
    second = shaped[..., half_dim:]
    if forward_turn:
        turned = jnp.concatenate(
            [first * cosine - second * sine, second * cosine + first * sine], axis=-1
        )
    else:
        turned = jnp.concatenate(
            [first * cosine + second * sine, second * cosine - first * sine], axis=-1
        )
    return turned.reshape(values.shape)


def project(activations, weight):
    return jnp.einsum("std,de->ste", activations, weight, preferred_element_type=jnp.float32)


def project_back(gradient, weight):
    return jnp.einsum("ste,de->std", gradient, weight, preferred_element_type=jnp.float32)


def weight_grad(activations, gradient):
    return jnp.einsum("std,ste->de", activations, gradient, preferred_element_type=jnp.float32)


def allowed_mask(segments, query_first, query_count, key_first, key_count):
    seg_query = lax.dynamic_slice_in_dim(segments, query_first, query_count, 1)
    seg_key = lax.dynamic_slice_in_dim(segments, key_first, key_count, 1)
    query_place = query_first + jnp.arange(query_count, dtype=jnp.int32)
    key_place = key_first + jnp.arange(key_count, dtype=jnp.int32)
    causal = key_place[None, :] <= query_place[:, None]
    same_doc = seg_query[:, :, None] == seg_key[:, None, :]
    return (causal[None] & same_doc)[:, :, None, :]


def over_blocks(step_fn, running, pieces, block_rows):
    row_count = pieces[0].shape[1]
    block_count = row_count // block_rows
    stacked = tuple(
        (
            jnp.moveaxis(
                member.reshape((member.shape[0], block_count, block_rows) + member.shape[2:]), 1, 0
            )
            for member in pieces
        )
    )
    offsets = block_rows * jnp.arange(block_count, dtype=jnp.int32)

    def advance(current, scan_entry):
        return (step_fn(current, scan_entry[:-1], scan_entry[-1]), None)

    running, unused = lax.scan(advance, running, stacked + (offsets,))
    return running


def add_rows(buffer, update, first_row):
    current = lax.dynamic_slice_in_dim(buffer, first_row, update.shape[1], 1)
    return lax.dynamic_update_slice_in_dim(buffer, current + update, first_row, 1)


def unchanged(running):
    return running


def local(
    inputs,
    v_first,
    grad_out,
    positions,
    segments,
    w_query,
    w_key,
    w_value,
    w_out,
    w_gate,
    w_up,
    w_down,
    gain_attn,
    gain_ffn,
):
    gathered = (
        lax.all_gather(w_query, ("ulysses", "blk"), axis=0, tiled=True),
        lax.all_gather(w_key, ("ulysses", "blk"), axis=0, tiled=True),
        lax.all_gather(w_value, ("ulysses", "blk"), axis=0, tiled=True),
        lax.all_gather(w_out, ("ulysses", "blk"), axis=0, tiled=True),
        lax.all_gather(w_gate, ("ulysses", "blk"), axis=0, tiled=True),
        lax.all_gather(w_up, ("ulysses", "blk"), axis=0, tiled=True),
        lax.all_gather(w_down, ("ulysses", "blk"), axis=0, tiled=True),
        lax.all_gather(gain_attn, ("ulysses", "blk"), axis=0, tiled=True),
        lax.all_gather(gain_ffn, ("ulysses", "blk"), axis=0, tiled=True),
    )
    (
        full_query,
        full_key,
        full_value,
        full_out,
        full_gate,
        full_up,
        full_down,
        full_gain_attn,
        full_gain_ffn,
    ) = gathered
    score_scale = HD ** (-0.5)
    residual = inputs.astype(jnp.float32)
    normed_f, hatted_attn, factor_attn = norm_rows(residual, full_gain_attn.astype(jnp.float32))
    normed = normed_f.astype(jnp.bfloat16)
    cosine, sine = rope_tables(positions)
    query_tok = rotate(project(normed, full_query), cosine, sine, True).astype(jnp.bfloat16)
    key_tok = rotate(project(normed, full_key), cosine, sine, True).astype(jnp.bfloat16)
    value_tok = (0.5 * project(normed, full_value) + 0.5 * v_first.astype(jnp.float32)).astype(
        jnp.bfloat16
    )
    query_head, key_head, value_head = (
        lax.all_to_all(query_tok, "ulysses", split_axis=2, concat_axis=1, tiled=True),
        lax.all_to_all(key_tok, "ulysses", split_axis=2, concat_axis=1, tiled=True),
        lax.all_to_all(value_tok, "ulysses", split_axis=2, concat_axis=1, tiled=True),
    )
    seq_count, block_rows, width = query_head.shape
    heads_local = width // HD
    query_start = lax.axis_index("blk") * block_rows
    full_rows = block_rows * lax.axis_size("blk")

    def split_heads(values):
        return values.reshape(values.shape[0], values.shape[1], heads_local, HD)

    query_four = split_heads(query_head)

    def attend_rows(running, pieces, first_row):
        key_rows, value_rows = pieces
        key_count = key_rows.shape[1]

        def attend_compute(current):
            best, total, accum = current
            allowed = allowed_mask(segments, query_start, block_rows, first_row, key_count)
            scores = (
                jnp.einsum(
                    "sqhd,skhd->sqhk",
                    query_four,
                    split_heads(key_rows),
                    preferred_element_type=jnp.float32,
                )
                * score_scale
            )
            masked = jnp.where(allowed, scores, neg_big)
            new_best = jnp.maximum(best, jnp.max(masked, axis=-1))
            weights = jnp.where(allowed, jnp.exp(masked - new_best[..., None]), 0.0)
            rescale = jnp.exp(best - new_best)
            total = total * rescale + jnp.sum(weights, axis=-1)
            accum = accum * rescale[..., None] + jnp.einsum(
                "sqhk,skhd->sqhd",
                weights.astype(jnp.bfloat16),
                split_heads(value_rows),
                preferred_element_type=jnp.float32,
            )
            return (new_best, total, accum)

        return lax.cond(
            first_row <= query_start + block_rows - 1, attend_compute, unchanged, running
        )

    stat_zeros = jnp.zeros((seq_count, block_rows, heads_local), jnp.float32)
    head_zeros = jnp.zeros((seq_count, block_rows, heads_local, HD), jnp.float32)
    initial = (
        jnp.full((seq_count, block_rows, heads_local), neg_big, jnp.float32),
        stat_zeros,
        head_zeros,
    )
    best, total, accum = over_blocks(
        attend_rows,
        initial,
        (
            lax.all_gather(key_head, "blk", axis=1, tiled=True),
            lax.all_gather(value_head, "blk", axis=1, tiled=True),
        ),
        block_rows,
    )
    log_total = best + jnp.log(total)
    attn_heads = accum / total[..., None]
    attn_low = attn_heads.reshape(seq_count, block_rows, width).astype(jnp.bfloat16)
    mixed = lax.all_to_all(attn_low, "ulysses", split_axis=1, concat_axis=2, tiled=True)
    attn_branch = project(mixed, full_out)
    hidden = residual + attn_branch
    normed_ffn_f, hatted_ffn, factor_ffn = norm_rows(hidden, full_gain_ffn.astype(jnp.float32))
    normed_ffn = normed_ffn_f.astype(jnp.bfloat16)
    gate = project(normed_ffn, full_gate)
    up_proj = project(normed_ffn, full_up)
    sigmoid_gate = jax.nn.sigmoid(gate)
    silu_gate = gate * sigmoid_gate
    act = (silu_gate * up_proj).astype(jnp.bfloat16)
    ffn_branch = project(act, full_down)
    output_f = hidden + ffn_branch
    output = output_f.astype(jnp.bfloat16)
    squares = lax.psum(
        (
            jnp.sum(residual * residual),
            jnp.sum(attn_branch * attn_branch),
            jnp.sum(output_f * output_f),
        ),
        ("ulysses", "blk"),
    )
    entry_count = residual.size * lax.axis_size("ulysses") * lax.axis_size("blk")
    statistics = jnp.sqrt(jnp.stack(squares) / entry_count)
    again = (
        lax.all_gather(w_query, ("ulysses", "blk"), axis=0, tiled=True),
        lax.all_gather(w_key, ("ulysses", "blk"), axis=0, tiled=True),
        lax.all_gather(w_value, ("ulysses", "blk"), axis=0, tiled=True),
        lax.all_gather(w_out, ("ulysses", "blk"), axis=0, tiled=True),
        lax.all_gather(w_gate, ("ulysses", "blk"), axis=0, tiled=True),
        lax.all_gather(w_up, ("ulysses", "blk"), axis=0, tiled=True),
        lax.all_gather(w_down, ("ulysses", "blk"), axis=0, tiled=True),
        lax.all_gather(gain_attn, ("ulysses", "blk"), axis=0, tiled=True),
        lax.all_gather(gain_ffn, ("ulysses", "blk"), axis=0, tiled=True),
    )
    (
        back_query,
        back_key,
        back_value,
        back_out,
        back_gate,
        back_up,
        back_down,
        back_gain_attn,
        back_gain_ffn,
    ) = again
    grad_act = project_back(grad_out, back_down)
    grad_gate = (grad_act * up_proj * sigmoid_gate * (1.0 + gate * (1.0 - sigmoid_gate))).astype(
        jnp.bfloat16
    )
    grad_up = (grad_act * silu_gate).astype(jnp.bfloat16)
    grad_normed_ffn = project_back(grad_gate, back_gate) + project_back(grad_up, back_up)
    grad_ffn_norm, grad_gain_ffn = norm_back(
        grad_normed_ffn, hatted_ffn, factor_ffn, back_gain_ffn.astype(jnp.float32)
    )
    grad_hidden = grad_out.astype(jnp.float32) + grad_ffn_norm
    grad_branch = grad_hidden.astype(jnp.bfloat16)
    grad_mixed = project_back(grad_branch, back_out).astype(jnp.bfloat16)
    dout_head = lax.all_to_all(grad_mixed, "ulysses", split_axis=2, concat_axis=1, tiled=True)
    dout_four = split_heads(dout_head)
    row_dot = jnp.sum(dout_four.astype(jnp.float32) * attn_heads, axis=-1)

    def grad_rows(running, pieces, first_row):
        key_rows, value_rows = pieces
        key_count = key_rows.shape[1]

        def grad_compute(current):
            grad_query, grad_keys, grad_values = current
            key_part = split_heads(key_rows)
            allowed = allowed_mask(segments, query_start, block_rows, first_row, key_count)
            scores = (
                jnp.einsum(
                    "sqhd,skhd->sqhk", query_four, key_part, preferred_element_type=jnp.float32
                )
                * score_scale
            )
            probs = jnp.where(allowed, jnp.exp(scores - log_total[..., None]), 0.0)
            prob_grad = jnp.einsum(
                "sqhd,skhd->sqhk",
                dout_four,
                split_heads(value_rows),
                preferred_element_type=jnp.float32,
            )
            score_grad = (probs * (prob_grad - row_dot[..., None])).astype(jnp.bfloat16)
            grad_query = (
                grad_query
                + jnp.einsum(
                    "sqhk,skhd->sqhd", score_grad, key_part, preferred_element_type=jnp.float32
                )
                * score_scale
            )
            key_term = (
                jnp.einsum(
                    "sqhk,sqhd->skhd", score_grad, query_four, preferred_element_type=jnp.float32
                )
                * score_scale
            )
            value_term = jnp.einsum(
                "sqhk,sqhd->skhd",
                probs.astype(jnp.bfloat16),
                dout_four,
                preferred_element_type=jnp.float32,
            )
            return (
                grad_query,
                add_rows(grad_keys, key_term, first_row),
                add_rows(grad_values, value_term, first_row),
            )

        return lax.cond(first_row <= query_start + block_rows - 1, grad_compute, unchanged, running)

    full_zeros = jnp.zeros((seq_count, full_rows, heads_local, HD), jnp.float32)
    grad_query_own, grad_keys_all, grad_values_all = over_blocks(
        grad_rows,
        (head_zeros, full_zeros, full_zeros),
        (
            lax.all_gather(key_head, "blk", axis=1, tiled=True),
            lax.all_gather(value_head, "blk", axis=1, tiled=True),
        ),
        block_rows,
    )
    grad_key_own, grad_value_own = (
        lax.psum_scatter(
            grad_keys_all.reshape(seq_count, full_rows, width).astype(jnp.bfloat16),
            "blk",
            scatter_dimension=1,
            tiled=True,
        ).astype(jnp.float32),
        lax.psum_scatter(
            grad_values_all.reshape(seq_count, full_rows, width).astype(jnp.bfloat16),
            "blk",
            scatter_dimension=1,
            tiled=True,
        ).astype(jnp.float32),
    )
    grad_query_own = grad_query_own.reshape(seq_count, block_rows, width)
    grad_query_tok, grad_key_tok, grad_value_tok = (
        lax.all_to_all(
            grad_query_own.astype(jnp.bfloat16), "ulysses", split_axis=1, concat_axis=2, tiled=True
        ),
        lax.all_to_all(
            grad_key_own.astype(jnp.bfloat16), "ulysses", split_axis=1, concat_axis=2, tiled=True
        ),
        lax.all_to_all(
            grad_value_own.astype(jnp.bfloat16), "ulysses", split_axis=1, concat_axis=2, tiled=True
        ),
    )
    grad_query_raw = rotate(grad_query_tok.astype(jnp.float32), cosine, sine, False).astype(
        jnp.bfloat16
    )
    grad_key_raw = rotate(grad_key_tok.astype(jnp.float32), cosine, sine, False).astype(
        jnp.bfloat16
    )
    grad_v_first = grad_value_tok * 0.5
    grad_normed = (
        project_back(grad_query_raw, back_query)
        + project_back(grad_key_raw, back_key)
        + project_back(grad_v_first, back_value)
    )
    grad_attn_norm, grad_gain_attn = norm_back(
        grad_normed, hatted_attn, factor_attn, back_gain_attn.astype(jnp.float32)
    )
    grad_inputs = (grad_hidden + grad_attn_norm).astype(jnp.bfloat16)
    model_width = w_query.shape[1]
    hidden_width = w_gate.shape[1]
    owned = lax.psum_scatter(
        jnp.concatenate(
            [
                weight_grad(normed, grad_query_raw),
                weight_grad(normed, grad_key_raw),
                weight_grad(normed, grad_v_first),
                weight_grad(mixed, grad_branch),
                weight_grad(normed_ffn, grad_gate),
                weight_grad(normed_ffn, grad_up),
                grad_gain_attn[:, None],
                grad_gain_ffn[:, None],
            ],
            axis=1,
        ),
        ("ulysses", "blk"),
        scatter_dimension=0,
        tiled=True,
    )
    grad_w_down = lax.psum_scatter(
        weight_grad(act, grad_out), ("ulysses", "blk"), scatter_dimension=0, tiled=True
    )
    column = 0
    pieces = []
    for span in (model_width, model_width, model_width, model_width, hidden_width, hidden_width):
        pieces.append(owned[:, column : column + span])
        column = column + span
    grad_gain_attn_own = owned[:, column]
    grad_gain_ffn_own = owned[:, column + 1]
    return (
        output,
        grad_inputs,
        grad_v_first,
        pieces[0],
        pieces[1],
        pieces[2],
        pieces[3],
        pieces[4],
        pieces[5],
        grad_w_down,
        grad_gain_attn_own,
        grad_gain_ffn_own,
        statistics,
    )


MESH = pl.DeviceIdType.MESH
LANES = 128
VMEM_BYTES = 61 << 20
f32 = jnp.float32
bf16 = jnp.bfloat16
QB, KB = 512, 256


class Copy:
    def __init__(self, copy, send_at, recv_at, when):
        self.copy, self.at, self.recv_at, self.when = copy, send_at, recv_at, when

    def wait_recv(self):
        self.copy.wait_recv()

    def wait_send(self):
        if self.when is None:
            self.copy.wait_send()
        else:
            pl.when(self.when)(self.copy.wait_send)


class Net:
    def __init__(self, send_sems, recv_sems):
        self.send_sems, self.recv_sems = send_sems, recv_sems
        self.count, self.open = 0, []

    def push(self, src, dst, u, b, when=None, recv_at=None, at=None):
        if at is None:
            at = self.count
            self.count += 1
        recv_at = at if recv_at is None else recv_at
        copy = pltpu.make_async_remote_copy(
            src_ref=src,
            dst_ref=dst,
            send_sem=self.send_sems.at[at],
            recv_sem=self.recv_sems.at[recv_at],
            device_id=(u, b),
            device_id_type=MESH,
        )
        if when is None:
            copy.start()
        else:
            pl.when(when)(copy.start)
        made = Copy(copy, at, recv_at, when)
        self.open.append(made)
        return made

    def sent(self, copies):
        for copy in copies:
            copy.wait_send()
        self.open = [copy for copy in self.open if copy not in copies]

    def drain(self):
        for copy in self.open:
            copy.wait_send()
        self.open = []


def arrive(copies):
    for copy in copies:
        copy.wait_recv()


def here():
    return lax.axis_index("ulysses"), lax.axis_index("blk")


def greet(u, b, n_u, n_b):
    barrier = pltpu.get_barrier_semaphore()
    for off in range(1, n_u):
        pl.semaphore_signal(barrier, inc=1, device_id=(u ^ off, b), device_id_type=MESH)
    for off in range(1, n_b):
        pl.semaphore_signal(barrier, inc=1, device_id=(u, b ^ off), device_id_type=MESH)
    pl.semaphore_wait(barrier, n_u - 1 + n_b - 1)


def dot(left, right):
    return jnp.dot(left, right, preferred_element_type=f32)


def dot_nt(left, right):
    return lax.dot_general(left, right, (((1,), (1,)), ((), ())), preferred_element_type=f32)


def dot_tn(left, right):
    return lax.dot_general(left, right, (((0,), (0,)), ((), ())), preferred_element_type=f32)


def at_block(index, size):
    return pl.ds(pl.multiple_of(index * size, size), size)


def lane_of(shape):
    return lax.broadcasted_iota(jnp.int32, shape, len(shape) - 1)


def swap_halves(tile):
    return pltpu.roll(tile, HD, tile.ndim - 1)


def partner(tile):
    low = lane_of(tile.shape) % HD < HD // 2
    return jnp.where(low, pltpu.roll(tile, LANES - HD // 2, 1), pltpu.roll(tile, HD // 2, 1))


def pack_rows(rows):
    half = rows.shape[0] // 2
    low = lane_of((half, LANES)) < HD
    return jnp.where(low, rows[:half], swap_halves(rows[half:]))


def unpack_rows(packed):
    return jnp.concatenate([packed, swap_halves(packed)], axis=0)


class Gather:
    def __init__(self, net, slot, u, b):
        self.net, self.slot, self.u, self.b = net, slot, u, b
        self.inner = ((b // 2) == 1) | ((b // 2) == 2)
        mine = slot(b)
        self.two = net.push(mine, mine, u, b ^ 4)
        self.one = net.push(mine, mine, u, b ^ 2)
        self.three = net.push(mine, mine, u, b ^ 6, when=self.inner)
        self.side = [net.push(mine, mine, u, b ^ 1)]

    def beside(self, owner):
        got = self.slot(owner)
        self.side.append(self.net.push(got, got, self.u, self.b ^ 1))

    def forward(self):
        self.two.wait_recv()
        got = self.slot(self.b ^ 4)
        self.net.push(got, got, self.u, self.b ^ 2, when=self.inner, recv_at=self.three.at)
        self.beside(self.b ^ 4)

    def relay(self):
        self.one.wait_recv()
        self.beside(self.b ^ 2)
        self.three.wait_recv()
        self.beside(self.b ^ 6)

    def finish(self):
        arrive(self.side)


class Scatter:
    def __init__(self, net, u, b, mine, paired, summed, landed):
        self.net, self.u, self.b = net, u, b
        self.mine, self.paired, self.summed, self.landed = mine, paired, summed, landed
        self.z = b // 2
        self.inner = (self.z == 1) | (self.z == 2)
        self.swap = [net.push(mine(z, 1 - b % 2), paired.at[z], u, b ^ 1) for z in range(4)]

    def add(self, z):
        self.summed[z] = (self.mine(z, self.b % 2)[...].astype(f32) + self.paired[z].astype(f32)).astype(bf16)

    def middle(self):
        net, u, b, z, inner = self.net, self.u, self.b, self.z, self.inner
        outer = jnp.logical_not(inner)
        arrive(self.swap)
        self.add(z ^ 3)
        far = self.summed.at[z ^ 3]
        self.extra = net.push(far, self.landed.at[3], u, b ^ 2, when=outer)
        self.three = net.push(far, self.landed.at[2], u, b ^ 6, when=inner)
        self.add(z ^ 2)
        self.two = net.push(self.summed.at[z ^ 2], self.landed.at[1], u, b ^ 4, when=outer)
        self.add(z ^ 1)
        self.one = net.push(self.summed.at[z ^ 1], self.landed.at[0], u, b ^ 2)
        self.add(z)

    def merge(self):
        net, u, b, z = self.net, self.u, self.b, self.z

        @pl.when(self.inner)
        def _():
            self.extra.wait_recv()
            self.summed[z ^ 2] = (self.summed[z ^ 2].astype(f32) + self.landed[3].astype(f32)).astype(bf16)

        net.push(self.summed.at[z ^ 2], self.landed.at[1], u, b ^ 4, when=self.inner, at=self.two.at)

    def finish(self, total):
        self.one.wait_recv()
        self.two.wait_recv()
        total[...] = (
            self.summed[self.z].astype(f32) + self.landed[0].astype(f32) + self.landed[1].astype(f32)
        ).astype(total.dtype)

        @pl.when(self.inner)
        def _():
            self.three.wait_recv()
            total[...] = (total[...].astype(f32) + self.landed[2].astype(f32)).astype(total.dtype)


def fill_units(units, tb, store):
    def one(block, carry):
        low = lane_of((tb, LANES)) < HD
        tile = units[block, 0:tb].astype(f32)
        query = jnp.where(low, tile * HD ** (-0.5), 0.0)
        key = jnp.where(low, swap_halves(tile), 0.0)
        value = jnp.where(low, unpack_rows(units[block, tb:].astype(f32)), 0.0)
        store(block, query, key, value)
        return carry

    lax.fori_loop(0, units.shape[0], one, 0)


def allowed_block(first_key, first_query, low_row):
    key_place = first_key + lax.broadcasted_iota(jnp.int32, (KB, QB), 0)
    query_place = first_query + lax.broadcasted_iota(jnp.int32, (KB, QB), 1)
    return (key_place <= query_place) & (key_place >= low_row)


def layer_kernel(dims, names, *refs):
    n_u, n_b, seqs, td, rows, heads = dims
    r = types.SimpleNamespace(**dict(zip(names, refs)))
    tb = n_u * td
    tokens = seqs * tb
    seq = n_b * tb
    n_z = n_b // 2
    width = r.x.shape[2]
    u, b = here()
    net = Net(r.send_sems, r.recv_sems)
    others = [u ^ off for off in range(1, n_u)]
    slab = at_block(u, td)
    mine = at_block(b, rows)
    ff = r.wdg.shape[0]
    ff_rows = ff // n_b

    def part(v):
        return at_block(v, td)

    greet(u, b, n_u, n_b)
    got_w = [net.push(r.wqkv.at[v], r.wq.at[u, mine], v, b) for v in others]
    got_g = [net.push(r.gains, r.gbuf.at[b, u], v, b) for v in others]
    r.wo[mine] = r.wout[...]
    g_out = Gather(net, lambda c: r.wo.at[at_block(c, rows)], u, b)
    got_x = [net.push(r.x, r.xg.at[:, slab], v, b) for v in others]
    r.wq[u, mine] = r.wqkv[u]
    r.gbuf[b, u] = r.gains[...]
    r.xg[:, slab] = r.x[...]
    r.vfg[:, slab] = r.vf[u]
    r.gog[:, slab] = r.go[...]
    arrive(got_w)
    g_qkv = Gather(net, lambda c: r.wq.at[:, at_block(c, rows)], u, b)
    arrive(got_g)
    got_g = [net.push(r.gbuf.at[b], r.gbuf.at[b], u, b ^ off) for off in range(1, n_b)]
    got_v = [net.push(r.vf.at[v], r.vfg.at[:, slab], v, b) for v in others]
    r.wg[u, mine] = r.wgu[u]
    got_o = [net.push(r.wgu.at[v], r.wg.at[u, mine], v, b) for v in others]
    arrive(got_g)
    per_tile = LANES // rows
    for tile in range(n_u * n_b // per_tile):
        total = None
        for index in range(tile * per_tile, (tile + 1) * per_tile):
            term = r.gbuf[index % n_b, index // n_b]
            total = term if total is None else total + term
        r.gain[:, tile * LANES : (tile + 1) * LANES] = total
    arrive(got_x)

    def norm(step, carry):
        s, place = step // 2, at_block(step % 2, tb // 2)
        values = r.xg[s, place].astype(f32)
        factor = lax.rsqrt(jnp.mean(values * values, axis=-1, keepdims=True) + epsilon)
        r.normed[s, place] = (values * factor * r.gain[0:1, :]).astype(bf16)
        return carry

    lax.fori_loop(0, 2 * seqs, norm, 0)
    got_go = [net.push(r.go, r.gog.at[:, slab], v, b) for v in others]
    g_out.forward()
    g_qkv.forward()
    arrive(got_v)
    g_qkv.relay()
    g_qkv.finish()

    for s in range(seqs):
        left = r.normed[s]
        for n in range(heads // 2):
            found = dot(left, r.wq[:, :, n * 256 : (n + 1) * 256].reshape(width, 256))
            for i in range(2):
                tile = found[:, i * LANES : (i + 1) * LANES]
                turned = tile * r.cosr[s] + partner(tile) * r.sinr[s]
                r.stage[s * heads + 2 * n + i, 0:tb] = turned.astype(bf16)
        for n in range(heads // 4):
            first_lane = heads * LANES + n * 256
            found = dot(left, r.wq[:, :, first_lane : first_lane + 256].reshape(width, 256))
            for i in range(2):
                first = r.vfg[s, :, n * 256 + i * LANES : n * 256 + (i + 1) * LANES].astype(f32)
                value = 0.5 * found[:, i * LANES : (i + 1) * LANES] + 0.5 * first
                unit = s * heads + 4 * n + 2 * i
                r.stage[unit, tb:] = pack_rows(value).astype(bf16)
                r.stage[unit + 1, tb:] = pack_rows(swap_halves(value)).astype(bf16)
    got_q = [net.push(r.stage.at[b ^ off], r.units.at[b], u, b ^ off) for off in range(n_b - 1, 0, -1)]
    r.units[b] = r.stage[b]
    r.wdg[at_block(b, ff_rows)] = r.wd[...]
    g_out.relay()
    arrive(got_q)
    g_out.finish()

    g_down = Gather(net, lambda c: r.wdg.at[at_block(c, ff_rows)], u, b)

    def store(block, query, key, value):
        place = at_block(block, tb)
        r.keys[place] = key.astype(bf16)
        r.key_t[:, place] = jnp.transpose(key)[:HD].astype(bf16)
        r.query[place] = query.astype(bf16)
        r.query_t[:, place] = jnp.transpose(query).astype(bf16)
        r.value[place] = value.astype(bf16)
        r.value_t[:, place] = jnp.transpose(value)[:HD].astype(bf16)

    fill_units(r.units, tb, store)

    def attend(qb, carry):
        q_at = at_block(qb, QB)
        query = r.query_t[:, q_at]
        low_row = r.low[0:1, q_at]
        r.acc[...] = jnp.zeros_like(r.acc)

        def inner(kb, state):
            best, total = state
            k_at = at_block(kb, KB)
            scores = dot(r.keys[k_at], query)
            scores = jnp.where(allowed_block(kb * KB, qb * QB, low_row), scores, neg_big)
            new_best = jnp.maximum(best, jnp.max(scores, axis=0, keepdims=True))
            weights = jnp.exp(scores - new_best)
            rescale = jnp.exp(best - new_best)
            total = total * rescale + jnp.sum(weights, axis=0, keepdims=True)
            r.acc[...] = r.acc[...] * rescale + dot(r.value_t[:, k_at], weights.astype(bf16))
            return new_best, total

        start = (jnp.full((1, QB), neg_big, f32), jnp.zeros((1, QB), f32))
        best, total = lax.fori_loop(0, (qb + 1) * (QB // KB), inner, start)
        out = r.acc[...] / total
        r.heads_t[:, q_at] = out
        r.lse[:, q_at] = jnp.broadcast_to(best + jnp.log(total), (8, QB))
        turned = jnp.transpose(jnp.concatenate([out, jnp.zeros_like(out)], axis=0))
        for i in range(QB // tb):
            r.ostage[qb * (QB // tb) + i] = pack_rows(turned[i * tb : (i + 1) * tb]).astype(bf16)
        return carry

    lax.fori_loop(0, seq // QB, attend, 0)
    got = [net.push(r.ostage.at[b ^ off], r.parts.at[b], u, b ^ off) for off in range(n_b - 1, 0, -1)]
    r.parts[b] = r.ostage[b]
    g_down.forward()
    arrive(got)
    arrive(got_o)
    g_gate = Gather(net, lambda c: r.wg.at[:, at_block(c, rows)], u, b)
    half = tb // 2
    for s in range(seqs):
        for pair in range(heads // 2):
            one = r.parts[s * heads + 2 * pair].astype(f32)
            two = r.parts[s * heads + 2 * pair + 1].astype(f32)
            low_lane = lane_of(one.shape) < HD
            lanes = slice(pair * LANES, (pair + 1) * LANES)
            r.mix[s, :half, lanes] = jnp.where(low_lane, one, swap_halves(two)).astype(bf16)
            r.mix[s, half:, lanes] = jnp.where(low_lane, swap_halves(one), two).astype(bf16)

    def project_out(s, carry):
        r.branch[s] = dot(r.mix[s], r.wo[...]).astype(bf16)
        return carry

    lax.fori_loop(0, seqs, project_out, 0)
    got = [net.push(r.branch.at[:, part(v)], r.landed_b.at[u], v, b) for v in others]
    r.landed_b[u] = r.branch[:, slab]
    g_down.relay()
    arrive(got)
    r.sums[...] = jnp.zeros_like(r.sums)
    for s in range(seqs):
        total = sum(r.landed_b[v, s].astype(f32) for v in range(n_u))
        own = r.x[s].astype(f32)
        hid = own + total
        r.hidden[s] = hid
        factor = lax.rsqrt(jnp.mean(hid * hid, axis=-1, keepdims=True) + epsilon)
        r.nf_own[s] = (hid * factor * r.gain[1:2, :]).astype(bf16)
        r.sums[0:1] = r.sums[0:1] + jnp.sum(own * own, axis=0, keepdims=True)
        r.sums[1:2] = r.sums[1:2] + jnp.sum(total * total, axis=0, keepdims=True)
    got = [net.push(r.nf_own, r.nf.at[:, slab], v, b) for v in others]
    r.nf[:, slab] = r.nf_own[...]
    arrive(got_go)
    g_down.finish()
    g_gate.forward()
    g_gate.relay()
    arrive(got)
    g_gate.finish()

    def hidden_units(s, carry):
        left = r.nf[s]
        grad = r.gog[s]
        for n in range(ff // 256):
            span = slice(n * 256, (n + 1) * 256)
            up_span = slice(ff + n * 256, ff + (n + 1) * 256)
            gate = dot(left, r.wg[:, :, span].reshape(width, 256))
            up = dot(left, r.wg[:, :, up_span].reshape(width, 256))
            grad_act = dot_nt(grad, r.wdg[span])
            sig = 1.0 / (1.0 + jnp.exp(-gate))
            silu = gate * sig
            r.act[s, :, span] = (silu * up).astype(bf16)
            r.dgu[s, :, span] = (grad_act * up * sig * (1.0 + gate * (1.0 - sig))).astype(bf16)
            r.dgu[s, :, up_span] = (grad_act * silu).astype(bf16)
        return carry

    lax.fori_loop(0, seqs, hidden_units, 0)

    def back_units(s, carry):
        left = r.dgu[s]
        for v in range(n_u):
            r.d_low[s, :, v * 256 : (v + 1) * 256] = dot_nt(left, r.wg[v]).astype(bf16)
        return carry

    lax.fori_loop(0, seqs, back_units, 0)
    got_d = [net.push(r.d_low.at[:, part(v)], r.landed_d.at[u], v, b) for v in others]
    r.landed_d[u] = r.d_low[:, slab]

    half_units = ff // 2
    for n in range(2):
        span = slice(n * half_units, (n + 1) * half_units)
        found = dot_tn(r.act[:, :, span].reshape(tokens, half_units), r.gog[...].reshape(tokens, width))
        r.wd_buf[n * (n_z // 2) : (n + 1) * (n_z // 2)] = found.astype(bf16).reshape(
            n_z // 2, 2, ff_rows, width
        )
    s_down = Scatter(net, u, b, lambda z, c: r.wd_buf.at[z, c], r.wd_pair, r.wd_sum, r.wd_land)
    for v in range(n_u):
        left = r.nf[:, :, v * 256 : (v + 1) * 256].reshape(tokens, 256)
        found = dot_tn(left, r.dgu[...].reshape(tokens, 2 * ff))
        r.wg_buf[:, :, v] = found.astype(bf16).reshape(n_z, 2, rows, 2 * ff)
        if v == 1:
            s_down.middle()
    s_gate = Scatter(net, u, b, lambda z, c: r.wg_buf.at[z, c], r.wg_pair, r.wg_sum, r.wg_land)

    arrive(got_d)
    for s in range(seqs):
        grad_normed = sum(r.landed_d[v, s].astype(f32) for v in range(n_u))
        hid = r.hidden[s]
        factor = lax.rsqrt(jnp.mean(hid * hid, axis=-1, keepdims=True) + epsilon)
        hat = hid * factor
        scaled = grad_normed * r.gain[1:2, :]
        inner = jnp.mean(scaled * hat, axis=-1, keepdims=True)
        total = r.go[s].astype(f32) + factor * (scaled - hat * inner)
        r.ghid[s] = total
        r.gb_own[s] = total.astype(bf16)
        r.sums[4:5] = r.sums[4:5] + jnp.sum(grad_normed * hat, axis=0, keepdims=True)
    got_b = [net.push(r.gb_own, r.gb.at[:, slab], v, b) for v in others]
    r.gb[:, slab] = r.gb_own[...]
    s_down.merge()

    def forward(s, carry):
        r.f_low[s] = dot(r.act[s], r.wdg[...]).astype(bf16)
        return carry

    lax.fori_loop(0, seqs, forward, 0)
    arrive(got_b)
    for s in range(seqs):
        for pair in range(heads // 2):
            found = dot_nt(r.gb[s], r.wo[pair * LANES : (pair + 1) * LANES])
            r.ostage2[s * heads + 2 * pair] = pack_rows(found).astype(bf16)
            r.ostage2[s * heads + 2 * pair + 1] = pack_rows(swap_halves(found)).astype(bf16)
    got_u = [net.push(r.ostage2.at[b ^ off], r.grads.at[b], u, b ^ off) for off in range(n_b - 1, 0, -1)]
    r.grads[b] = r.ostage2[b]
    got_f = [net.push(r.f_low.at[:, part(v)], r.landed_f.at[u], v, b) for v in others]
    r.landed_f[u] = r.f_low[:, slab]
    found = dot_tn(r.mix[...].reshape(tokens, heads * HD), r.gb[...].reshape(tokens, width))
    r.wo_buf[...] = found.astype(bf16).reshape(n_z, 2, rows, width)
    s_out = Scatter(net, u, b, lambda z, c: r.wo_buf.at[z, c], r.wo_pair, r.wo_sum, r.wo_land)
    arrive(got_u)
    s_gate.middle()

    def more(block, carry):
        place = at_block(block, tb)
        g = unpack_rows(r.grads[block].astype(f32))
        g = jnp.where(lane_of(g.shape) < HD, g, 0.0)
        r.grad[place] = g.astype(bf16)
        turned = jnp.transpose(g)
        r.grad_t[:, place] = turned.astype(bf16)
        total = jnp.sum(turned[:HD] * r.heads_t[:, place], axis=0, keepdims=True)
        r.row_dot[:, place] = jnp.broadcast_to(total, (8, tb))
        return carry

    lax.fori_loop(0, n_b, more, 0)
    r.dq_t[...] = jnp.zeros_like(r.dq_t)
    net.sent(got_q)

    def outer(kb, carry):
        k_at = at_block(kb, KB)
        r.dk[...] = jnp.zeros_like(r.dk)
        r.dv[...] = jnp.zeros_like(r.dv)

        def inner(qb, carry):
            q_at = at_block(qb, QB)
            scores = dot(r.keys[k_at], r.query_t[:, q_at])
            seen = allowed_block(kb * KB, qb * QB, r.low[0:1, q_at])
            probs = jnp.where(seen, jnp.exp(scores - r.lse[0:1, q_at]), 0.0)
            prob_grad = dot(r.value[k_at], r.grad_t[:, q_at])
            score_grad = (probs * (prob_grad - r.row_dot[0:1, q_at])).astype(bf16)
            r.dv[...] += dot(probs.astype(bf16), r.grad[q_at])
            r.dk[...] += dot(score_grad, r.query[q_at])
            r.dq_t[:, q_at] += dot(r.key_t[:, k_at], score_grad)
            return carry

        lax.fori_loop(kb // (QB // KB), seq // QB, inner, 0)
        low_lane = lane_of((KB, LANES)) < HD
        r.stage[kb, 0:tb] = jnp.where(low_lane, 0.0, swap_halves(r.dk[...])).astype(bf16)
        r.stage[kb, tb:] = pack_rows(r.dv[...]).astype(bf16)
        return carry

    lax.fori_loop(0, seq // KB, outer, 0)

    def turn_query(block, carry):
        columns = r.dq_t[:, at_block(block, tb)] * HD ** (-0.5)
        turned = jnp.transpose(jnp.concatenate([columns, jnp.zeros_like(columns)], axis=0))
        low_lane = lane_of(turned.shape) < HD
        r.stage[block, 0:tb] = jnp.where(low_lane, turned, r.stage[block, 0:tb].astype(f32)).astype(bf16)
        return carry

    lax.fori_loop(0, n_b, turn_query, 0)
    got = [net.push(r.stage.at[b ^ off], r.returned.at[b], u, b ^ off) for off in range(n_b - 1, 0, -1)]
    r.returned[b] = r.stage[b]
    s_gate.merge()
    s_out.middle()
    arrive(got_f)
    for s in range(seqs):
        total = r.hidden[s] + sum(r.landed_f[v, s].astype(f32) for v in range(n_u))
        r.out[s] = total.astype(bf16)
        r.sums[2:3] = r.sums[2:3] + jnp.sum(total * total, axis=0, keepdims=True)
    s_down.finish(r.dwd)
    arrive(got)

    wide = heads * LANES
    for s in range(seqs):
        for head in range(heads):
            tile = r.returned[s * heads + head, 0:tb].astype(f32)
            turned = tile * r.cosr[s] - partner(tile) * r.sinr[s]
            r.raw[s, :, head * LANES : (head + 1) * LANES] = turned.astype(bf16)
        for pair in range(heads // 2):
            one = unpack_rows(r.returned[s * heads + 2 * pair, tb:].astype(f32))
            two = unpack_rows(r.returned[s * heads + 2 * pair + 1, tb:].astype(f32))
            both = 0.5 * jnp.where(lane_of(one.shape) < HD, one, swap_halves(two))
            r.raw[s, :, wide + pair * LANES : wide + (pair + 1) * LANES] = both.astype(bf16)
    columns = r.raw.shape[2]
    for v in range(n_u):
        left = r.normed[:, :, v * 256 : (v + 1) * 256].reshape(tokens, 256)
        found = dot_tn(left, r.raw[...].reshape(tokens, columns))
        r.wq_buf[:, :, v] = found.astype(bf16).reshape(n_z, 2, rows, columns)
    s_qkv = Scatter(net, u, b, lambda z, c: r.wq_buf.at[z, c], r.wq_pair, r.wq_sum, r.wq_land)
    s_out.merge()

    def back_inputs(s, carry):
        left = r.raw[s]
        for v in range(n_u):
            r.gin_low[s, :, v * 256 : (v + 1) * 256] = dot_nt(left, r.wq[v]).astype(bf16)
        return carry

    lax.fori_loop(0, seqs, back_inputs, 0)
    got_g = [net.push(r.gin_low.at[:, part(v)], r.landed_g.at[u], v, b) for v in others]
    r.landed_g[u] = r.gin_low[:, slab]
    s_qkv.middle()
    got_v = [net.push(r.raw.at[:, part(v), pl.ds(wide, heads * HD)], r.gv.at[u], v, b) for v in others]
    r.gv[u] = r.raw[:, slab, wide:]
    s_gate.finish(r.wg_low)
    got_c = [net.push(r.wg_low.at[v], r.dwgu.at[u], v, b) for v in others]
    r.dwgu[u] = r.wg_low[u]
    s_qkv.merge()
    s_out.finish(r.dwo)
    arrive(got_g)
    for s in range(seqs):
        grad_normed = sum(r.landed_g[v, s].astype(f32) for v in range(n_u))
        own = r.x[s].astype(f32)
        factor = lax.rsqrt(jnp.mean(own * own, axis=-1, keepdims=True) + epsilon)
        hat = own * factor
        scaled = grad_normed * r.gain[0:1, :]
        inner = jnp.mean(scaled * hat, axis=-1, keepdims=True)
        r.gin[s] = (r.ghid[s] + factor * (scaled - hat * inner)).astype(bf16)
        r.sums[3:4] = r.sums[3:4] + jnp.sum(grad_normed * hat, axis=0, keepdims=True)
    got_s = [net.push(r.sums, r.sums_u.at[u], v, b) for v in others]
    r.sums_u[u] = r.sums[...]
    arrive(got_s)
    r.sums_b[b] = sum(r.sums_u[v] for v in range(n_u))
    got_s = [net.push(r.sums_b.at[b], r.sums_b.at[b], u, b ^ off) for off in range(1, n_b)]
    arrive(got_v)
    for v in range(n_u):
        r.gvf[:, :, v * 256 : (v + 1) * 256] = r.gv[v]
    arrive(got_s)
    r.totals[...] = sum(r.sums_b[c] for c in range(n_b))
    s_qkv.finish(r.wq_low)
    got = [net.push(r.wq_low.at[v], r.dwq.at[u], v, b) for v in others]
    r.dwq[u] = r.wq_low[u]
    arrive(got_c)
    arrive(got)
    net.drain()


def pad_to(values, axis, size):
    widths = [(0, 0)] * values.ndim
    widths[axis] = (0, size - values.shape[axis])
    return jnp.pad(values, widths)


def local_units(
    inputs, v_first, grad_out, positions, segments,
    w_query, w_key, w_value, w_out, w_gate, w_up, w_down, gain_attn, gain_ffn,
):
    n_u, n_b = lax.axis_size("ulysses"), lax.axis_size("blk")
    u, b = here()
    seqs, td, width = inputs.shape
    rows = w_query.shape[0]
    heads = HEADS // n_u
    tb = n_u * td
    seq = n_b * tb
    ff_own = w_down.shape[0]
    ff_pad = -(-ff_own // 32) * 32
    ff = ff_pad * n_b
    dims = (n_u, n_b, seqs, td, rows, heads)

    place = jnp.arange(seq, dtype=jnp.int32)
    cut = jnp.sum(1 - segments, axis=1, keepdims=True)
    first = jnp.where(segments == 1, cut, 0)
    low = lax.dynamic_slice_in_dim(first, b // heads, 1, 0)
    low = jnp.broadcast_to(low, (8, seq))
    local_place = (place[None, :] - first).astype(f32)
    angle_rows = lax.dynamic_slice_in_dim(local_place, b * tb, tb, 1)
    inverse = rope_base ** (-2.0 * jnp.arange(HD // 2, dtype=f32) / HD)
    angles = angle_rows[:, :, None] * inverse
    cosine, sine = jnp.cos(angles), jnp.sin(angles)
    cosr = jnp.concatenate([cosine] * 4, axis=-1)
    sinr = jnp.concatenate([-sine, sine] * 2, axis=-1)

    qk = jnp.stack([w_query.reshape(rows, n_u, heads, HD), w_key.reshape(rows, n_u, heads, HD)], axis=3)
    wqkv = jnp.concatenate(
        [qk.reshape(rows, n_u, heads * 2 * HD), w_value.reshape(rows, n_u, heads * HD)], axis=2
    )
    wqkv = jnp.moveaxis(wqkv, 1, 0)

    def hidden_columns(weight):
        parted = pad_to(weight.reshape(rows, n_u, n_b, ff_own), 3, ff_pad)
        return parted.reshape(rows, n_u, ff)

    wgu = jnp.moveaxis(
        jnp.concatenate([hidden_columns(w_gate), hidden_columns(w_up)], axis=2), 1, 0
    )
    wd = pad_to(w_down, 0, ff_pad)
    vf = jnp.moveaxis(v_first.reshape(seqs, td, n_u, heads * HD), 2, 0)
    pair = jnp.stack([gain_attn, gain_ffn]).astype(f32)
    lane = (jnp.arange(LANES) // rows) == (u * n_b + b) % (LANES // rows)
    gains = pad_to(jnp.where(lane[None, :], jnp.tile(pair, (1, LANES // rows)), 0.0), 0, 8)

    columns = 3 * heads * HD
    n_z = n_b // 2
    own, block = (seqs, td, width), (seqs, tb, width)
    inputs_of = dict(
        x=inputs, vf=vf, go=grad_out, wqkv=wqkv, wgu=wgu, wout=w_out, wd=wd, gains=gains,
        cosr=cosr, sinr=sinr, low=low,
    )
    outs = dict(
        out=(own, bf16), gin=(own, bf16), gvf=(own, bf16), dwq=((n_u, rows, columns), bf16),
        dwo=((rows, width), f32), dwd=((ff_pad, width), f32), dwgu=((n_u, rows, 2 * ff), bf16),
        totals=((8, width), f32),
    )
    scratch = dict(
        xg=(block, bf16), vfg=((seqs, tb, heads * HD), bf16), gbuf=((n_b, n_u, 8, LANES), f32),
        gain=((8, width), f32), normed=(block, bf16), wq=((n_u, n_b * rows, columns), bf16),
        gog=(block, bf16), wg=((n_u, n_b * rows, 2 * ff), bf16), wdg=((ff, width), bf16),
        wo=((n_b * rows, width), bf16), stage=((n_b, tb + tb // 2, LANES), bf16),
        units=((n_b, tb + tb // 2, LANES), bf16), keys=((seq, LANES), bf16), key_t=((HD, seq), bf16),
        query=((seq, LANES), bf16), query_t=((LANES, seq), bf16), value=((seq, LANES), bf16),
        value_t=((HD, seq), bf16), acc=((HD, QB), f32), heads_t=((HD, seq), f32), lse=((8, seq), f32),
        ostage=((n_b, tb // 2, LANES), bf16), parts=((n_b, tb // 2, LANES), bf16),
        mix=((seqs, tb, heads * HD), bf16), branch=(block, bf16), landed_b=((n_u,) + own, bf16),
        sums=((8, width), f32), hidden=(own, f32), nf_own=(own, bf16), nf=(block, bf16),
        act=((seqs, tb, ff), bf16), dgu=((seqs, tb, 2 * ff), bf16), d_low=(block, bf16),
        landed_d=((n_u,) + own, bf16), ghid=(own, f32), gb_own=(own, bf16), gb=(block, bf16),
        f_low=(block, bf16), landed_f=((n_u,) + own, bf16),
        wd_buf=((n_z, 2, ff_pad, width), bf16), wd_pair=((n_z, ff_pad, width), bf16),
        wd_sum=((n_z, ff_pad, width), bf16), wd_land=((n_z, ff_pad, width), bf16),
        wg_buf=((n_z, 2, n_u, rows, 2 * ff), bf16), wg_pair=((n_z, n_u, rows, 2 * ff), bf16),
        wg_sum=((n_z, n_u, rows, 2 * ff), bf16), wg_land=((n_z, n_u, rows, 2 * ff), bf16),
        wg_low=((n_u, rows, 2 * ff), bf16),
        ostage2=((n_b, tb // 2, LANES), bf16), grads=((n_b, tb // 2, LANES), bf16),
        wo_buf=((n_z, 2, rows, width), bf16), wo_pair=((n_z, rows, width), bf16),
        wo_sum=((n_z, rows, width), bf16), wo_land=((n_z, rows, width), bf16),
        grad=((seq, LANES), bf16), grad_t=((LANES, seq), bf16), row_dot=((8, seq), f32),
        dq_t=((HD, seq), f32), dk=((KB, LANES), f32), dv=((KB, LANES), f32),
        returned=((n_b, tb + tb // 2, LANES), bf16), raw=((seqs, tb, columns), bf16),
        gin_low=(block, bf16), landed_g=((n_u,) + own, bf16), gv=((n_u, seqs, td, heads * HD), bf16),
        wq_buf=((n_z, 2, n_u, rows, columns), bf16), wq_pair=((n_z, n_u, rows, columns), bf16),
        wq_sum=((n_z, n_u, rows, columns), bf16), wq_land=((n_z, n_u, rows, columns), bf16),
        wq_low=((n_u, rows, columns), bf16), sums_u=((n_u, 8, width), f32), sums_b=((n_b, 8, width), f32),
    )
    names = [*inputs_of, *outs, *scratch, "send_sems", "recv_sems"]
    vmem = pl.BlockSpec(memory_space=pltpu.VMEM)
    results = pl.pallas_call(
        functools.partial(layer_kernel, dims, names),
        out_shape=[jax.ShapeDtypeStruct(shape, dtype) for shape, dtype in outs.values()],
        in_specs=[vmem] * len(inputs_of),
        out_specs=[vmem] * len(outs),
        scratch_shapes=[pltpu.VMEM(shape, dtype) for shape, dtype in scratch.values()]
        + [pltpu.SemaphoreType.DMA((SEMAPHORES,))] * 2,
        compiler_params=pltpu.CompilerParams(
            collective_id=1, has_side_effects=True, vmem_limit_bytes=VMEM_BYTES
        ),
        name="layer",
    )(*inputs_of.values())
    got = dict(zip(outs, results))
    dwq = jnp.moveaxis(got["dwq"].astype(f32), 0, 1)
    dqk = dwq[:, :, : heads * 2 * HD].reshape(rows, n_u, heads, 2, HD)
    grad_w_query = dqk[:, :, :, 0].reshape(rows, width)
    grad_w_key = dqk[:, :, :, 1].reshape(rows, width)
    grad_w_value = dwq[:, :, heads * 2 * HD :].reshape(rows, width)
    dwgu = jnp.moveaxis(got["dwgu"].astype(f32), 0, 1).reshape(rows, n_u, 2, n_b, ff_pad)[..., :ff_own]
    grad_w_gate = dwgu[:, :, 0].reshape(rows, w_gate.shape[1])
    grad_w_up = dwgu[:, :, 1].reshape(rows, w_gate.shape[1])
    grad_w_down = got["dwd"][:ff_own]
    gain_at = (u * n_b + b) * rows
    sums = got["totals"]
    grad_gain_attn = lax.dynamic_slice_in_dim(sums[3], gain_at, rows, 0)
    grad_gain_ffn = lax.dynamic_slice_in_dim(sums[4], gain_at, rows, 0)
    statistics = jnp.sqrt(jnp.sum(sums[:3], axis=1) / (seqs * seq * width))
    return (
        got["out"], got["gin"], got["gvf"], grad_w_query, grad_w_key, grad_w_value, got["dwo"],
        grad_w_gate, grad_w_up, grad_w_down, grad_gain_attn, grad_gain_ffn, statistics,
    )


SEMAPHORES = 192


def fits_units(mesh):
    return mesh.shape["ulysses"] == 4 and mesh.shape["blk"] == 8


def solution(mesh):
    in_specs = (
        P(None, ("blk", "ulysses"), None),
        P(None, ("blk", "ulysses"), None),
        P(None, ("blk", "ulysses"), None),
        P(None, ("blk", "ulysses")),
        P(),
        P(("ulysses", "blk"), None),
        P(("ulysses", "blk"), None),
        P(("ulysses", "blk"), None),
        P(("ulysses", "blk"), None),
        P(("ulysses", "blk"), None),
        P(("ulysses", "blk"), None),
        P(("ulysses", "blk"), None),
        P(("ulysses", "blk")),
        P(("ulysses", "blk")),
    )
    out_specs = (
        P(None, ("blk", "ulysses"), None),
        P(None, ("blk", "ulysses"), None),
        P(None, ("blk", "ulysses"), None),
        P(("ulysses", "blk"), None),
        P(("ulysses", "blk"), None),
        P(("ulysses", "blk"), None),
        P(("ulysses", "blk"), None),
        P(("ulysses", "blk"), None),
        P(("ulysses", "blk"), None),
        P(("ulysses", "blk"), None),
        P(("ulysses", "blk")),
        P(("ulysses", "blk")),
        P(),
    )
    path = local_units if fits_units(mesh) else local
    return jax.shard_map(path, mesh=mesh, in_specs=in_specs, out_specs=out_specs, check_vma=False)
```

```python
import functools
import types

import jax
import jax.numpy as jnp
import numpy as np
from jax import lax
from jax.experimental import pallas as pl
from jax.experimental.pallas import tpu as pltpu
from jax.sharding import PartitionSpec as P

HEADS = 16
HD = 64


epsilon = 1e-06
rope_base = 10000.0
neg_big = -1e30


def norm_rows(values, gain):
    factor = lax.rsqrt(jnp.mean(values * values, axis=-1, keepdims=True) + epsilon)
    hatted = values * factor
    return (hatted * gain, hatted, factor)


def norm_back(grad_normed, hatted, factor, gain):
    scaled = grad_normed * gain
    inner = jnp.mean(scaled * hatted, axis=-1, keepdims=True)
    return (factor * (scaled - hatted * inner), jnp.sum(grad_normed * hatted, axis=(0, 1)))


def rope_tables(positions):
    half_dim = HD // 2
    inverse = rope_base ** (-2.0 * jnp.arange(half_dim, dtype=jnp.float32) / HD)
    angles = positions.astype(jnp.float32)[:, :, None] * inverse
    return (jnp.cos(angles)[:, :, None, :], jnp.sin(angles)[:, :, None, :])


def rotate(values, cosine, sine, forward_turn):
    shaped = values.reshape(values.shape[0], values.shape[1], HEADS, HD)
    half_dim = HD // 2
    first = shaped[..., :half_dim]
    second = shaped[..., half_dim:]
    if forward_turn:
        turned = jnp.concatenate(
            [first * cosine - second * sine, second * cosine + first * sine], axis=-1
        )
    else:
        turned = jnp.concatenate(
            [first * cosine + second * sine, second * cosine - first * sine], axis=-1
        )
    return turned.reshape(values.shape)


def project(activations, weight):
    return jnp.einsum("std,de->ste", activations, weight, preferred_element_type=jnp.float32)


def project_back(gradient, weight):
    return jnp.einsum("ste,de->std", gradient, weight, preferred_element_type=jnp.float32)


def weight_grad(activations, gradient):
    return jnp.einsum("std,ste->de", activations, gradient, preferred_element_type=jnp.float32)


def allowed_mask(segments, query_first, query_count, key_first, key_count):
    seg_query = lax.dynamic_slice_in_dim(segments, query_first, query_count, 1)
    seg_key = lax.dynamic_slice_in_dim(segments, key_first, key_count, 1)
    query_place = query_first + jnp.arange(query_count, dtype=jnp.int32)
    key_place = key_first + jnp.arange(key_count, dtype=jnp.int32)
    causal = key_place[None, :] <= query_place[:, None]
    same_doc = seg_query[:, :, None] == seg_key[:, None, :]
    return (causal[None] & same_doc)[:, :, None, :]


def over_blocks(step_fn, running, pieces, block_rows):
    row_count = pieces[0].shape[1]
    block_count = row_count // block_rows
    stacked = tuple(
        (
            jnp.moveaxis(
                member.reshape((member.shape[0], block_count, block_rows) + member.shape[2:]), 1, 0
            )
            for member in pieces
        )
    )
    offsets = block_rows * jnp.arange(block_count, dtype=jnp.int32)

    def advance(current, scan_entry):
        return (step_fn(current, scan_entry[:-1], scan_entry[-1]), None)

    running, unused = lax.scan(advance, running, stacked + (offsets,))
    return running


def add_rows(buffer, update, first_row):
    current = lax.dynamic_slice_in_dim(buffer, first_row, update.shape[1], 1)
    return lax.dynamic_update_slice_in_dim(buffer, current + update, first_row, 1)


def unchanged(running):
    return running


def local(
    inputs,
    v_first,
    grad_out,
    positions,
    segments,
    w_query,
    w_key,
    w_value,
    w_out,
    w_gate,
    w_up,
    w_down,
    gain_attn,
    gain_ffn,
):
    gathered = (
        lax.all_gather(w_query, ("ulysses", "blk"), axis=0, tiled=True),
        lax.all_gather(w_key, ("ulysses", "blk"), axis=0, tiled=True),
        lax.all_gather(w_value, ("ulysses", "blk"), axis=0, tiled=True),
        lax.all_gather(w_out, ("ulysses", "blk"), axis=0, tiled=True),
        lax.all_gather(w_gate, ("ulysses", "blk"), axis=0, tiled=True),
        lax.all_gather(w_up, ("ulysses", "blk"), axis=0, tiled=True),
        lax.all_gather(w_down, ("ulysses", "blk"), axis=0, tiled=True),
        lax.all_gather(gain_attn, ("ulysses", "blk"), axis=0, tiled=True),
        lax.all_gather(gain_ffn, ("ulysses", "blk"), axis=0, tiled=True),
    )
    (
        full_query,
        full_key,
        full_value,
        full_out,
        full_gate,
        full_up,
        full_down,
        full_gain_attn,
        full_gain_ffn,
    ) = gathered
    score_scale = HD ** (-0.5)
    residual = inputs.astype(jnp.float32)
    normed_f, hatted_attn, factor_attn = norm_rows(residual, full_gain_attn.astype(jnp.float32))
    normed = normed_f.astype(jnp.bfloat16)
    cosine, sine = rope_tables(positions)
    query_tok = rotate(project(normed, full_query), cosine, sine, True).astype(jnp.bfloat16)
    key_tok = rotate(project(normed, full_key), cosine, sine, True).astype(jnp.bfloat16)
    value_tok = (0.5 * project(normed, full_value) + 0.5 * v_first.astype(jnp.float32)).astype(
        jnp.bfloat16
    )
    query_head, key_head, value_head = (
        lax.all_to_all(query_tok, "ulysses", split_axis=2, concat_axis=1, tiled=True),
        lax.all_to_all(key_tok, "ulysses", split_axis=2, concat_axis=1, tiled=True),
        lax.all_to_all(value_tok, "ulysses", split_axis=2, concat_axis=1, tiled=True),
    )
    seq_count, block_rows, width = query_head.shape
    heads_local = width // HD
    query_start = lax.axis_index("blk") * block_rows
    full_rows = block_rows * lax.axis_size("blk")

    def split_heads(values):
        return values.reshape(values.shape[0], values.shape[1], heads_local, HD)

    query_four = split_heads(query_head)

    def attend_rows(running, pieces, first_row):
        key_rows, value_rows = pieces
        key_count = key_rows.shape[1]

        def attend_compute(current):
            best, total, accum = current
            allowed = allowed_mask(segments, query_start, block_rows, first_row, key_count)
            scores = (
                jnp.einsum(
                    "sqhd,skhd->sqhk",
                    query_four,
                    split_heads(key_rows),
                    preferred_element_type=jnp.float32,
                )
                * score_scale
            )
            masked = jnp.where(allowed, scores, neg_big)
            new_best = jnp.maximum(best, jnp.max(masked, axis=-1))
            weights = jnp.where(allowed, jnp.exp(masked - new_best[..., None]), 0.0)
            rescale = jnp.exp(best - new_best)
            total = total * rescale + jnp.sum(weights, axis=-1)
            accum = accum * rescale[..., None] + jnp.einsum(
                "sqhk,skhd->sqhd",
                weights.astype(jnp.bfloat16),
                split_heads(value_rows),
                preferred_element_type=jnp.float32,
            )
            return (new_best, total, accum)

        return lax.cond(
            first_row <= query_start + block_rows - 1, attend_compute, unchanged, running
        )

    stat_zeros = jnp.zeros((seq_count, block_rows, heads_local), jnp.float32)
    head_zeros = jnp.zeros((seq_count, block_rows, heads_local, HD), jnp.float32)
    initial = (
        jnp.full((seq_count, block_rows, heads_local), neg_big, jnp.float32),
        stat_zeros,
        head_zeros,
    )
    best, total, accum = over_blocks(
        attend_rows,
        initial,
        (
            lax.all_gather(key_head, "blk", axis=1, tiled=True),
            lax.all_gather(value_head, "blk", axis=1, tiled=True),
        ),
        block_rows,
    )
    log_total = best + jnp.log(total)
    attn_heads = accum / total[..., None]
    attn_low = attn_heads.reshape(seq_count, block_rows, width).astype(jnp.bfloat16)
    mixed = lax.all_to_all(attn_low, "ulysses", split_axis=1, concat_axis=2, tiled=True)
    attn_branch = project(mixed, full_out)
    hidden = residual + attn_branch
    normed_ffn_f, hatted_ffn, factor_ffn = norm_rows(hidden, full_gain_ffn.astype(jnp.float32))
    normed_ffn = normed_ffn_f.astype(jnp.bfloat16)
    gate = project(normed_ffn, full_gate)
    up_proj = project(normed_ffn, full_up)
    sigmoid_gate = jax.nn.sigmoid(gate)
    silu_gate = gate * sigmoid_gate
    act = (silu_gate * up_proj).astype(jnp.bfloat16)
    ffn_branch = project(act, full_down)
    output_f = hidden + ffn_branch
    output = output_f.astype(jnp.bfloat16)
    squares = lax.psum(
        (
            jnp.sum(residual * residual),
            jnp.sum(attn_branch * attn_branch),
            jnp.sum(output_f * output_f),
        ),
        ("ulysses", "blk"),
    )
    entry_count = residual.size * lax.axis_size("ulysses") * lax.axis_size("blk")
    statistics = jnp.sqrt(jnp.stack(squares) / entry_count)
    again = (
        lax.all_gather(w_query, ("ulysses", "blk"), axis=0, tiled=True),
        lax.all_gather(w_key, ("ulysses", "blk"), axis=0, tiled=True),
        lax.all_gather(w_value, ("ulysses", "blk"), axis=0, tiled=True),
        lax.all_gather(w_out, ("ulysses", "blk"), axis=0, tiled=True),
        lax.all_gather(w_gate, ("ulysses", "blk"), axis=0, tiled=True),
        lax.all_gather(w_up, ("ulysses", "blk"), axis=0, tiled=True),
        lax.all_gather(w_down, ("ulysses", "blk"), axis=0, tiled=True),
        lax.all_gather(gain_attn, ("ulysses", "blk"), axis=0, tiled=True),
        lax.all_gather(gain_ffn, ("ulysses", "blk"), axis=0, tiled=True),
    )
    (
        back_query,
        back_key,
        back_value,
        back_out,
        back_gate,
        back_up,
        back_down,
        back_gain_attn,
        back_gain_ffn,
    ) = again
    grad_act = project_back(grad_out, back_down)
    grad_gate = (grad_act * up_proj * sigmoid_gate * (1.0 + gate * (1.0 - sigmoid_gate))).astype(
        jnp.bfloat16
    )
    grad_up = (grad_act * silu_gate).astype(jnp.bfloat16)
    grad_normed_ffn = project_back(grad_gate, back_gate) + project_back(grad_up, back_up)
    grad_ffn_norm, grad_gain_ffn = norm_back(
        grad_normed_ffn, hatted_ffn, factor_ffn, back_gain_ffn.astype(jnp.float32)
    )
    grad_hidden = grad_out.astype(jnp.float32) + grad_ffn_norm
    grad_branch = grad_hidden.astype(jnp.bfloat16)
    grad_mixed = project_back(grad_branch, back_out).astype(jnp.bfloat16)
    dout_head = lax.all_to_all(grad_mixed, "ulysses", split_axis=2, concat_axis=1, tiled=True)
    dout_four = split_heads(dout_head)
    row_dot = jnp.sum(dout_four.astype(jnp.float32) * attn_heads, axis=-1)

    def grad_rows(running, pieces, first_row):
        key_rows, value_rows = pieces
        key_count = key_rows.shape[1]

        def grad_compute(current):
            grad_query, grad_keys, grad_values = current
            key_part = split_heads(key_rows)
            allowed = allowed_mask(segments, query_start, block_rows, first_row, key_count)
            scores = (
                jnp.einsum(
                    "sqhd,skhd->sqhk", query_four, key_part, preferred_element_type=jnp.float32
                )
                * score_scale
            )
            probs = jnp.where(allowed, jnp.exp(scores - log_total[..., None]), 0.0)
            prob_grad = jnp.einsum(
                "sqhd,skhd->sqhk",
                dout_four,
                split_heads(value_rows),
                preferred_element_type=jnp.float32,
            )
            score_grad = (probs * (prob_grad - row_dot[..., None])).astype(jnp.bfloat16)
            grad_query = (
                grad_query
                + jnp.einsum(
                    "sqhk,skhd->sqhd", score_grad, key_part, preferred_element_type=jnp.float32
                )
                * score_scale
            )
            key_term = (
                jnp.einsum(
                    "sqhk,sqhd->skhd", score_grad, query_four, preferred_element_type=jnp.float32
                )
                * score_scale
            )
            value_term = jnp.einsum(
                "sqhk,sqhd->skhd",
                probs.astype(jnp.bfloat16),
                dout_four,
                preferred_element_type=jnp.float32,
            )
            return (
                grad_query,
                add_rows(grad_keys, key_term, first_row),
                add_rows(grad_values, value_term, first_row),
            )

        return lax.cond(first_row <= query_start + block_rows - 1, grad_compute, unchanged, running)

    full_zeros = jnp.zeros((seq_count, full_rows, heads_local, HD), jnp.float32)
    grad_query_own, grad_keys_all, grad_values_all = over_blocks(
        grad_rows,
        (head_zeros, full_zeros, full_zeros),
        (
            lax.all_gather(key_head, "blk", axis=1, tiled=True),
            lax.all_gather(value_head, "blk", axis=1, tiled=True),
        ),
        block_rows,
    )
    grad_key_own, grad_value_own = (
        lax.psum_scatter(
            grad_keys_all.reshape(seq_count, full_rows, width).astype(jnp.bfloat16),
            "blk",
            scatter_dimension=1,
            tiled=True,
        ).astype(jnp.float32),
        lax.psum_scatter(
            grad_values_all.reshape(seq_count, full_rows, width).astype(jnp.bfloat16),
            "blk",
            scatter_dimension=1,
            tiled=True,
        ).astype(jnp.float32),
    )
    grad_query_own = grad_query_own.reshape(seq_count, block_rows, width)
    grad_query_tok, grad_key_tok, grad_value_tok = (
        lax.all_to_all(
            grad_query_own.astype(jnp.bfloat16), "ulysses", split_axis=1, concat_axis=2, tiled=True
        ),
        lax.all_to_all(
            grad_key_own.astype(jnp.bfloat16), "ulysses", split_axis=1, concat_axis=2, tiled=True
        ),
        lax.all_to_all(
            grad_value_own.astype(jnp.bfloat16), "ulysses", split_axis=1, concat_axis=2, tiled=True
        ),
    )
    grad_query_raw = rotate(grad_query_tok.astype(jnp.float32), cosine, sine, False).astype(
        jnp.bfloat16
    )
    grad_key_raw = rotate(grad_key_tok.astype(jnp.float32), cosine, sine, False).astype(
        jnp.bfloat16
    )
    grad_v_first = grad_value_tok * 0.5
    grad_normed = (
        project_back(grad_query_raw, back_query)
        + project_back(grad_key_raw, back_key)
        + project_back(grad_v_first, back_value)
    )
    grad_attn_norm, grad_gain_attn = norm_back(
        grad_normed, hatted_attn, factor_attn, back_gain_attn.astype(jnp.float32)
    )
    grad_inputs = (grad_hidden + grad_attn_norm).astype(jnp.bfloat16)
    model_width = w_query.shape[1]
    hidden_width = w_gate.shape[1]
    owned = lax.psum_scatter(
        jnp.concatenate(
            [
                weight_grad(normed, grad_query_raw),
                weight_grad(normed, grad_key_raw),
                weight_grad(normed, grad_v_first),
                weight_grad(mixed, grad_branch),
                weight_grad(normed_ffn, grad_gate),
                weight_grad(normed_ffn, grad_up),
                grad_gain_attn[:, None],
                grad_gain_ffn[:, None],
            ],
            axis=1,
        ),
        ("ulysses", "blk"),
        scatter_dimension=0,
        tiled=True,
    )
    grad_w_down = lax.psum_scatter(
        weight_grad(act, grad_out), ("ulysses", "blk"), scatter_dimension=0, tiled=True
    )
    column = 0
    pieces = []
    for span in (model_width, model_width, model_width, model_width, hidden_width, hidden_width):
        pieces.append(owned[:, column : column + span])
        column = column + span
    grad_gain_attn_own = owned[:, column]
    grad_gain_ffn_own = owned[:, column + 1]
    return (
        output,
        grad_inputs,
        grad_v_first,
        pieces[0],
        pieces[1],
        pieces[2],
        pieces[3],
        pieces[4],
        pieces[5],
        grad_w_down,
        grad_gain_attn_own,
        grad_gain_ffn_own,
        statistics,
    )


MESH = pl.DeviceIdType.MESH
LANES = 128
VMEM_BYTES = 61 << 20
f32 = jnp.float32
bf16 = jnp.bfloat16
QB, KB = 512, 256


class Copy:
    def __init__(self, copy, send_at, recv_at, when):
        self.copy, self.at, self.recv_at, self.when = copy, send_at, recv_at, when

    def wait_recv(self):
        self.copy.wait_recv()

    def wait_send(self):
        if self.when is None:
            self.copy.wait_send()
        else:
            pl.when(self.when)(self.copy.wait_send)


class Net:
    def __init__(self, send_sems, recv_sems):
        self.send_sems, self.recv_sems = send_sems, recv_sems
        self.count, self.open = 0, []

    def push(self, src, dst, u, b, when=None, recv_at=None, at=None):
        if at is None:
            at = self.count
            self.count += 1
        recv_at = at if recv_at is None else recv_at
        copy = pltpu.make_async_remote_copy(
            src_ref=src,
            dst_ref=dst,
            send_sem=self.send_sems.at[at],
            recv_sem=self.recv_sems.at[recv_at],
            device_id=(u, b),
            device_id_type=MESH,
        )
        if when is None:
            copy.start()
        else:
            pl.when(when)(copy.start)
        made = Copy(copy, at, recv_at, when)
        self.open.append(made)
        return made

    def sent(self, copies):
        for copy in copies:
            copy.wait_send()
        self.open = [copy for copy in self.open if copy not in copies]

    def drain(self):
        for copy in self.open:
            copy.wait_send()
        self.open = []


def arrive(copies):
    for copy in copies:
        copy.wait_recv()


def here():
    return lax.axis_index("ulysses"), lax.axis_index("blk")


def greet(u, b, n_u, n_b):
    barrier = pltpu.get_barrier_semaphore()
    for off in range(1, n_u):
        pl.semaphore_signal(barrier, inc=1, device_id=(u ^ off, b), device_id_type=MESH)
    for off in range(1, n_b):
        pl.semaphore_signal(barrier, inc=1, device_id=(u, b ^ off), device_id_type=MESH)
    pl.semaphore_wait(barrier, n_u - 1 + n_b - 1)


def dot(left, right):
    return jnp.dot(left, right, preferred_element_type=f32)


def dot_nt(left, right):
    return lax.dot_general(left, right, (((1,), (1,)), ((), ())), preferred_element_type=f32)


def dot_tn(left, right):
    return lax.dot_general(left, right, (((0,), (0,)), ((), ())), preferred_element_type=f32)


def at_block(index, size):
    return pl.ds(pl.multiple_of(index * size, size), size)


def lane_of(shape):
    return lax.broadcasted_iota(jnp.int32, shape, len(shape) - 1)


def swap_halves(tile):
    return pltpu.roll(tile, HD, tile.ndim - 1)


def partner(tile):
    low = lane_of(tile.shape) % HD < HD // 2
    return jnp.where(low, pltpu.roll(tile, LANES - HD // 2, 1), pltpu.roll(tile, HD // 2, 1))


def pack_rows(rows):
    half = rows.shape[0] // 2
    low = lane_of((half, LANES)) < HD
    return jnp.where(low, rows[:half], swap_halves(rows[half:]))


def unpack_rows(packed):
    return jnp.concatenate([packed, swap_halves(packed)], axis=0)


class Exchange:
    def __init__(self, net, staged, landed, u, b, n_b):
        self.net, self.staged, self.landed, self.u, self.b, self.n_b = net, staged, landed, u, b, n_b
        self.at = net.count
        net.count += n_b

    def copy(self, to, slot_from):
        return pltpu.make_async_remote_copy(
            src_ref=self.staged.at[to],
            dst_ref=self.landed.at[slot_from],
            send_sem=self.net.send_sems.at[self.at + to],
            recv_sem=self.net.recv_sems.at[self.at + slot_from],
            device_id=(self.u, to),
            device_id_type=MESH,
        )

    def give(self, to):
        @pl.when(to != self.b)
        def _():
            self.copy(to, self.b).start()

    def take(self):
        for off in range(1, self.n_b):
            self.copy(self.b ^ off, self.b ^ off).wait_recv()

    def sent(self):
        for off in range(1, self.n_b):
            self.copy(self.b ^ off, self.b).wait_send()


class Gather:
    def __init__(self, net, slot, u, b):
        self.net, self.slot, self.u, self.b = net, slot, u, b
        self.inner = ((b // 2) == 1) | ((b // 2) == 2)
        mine = slot(b)
        self.two = net.push(mine, mine, u, b ^ 4)
        self.one = net.push(mine, mine, u, b ^ 2)
        self.three = net.push(mine, mine, u, b ^ 6, when=self.inner)
        self.side = [net.push(mine, mine, u, b ^ 1)]

    def beside(self, owner):
        got = self.slot(owner)
        self.side.append(self.net.push(got, got, self.u, self.b ^ 1))

    def forward(self):
        self.two.wait_recv()
        got = self.slot(self.b ^ 4)
        self.net.push(got, got, self.u, self.b ^ 2, when=self.inner, recv_at=self.three.at)
        self.beside(self.b ^ 4)

    def relay(self):
        self.one.wait_recv()
        self.beside(self.b ^ 2)
        self.three.wait_recv()
        self.beside(self.b ^ 6)

    def finish(self):
        arrive(self.side)


class Scatter:
    def __init__(self, net, u, b, mine, paired, summed, landed):
        self.net, self.u, self.b = net, u, b
        self.mine, self.paired, self.summed, self.landed = mine, paired, summed, landed
        self.z = b // 2
        self.inner = (self.z == 1) | (self.z == 2)
        self.swap = [net.push(mine(z, 1 - b % 2), paired.at[z], u, b ^ 1) for z in range(4)]

    def add(self, z):
        self.summed[z] = (self.mine(z, self.b % 2)[...].astype(f32) + self.paired[z].astype(f32)).astype(bf16)

    def middle(self):
        net, u, b, z, inner = self.net, self.u, self.b, self.z, self.inner
        outer = jnp.logical_not(inner)
        arrive(self.swap)
        self.add(z ^ 3)
        far = self.summed.at[z ^ 3]
        self.extra = net.push(far, self.landed.at[3], u, b ^ 2, when=outer)
        self.three = net.push(far, self.landed.at[2], u, b ^ 6, when=inner)
        self.add(z ^ 2)
        self.two = net.push(self.summed.at[z ^ 2], self.landed.at[1], u, b ^ 4, when=outer)
        self.add(z ^ 1)
        self.one = net.push(self.summed.at[z ^ 1], self.landed.at[0], u, b ^ 2)
        self.add(z)

    def merge(self):
        net, u, b, z = self.net, self.u, self.b, self.z

        @pl.when(self.inner)
        def _():
            self.extra.wait_recv()
            self.summed[z ^ 2] = (self.summed[z ^ 2].astype(f32) + self.landed[3].astype(f32)).astype(bf16)

        net.push(self.summed.at[z ^ 2], self.landed.at[1], u, b ^ 4, when=self.inner, at=self.two.at)

    def finish(self, total):
        self.one.wait_recv()
        self.two.wait_recv()
        total[...] = (
            self.summed[self.z].astype(f32) + self.landed[0].astype(f32) + self.landed[1].astype(f32)
        ).astype(total.dtype)

        @pl.when(self.inner)
        def _():
            self.three.wait_recv()
            total[...] = (total[...].astype(f32) + self.landed[2].astype(f32)).astype(total.dtype)


def fill_units(units, tb, store):
    def one(block, carry):
        low = lane_of((tb, LANES)) < HD
        tile = units[block, 0:tb].astype(f32)
        query = jnp.where(low, tile * HD ** (-0.5), 0.0)
        key = jnp.where(low, swap_halves(tile), 0.0)
        value = jnp.where(low, unpack_rows(units[block, tb:].astype(f32)), 0.0)
        store(block, query, key, value)
        return carry

    lax.fori_loop(0, units.shape[0], one, 0)


def allowed_block(first_key, first_query, low_row, keys=KB, queries=QB):
    key_place = first_key + lax.broadcasted_iota(jnp.int32, (keys, queries), 0)
    query_place = first_query + lax.broadcasted_iota(jnp.int32, (keys, queries), 1)
    return (key_place <= query_place) & (key_place >= low_row)


def widen(rows, size, padded):
    zeros = jnp.zeros((rows.shape[0], padded - size), rows.dtype)
    pieces = []
    for at in range(0, rows.shape[1], size):
        pieces += [rows[:, at : at + size], zeros]
    return jnp.concatenate(pieces, axis=1)


def rope_rows(base, cut, count):
    place = base + lax.broadcasted_iota(jnp.int32, (count, LANES), 0)
    place = place.astype(f32)
    local_place = jnp.where(place >= cut, place - cut, place)
    pair = lane_of((count, LANES)) % (HD // 2)
    inverse = jnp.zeros((1, LANES), f32)
    for i in range(HD // 2):
        inverse = jnp.where(pair[0:1] == i, float(np.float32(rope_base ** (-2.0 * i / HD))), inverse)
    angles = local_place * inverse
    sign = jnp.where(lane_of((count, LANES)) % HD < HD // 2, -1.0, 1.0)
    return jnp.cos(angles), sign * jnp.sin(angles)


def layer_kernel(dims, names, *refs):
    n_u, n_b, seqs, td, rows, heads = dims
    r = types.SimpleNamespace(**dict(zip(names, refs)))
    tb = n_u * td
    tokens = seqs * tb
    seq = n_b * tb
    n_z = n_b // 2
    width = r.x.shape[2]
    u, b = here()
    net = Net(r.send_sems, r.recv_sems)
    others = [u ^ off for off in range(1, n_u)]
    slab = at_block(u, td)
    mine = at_block(b, rows)
    ff = r.wdg.shape[0]
    ff_rows = ff // n_b

    def part(v):
        return at_block(v, td)

    share = heads * HD
    thirds = (r.wq_in, r.wk_in, r.wv_in)
    r.gains[...] = jnp.zeros_like(r.gains)
    for row, gain in enumerate((r.ga, r.gf)):
        r.gains[row : row + 1, 0:rows] = gain[...].astype(f32).reshape(1, rows)
    lane_place = (b % (LANES // rows)) * rows
    r.gains[...] = pltpu.roll(r.gains[...], lane_place, 1)
    greet(u, b, n_u, n_b)
    got_w = [
        net.push(w.at[:, at_block(v, share)], r.wq.at[u, mine, pl.ds(i * share, share)], v, b)
        for i, w in enumerate(thirds)
        for v in others
    ]
    got_g = [net.push(r.gains, r.gbuf.at[b, u], v, b) for v in others]
    r.wo[mine] = r.wout[...]
    g_out = Gather(net, lambda c: r.wo.at[at_block(c, rows)], u, b)
    got_x = [net.push(r.x, r.xg.at[:, slab], v, b) for v in others]
    for i, w in enumerate(thirds):
        r.wq[u, mine, i * share : (i + 1) * share] = w[:, at_block(u, share)]
    r.gbuf[b, u] = r.gains[...]
    r.xg[:, slab] = r.x[...]
    r.vfg[:, slab] = r.vf[:, :, at_block(u, share)]
    r.gog[:, slab] = r.go[...]
    arrive(got_w)
    g_qk = Gather(net, lambda c: r.wq.at[:, at_block(c, rows), pl.ds(0, 2 * share)], u, b)
    g_v = Gather(net, lambda c: r.wq.at[:, at_block(c, rows), pl.ds(2 * share, share)], u, b)
    arrive(got_g)
    got_g = [net.push(r.gbuf.at[b], r.gbuf.at[b], u, b ^ off) for off in range(1, n_b)]
    got_v = [net.push(r.vf.at[:, :, at_block(v, share)], r.vfg.at[:, slab], v, b) for v in others]
    ff_own = r.wd.shape[0]
    for i, w in enumerate((r.wg_in, r.wu_in)):
        wide_rows = widen(w[...], ff_own, ff_rows)
        for v in range(n_u):
            r.wgu[v, :, i * ff : (i + 1) * ff] = wide_rows[:, v * ff : (v + 1) * ff]
    r.wg[u, mine] = r.wgu[u]
    got_o = [net.push(r.wgu.at[v], r.wg.at[u, mine], v, b) for v in others]
    arrive(got_g)
    per_tile = LANES // rows
    for tile in range(n_u * n_b // per_tile):
        total = None
        for index in range(tile * per_tile, (tile + 1) * per_tile):
            term = r.gbuf[index % n_b, index // n_b]
            total = term if total is None else total + term
        r.gain[:, tile * LANES : (tile + 1) * LANES] = total
    seq_of_unit = b // heads
    for s in range(seqs):
        cut = jnp.sum((1 - r.segments[s : s + 1, :]).astype(f32), axis=1, keepdims=True)
        r.cosr[s], r.sinr[s] = rope_rows(b * tb, cut, tb)

        @pl.when(seq_of_unit == s)
        def _():
            key_place = lane_of((8, seq)).astype(f32)
            r.low[...] = jnp.where(key_place >= cut, cut, 0.0).astype(jnp.int32)

    arrive(got_x)

    def norm(step, carry):
        s, place = step // 2, at_block(step % 2, tb // 2)
        values = r.xg[s, place].astype(f32)
        factor = lax.rsqrt(jnp.mean(values * values, axis=-1, keepdims=True) + epsilon)
        hat = values * factor
        r.hat[s, place] = hat.astype(bf16)
        r.normed[s, place] = (hat * r.gain[0:1, :]).astype(bf16)
        return carry

    lax.fori_loop(0, 2 * seqs, norm, 0)
    got_go = [net.push(r.go, r.gog.at[:, slab], v, b) for v in others]
    g_qk.forward()
    g_qk.relay()
    g_v.forward()
    g_qk.finish()

    x_qk = Exchange(net, r.stage.at[:, pl.ds(0, tb)], r.units.at[:, pl.ds(0, tb)], u, b, n_b)
    x_v = Exchange(net, r.stage.at[:, pl.ds(tb, tb // 2)], r.units.at[:, pl.ds(tb, tb // 2)], u, b, n_b)
    for s in range(seqs):
        left = r.normed[s]
        for n in range(heads // 4):
            spans = [slice(i * share + n * 256, i * share + (n + 1) * 256) for i in range(2)]
            pair_of = [dot(left, r.wq[:, :, span].reshape(width, 256)) for span in spans]
            for i in range(2):
                lanes = slice(i * LANES, (i + 1) * LANES)
                query, key = [f[:, lanes] * r.cosr[s] + partner(f[:, lanes]) * r.sinr[s] for f in pair_of]
                low_lane = lane_of(query.shape) < HD
                unit = s * heads + 4 * n + 2 * i
                r.stage[unit, 0:tb] = jnp.where(low_lane, query, swap_halves(key)).astype(bf16)
                r.stage[unit + 1, 0:tb] = jnp.where(low_lane, swap_halves(query), key).astype(bf16)
        for unit in range(s * heads, (s + 1) * heads):
            x_qk.give(unit)
    arrive(got_v)
    g_v.relay()
    g_v.finish()
    for s in range(seqs):
        left = r.normed[s]
        for n in range(heads // 4):
            first_lane = 2 * share + n * 256
            found = dot(left, r.wq[:, :, first_lane : first_lane + 256].reshape(width, 256))
            for i in range(2):
                first = r.vfg[s, :, n * 256 + i * LANES : n * 256 + (i + 1) * LANES].astype(f32)
                value = 0.5 * found[:, i * LANES : (i + 1) * LANES] + 0.5 * first
                unit = s * heads + 4 * n + 2 * i
                r.stage[unit, tb:] = pack_rows(value).astype(bf16)
                r.stage[unit + 1, tb:] = pack_rows(swap_halves(value)).astype(bf16)
        for unit in range(s * heads, (s + 1) * heads):
            x_v.give(unit)
    r.units[b] = r.stage[b]
    for slot in range(n_b):
        r.wdg[slot * ff_rows + ff_own : (slot + 1) * ff_rows] = jnp.zeros((ff_rows - ff_own, width), bf16)
    r.wdg[pl.ds(pl.multiple_of(b * ff_rows, ff_rows), ff_own)] = r.wd[...]
    g_out.forward()
    g_out.relay()
    x_qk.take()
    x_v.take()
    g_out.finish()

    g_down = Gather(net, lambda c: r.wdg.at[pl.ds(pl.multiple_of(c * ff_rows, ff_rows), ff_own)], u, b)
    x_out = Exchange(net, r.ostage, r.parts, u, b, n_b)

    def store(block, query, key, value):
        place = at_block(block, tb)
        r.keys[place] = key.astype(bf16)
        r.key_t[:, place] = jnp.transpose(key)[:HD].astype(bf16)
        r.query[place] = query.astype(bf16)
        r.query_t[:, place] = jnp.transpose(query).astype(bf16)
        r.value[place] = value.astype(bf16)
        r.value_t[:, place] = jnp.transpose(value)[:HD].astype(bf16)

    fill_units(r.units, tb, store)

    def attend(step, carry):
        qb = seq // QB - 1 - step
        q_at = at_block(qb, QB)
        query = r.query_t[:, q_at]
        low_row = r.low[0:1, q_at]
        r.acc[...] = jnp.zeros_like(r.acc)

        def inner(kb, state):
            best, total = state
            k_at = at_block(kb, KB)
            scores = dot(r.keys[k_at], query)
            scores = jnp.where(allowed_block(kb * KB, qb * QB, low_row), scores, neg_big)
            new_best = jnp.maximum(best, jnp.max(scores, axis=0, keepdims=True))
            weights = jnp.exp(scores - new_best)
            rescale = jnp.exp(best - new_best)
            total = total * rescale + jnp.sum(weights, axis=0, keepdims=True)
            r.acc[...] = r.acc[...] * rescale + dot(r.value_t[:, k_at], weights.astype(bf16))
            return new_best, total

        start = (jnp.full((1, QB), neg_big, f32), jnp.zeros((1, QB), f32))
        best, total = lax.fori_loop(0, (qb + 1) * (QB // KB), inner, start)
        out = r.acc[...] / total
        r.heads_t[:, q_at] = out
        r.lse[:, q_at] = jnp.broadcast_to(best + jnp.log(total), (8, QB))
        turned = jnp.transpose(jnp.concatenate([out, jnp.zeros_like(out)], axis=0))
        for i in range(QB // tb):
            to = qb * (QB // tb) + i
            r.ostage[to] = pack_rows(turned[i * tb : (i + 1) * tb]).astype(bf16)
            x_out.give(to)
        return carry

    lax.fori_loop(0, seq // QB, attend, 0)
    r.parts[b] = r.ostage[b]
    g_down.forward()
    arrive(got_o)
    x_out.take()
    g_gate = Gather(net, lambda c: r.wg.at[:, at_block(c, rows)], u, b)

    half = tb // 2
    got_s = []
    for s in range(seqs):
        for pair in range(heads // 2):
            one = r.parts[s * heads + 2 * pair].astype(f32)
            two = r.parts[s * heads + 2 * pair + 1].astype(f32)
            low_lane = lane_of(one.shape) < HD
            lanes = slice(pair * LANES, (pair + 1) * LANES)
            r.mix[s, :half, lanes] = jnp.where(low_lane, one, swap_halves(two)).astype(bf16)
            r.mix[s, half:, lanes] = jnp.where(low_lane, swap_halves(one), two).astype(bf16)
        r.branch[s] = dot(r.mix[s], r.wo[...]).astype(bf16)
        got_s.append([net.push(r.branch.at[s, part(v)], r.landed.at[u, s], v, b) for v in others])
        r.landed[u, s] = r.branch[s, slab]
    g_down.relay()
    r.sums[...] = jnp.zeros_like(r.sums)
    got_n = []
    for s in range(seqs):
        arrive(got_s[s])
        total = sum(r.landed[v, s].astype(f32) for v in range(n_u))
        own = r.x[s].astype(f32)
        hid = own + total
        r.hidden[s] = hid
        factor = lax.rsqrt(jnp.mean(hid * hid, axis=-1, keepdims=True) + epsilon)
        r.nf_own[s] = (hid * factor * r.gain[1:2, :]).astype(bf16)
        got_n.append([net.push(r.nf_own.at[s], r.nf.at[s, slab], v, b) for v in others])
        r.nf[s, slab] = r.nf_own[s]
        r.sums[0:1] = r.sums[0:1] + jnp.sum(own * own, axis=0, keepdims=True)
        r.sums[1:2] = r.sums[1:2] + jnp.sum(total * total, axis=0, keepdims=True)
    arrive(got_go)
    g_down.finish()
    g_gate.forward()
    g_gate.relay()
    g_gate.finish()

    def hidden_units(s):
        left = r.nf[s]
        grad = r.gog[s]

        def some(n, carry):
            span, up_span = at_block(n, 256), at_block(n + ff // 256, 256)
            gate = dot(left, r.wg[:, :, span].reshape(width, 256))
            up = dot(left, r.wg[:, :, up_span].reshape(width, 256))
            grad_act = dot_nt(grad, r.wdg[span])
            sig = 1.0 / (1.0 + jnp.exp(-gate))
            silu = gate * sig
            r.act[s, :, span] = (silu * up).astype(bf16)
            r.dgu[s, :, span] = (grad_act * up * sig * (1.0 + gate * (1.0 - sig))).astype(bf16)
            r.dgu[s, :, up_span] = (grad_act * silu).astype(bf16)
            return carry

        lax.fori_loop(0, ff // 256, some, 0)

    got_d = []
    for s in range(seqs):
        arrive(got_n[s])
        hidden_units(s)
        left = r.dgu[s]
        for v in range(n_u):
            r.d_low[s, :, v * 256 : (v + 1) * 256] = dot_nt(left, r.wg[v]).astype(bf16)
        got_d.append([net.push(r.d_low.at[s, part(v)], r.landed.at[u, s], v, b) for v in others])
        r.landed[u, s] = r.d_low[s, slab]

    def grad_down(n):
        half_units = ff // 2
        span = slice(n * half_units, (n + 1) * half_units)
        found = dot_tn(r.act[:, :, span].reshape(tokens, half_units), r.gog[...].reshape(tokens, width))
        r.wd_buf[n * (n_z // 2) : (n + 1) * (n_z // 2)] = found.astype(bf16).reshape(
            n_z // 2, 2, ff_rows, width
        )

    def grad_gate(v):
        left = r.nf[:, :, v * 256 : (v + 1) * 256].reshape(tokens, 256)
        found = dot_tn(left, r.dgu[...].reshape(tokens, 2 * ff))
        r.wg_buf[:, :, v] = found.astype(bf16).reshape(n_z, 2, rows, 2 * ff)

    got_b = []

    def norm_back(s):
        arrive(got_d[s])
        grad_normed = sum(r.landed[v, s].astype(f32) for v in range(n_u))
        hid = r.hidden[s]
        factor = lax.rsqrt(jnp.mean(hid * hid, axis=-1, keepdims=True) + epsilon)
        hat = hid * factor
        scaled = grad_normed * r.gain[1:2, :]
        inner = jnp.mean(scaled * hat, axis=-1, keepdims=True)
        total = r.go[s].astype(f32) + factor * (scaled - hat * inner)
        r.ghid[s] = total
        r.gb_own[s] = total.astype(bf16)
        got_b.append([net.push(r.gb_own.at[s], r.xg.at[s, slab], v, b) for v in others])
        r.xg[s, slab] = r.gb_own[s]
        r.sums[4:5] = r.sums[4:5] + jnp.sum(grad_normed * hat, axis=0, keepdims=True)

    for n in range(2):
        grad_down(n)
    ff_cut = pl.ds(0, ff_own)
    s_down = Scatter(
        net, u, b, lambda z, c: r.wd_buf.at[z, c, ff_cut], r.wd_pair.at[:, ff_cut],
        r.wd_sum.at[:, ff_cut], r.wd_land.at[:, ff_cut],
    )
    norm_back(0)
    grad_gate(0)
    s_down.middle()
    norm_back(1)
    for v in range(1, n_u):
        grad_gate(v)
    s_down.merge()
    s_gate = Scatter(net, u, b, lambda z, c: r.wg_buf.at[z, c], r.wg_pair, r.wg_sum, r.wg_land)
    x_grad = Exchange(net, r.ostage2, r.grads, u, b, n_b)
    for s in range(seqs):
        arrive(got_b[s])
        for pair in range(heads // 2):
            found = dot_nt(r.xg[s], r.wo[pair * LANES : (pair + 1) * LANES])
            unit = s * heads + 2 * pair
            r.ostage2[unit] = pack_rows(found).astype(bf16)
            r.ostage2[unit + 1] = pack_rows(swap_halves(found)).astype(bf16)
            x_grad.give(unit)
            x_grad.give(unit + 1)
    r.grads[b] = r.ostage2[b]

    def forward(s, carry):
        r.f_low[s] = dot(r.act[s], r.wdg[...]).astype(bf16)
        return carry

    lax.fori_loop(0, seqs, forward, 0)
    got_f = [net.push(r.f_low.at[:, part(v)], r.landed_f.at[u], v, b) for v in others]
    r.landed_f[u] = r.f_low[:, slab]
    found = dot_tn(r.mix[...].reshape(tokens, share), r.xg[...].reshape(tokens, width))
    r.wo_buf[...] = found.astype(bf16).reshape(n_z, 2, rows, width)
    s_out = Scatter(net, u, b, lambda z, c: r.wo_buf.at[z, c], r.wo_pair, r.wo_sum, r.wo_land)
    x_grad.take()
    s_gate.middle()

    def more(block, carry):
        place = at_block(block, tb)
        g = unpack_rows(r.grads[block].astype(f32))
        g = jnp.where(lane_of(g.shape) < HD, g, 0.0)
        r.grad[place] = g.astype(bf16)
        turned = jnp.transpose(g)
        r.grad_t[:, place] = turned.astype(bf16)
        total = jnp.sum(turned[:HD] * r.heads_t[:, place], axis=0, keepdims=True)
        r.row_dot[:, place] = jnp.broadcast_to(total, (8, tb))
        return carry

    lax.fori_loop(0, n_b, more, 0)
    x_qk.sent()
    x_v.sent()
    x_back = Exchange(net, r.stage, r.returned, u, b, n_b)

    def backward(keys_at, first_key, queries_at, first_query):
        seen = allowed_block(first_key, first_query, r.low[0:1, queries_at], keys_at.size, queries_at.size)
        scores = dot(r.keys[keys_at], r.query_t[:, queries_at])
        probs = jnp.where(seen, jnp.exp(scores - r.lse[0:1, queries_at]), 0.0)
        prob_grad = dot(r.value[keys_at], r.grad_t[:, queries_at])
        score_grad = (probs * (prob_grad - r.row_dot[0:1, queries_at])).astype(bf16)
        r.dv[keys_at] += dot(probs.astype(bf16), r.grad[queries_at])
        r.dk[keys_at] += dot(score_grad, r.query[queries_at])
        r.dq_t[:, queries_at] += dot(r.key_t[:, keys_at], score_grad)

    def finished(block):
        place = at_block(block, tb)
        columns = r.dq_t[:, place] * HD ** (-0.5)
        turned = jnp.transpose(jnp.concatenate([columns, jnp.zeros_like(columns)], axis=0))
        low_lane = lane_of(turned.shape) < HD
        r.stage[block, 0:tb] = jnp.where(low_lane, turned, swap_halves(r.dk[place])).astype(bf16)
        r.stage[block, tb:] = pack_rows(r.dv[place]).astype(bf16)
        x_back.give(block)

    for buffer in (r.dq_t, r.dk, r.dv):
        buffer[...] = jnp.zeros_like(buffer)
    ratio = QB // KB

    @pl.when(b >= n_b // 2)
    def _():
        def outer(kb, carry):
            def inner(qb, carry):
                backward(at_block(kb, KB), kb * KB, at_block(qb, QB), qb * QB)
                return carry

            lax.fori_loop(kb // ratio, seq // QB, inner, 0)
            finished(kb)
            return carry

        lax.fori_loop(0, n_b, outer, 0)

    @pl.when(b < n_b // 2)
    def _():
        def outer(step, carry):
            qb = n_b - 1 - step

            def inner(kb, carry):
                backward(at_block(kb, QB), kb * QB, at_block(qb, KB), qb * KB)
                return carry

            lax.fori_loop(0, qb // ratio + 1, inner, 0)
            finished(qb)
            return carry

        lax.fori_loop(0, n_b, outer, 0)

    r.returned[b] = r.stage[b]
    s_gate.merge()
    s_out.middle()
    arrive(got_f)
    for s in range(seqs):
        total = r.hidden[s] + sum(r.landed_f[v, s].astype(f32) for v in range(n_u))
        r.out[s] = total.astype(bf16)
        r.sums[2:3] = r.sums[2:3] + jnp.sum(total * total, axis=0, keepdims=True)
    s_down.finish(r.gwd)
    x_back.take()

    for s in range(seqs):
        for pair in range(heads // 2):
            unit = s * heads + 2 * pair
            one, two = r.returned[unit, 0:tb].astype(f32), r.returned[unit + 1, 0:tb].astype(f32)
            low_lane = lane_of(one.shape) < HD
            grads = (
                jnp.where(low_lane, one, swap_halves(two)),
                jnp.where(low_lane, swap_halves(one), two),
            )
            for i, tile in enumerate(grads):
                turned = tile * r.cosr[s] - partner(tile) * r.sinr[s]
                at = i * share + pair * LANES
                r.raw[s, :, at : at + LANES] = turned.astype(bf16)
            one = unpack_rows(r.returned[unit, tb:].astype(f32))
            two = unpack_rows(r.returned[unit + 1, tb:].astype(f32))
            both = 0.5 * jnp.where(low_lane, one, swap_halves(two))
            at = 2 * share + pair * LANES
            r.raw[s, :, at : at + LANES] = both.astype(bf16)
    columns = r.raw.shape[2]
    for v in range(n_u):
        left = r.normed[:, :, v * 256 : (v + 1) * 256].reshape(tokens, 256)
        found = dot_tn(left, r.raw[...].reshape(tokens, columns))
        r.wq_buf[:, :, v] = found.astype(bf16).reshape(n_z, 2, rows, columns)
    s_qkv = Scatter(net, u, b, lambda z, c: r.wq_buf.at[z, c], r.wq_pair, r.wq_sum, r.wq_land)
    s_out.merge()

    got_g = []
    for s in range(seqs):
        left = r.raw[s]
        for v in range(n_u):
            lanes = slice(v * 256, (v + 1) * 256)
            found = dot_nt(left, r.wq[v])
            r.gin_low[s, :, lanes] = found.astype(bf16)
            term = jnp.sum(found * r.hat[s, :, lanes].astype(f32), axis=0, keepdims=True)
            r.sums[3:4, lanes] = r.sums[3:4, lanes] + term
        got_g.append([net.push(r.gin_low.at[s, part(v)], r.landed.at[u, s], v, b) for v in others])
        r.landed[u, s] = r.gin_low[s, slab]
    got_s = [net.push(r.sums, r.sums_u.at[u], v, b) for v in others]
    r.sums_u[u] = r.sums[...]
    s_qkv.middle()
    got_v = [net.push(r.raw.at[:, part(v), pl.ds(2 * share, share)], r.gv.at[u], v, b) for v in others]
    r.gv[u] = r.raw[:, slab, 2 * share :]
    s_gate.finish(r.wg_low)
    got_c = [net.push(r.wg_low.at[v], r.dwgu.at[u], v, b) for v in others]
    r.dwgu[u] = r.wg_low[u]
    s_qkv.merge()
    s_out.finish(r.gwo)
    arrive(got_s)
    r.sums_b[b] = sum(r.sums_u[v] for v in range(n_u))
    got_s = [net.push(r.sums_b.at[b], r.sums_b.at[b], u, b ^ off) for off in range(1, n_b)]
    for s in range(seqs):
        arrive(got_g[s])
        grad_normed = sum(r.landed[v, s].astype(f32) for v in range(n_u))
        own = r.x[s].astype(f32)
        factor = lax.rsqrt(jnp.mean(own * own, axis=-1, keepdims=True) + epsilon)
        hat = own * factor
        scaled = grad_normed * r.gain[0:1, :]
        inner = jnp.mean(scaled * hat, axis=-1, keepdims=True)
        r.gin[s] = (r.ghid[s] + factor * (scaled - hat * inner)).astype(bf16)
    arrive(got_v)
    for v in range(n_u):
        r.gvf[:, :, v * 256 : (v + 1) * 256] = r.gv[v]
    arrive(got_s)
    totals = sum(r.sums_b[c] for c in range(n_b))
    squares = jnp.sum(totals, axis=1, keepdims=True) / (seqs * seq * width)
    r.totals[...] = totals
    roots = jnp.sqrt(squares)
    lane = lane_of((1, LANES))
    r.stats[...] = jnp.where(lane == 0, roots[0:1], jnp.where(lane == 1, roots[1:2], roots[2:3]))[0, 0:3]
    per = LANES // rows
    tile = r.totals[:, at_block(u * (n_b // per) + b // per, LANES)]
    tile = pltpu.roll(tile, (LANES - lane_place) % LANES, 1)
    r.gga[...] = tile[3, 0:rows]
    r.ggf[...] = tile[4, 0:rows]
    s_qkv.finish(r.wq_low)
    got = [net.push(r.wq_low.at[v], r.dwq.at[u], v, b) for v in others]
    r.dwq[u] = r.wq_low[u]
    arrive(got_c)
    for i, to in enumerate((r.gwg, r.gwu)):
        pieces = [
            r.dwgu[v, :, i * ff + j * ff_rows : i * ff + j * ff_rows + ff_own].astype(f32)
            for v in range(n_u)
            for j in range(n_b)
        ]
        to[...] = jnp.concatenate(pieces, axis=1)
    arrive(got)
    for i, to in enumerate((r.gwq, r.gwk, r.gwv)):
        for v in range(n_u):
            to[:, v * share : (v + 1) * share] = r.dwq[v, :, i * share : (i + 1) * share].astype(f32)
    for exchange in (x_out, x_grad, x_back):
        exchange.sent()
    net.drain()


def hand_out_kernel(count, *refs):
    for given, taken in zip(refs[:count], refs[count:]):
        taken[...] = given[...]


def local_units(
    inputs, v_first, grad_out, positions, segments,
    w_query, w_key, w_value, w_out, w_gate, w_up, w_down, gain_attn, gain_ffn,
):
    n_u, n_b = lax.axis_size("ulysses"), lax.axis_size("blk")
    seqs, td, width = inputs.shape
    rows = w_query.shape[0]
    heads = HEADS // n_u
    tb = n_u * td
    seq = n_b * tb
    ff_own = w_down.shape[0]
    ff_pad = -(-ff_own // 32) * 32
    ff = ff_pad * n_b
    dims = (n_u, n_b, seqs, td, rows, heads)

    columns = 3 * heads * HD
    n_z = n_b // 2
    own, block = (seqs, td, width), (seqs, tb, width)
    inputs_of = dict(
        x=inputs, vf=v_first, go=grad_out, segments=segments, wq_in=w_query, wk_in=w_key, wv_in=w_value,
        wout=w_out, wg_in=w_gate, wu_in=w_up, wd=w_down, ga=gain_attn, gf=gain_ffn,
    )
    outs = dict(
        out=(own, bf16), gin=(own, bf16), gvf=(own, bf16), gwq=((rows, width), f32), gwk=((rows, width), f32),
        gwv=((rows, width), f32), gwo=((rows, width), f32), gwg=(w_gate.shape, f32), gwu=(w_gate.shape, f32),
        gwd=((ff_own, width), f32), gga=((rows,), f32), ggf=((rows,), f32), stats=((3,), f32),
    )
    scratch = dict(
        gains=((8, LANES), f32), wgu=((n_u, rows, 2 * ff), bf16), cosr=((seqs, tb, LANES), f32),
        sinr=((seqs, tb, LANES), f32), low=((8, seq), jnp.int32),
        dwq=((n_u, rows, columns), bf16), dwgu=((n_u, rows, 2 * ff), bf16),
        xg=(block, bf16), vfg=((seqs, tb, heads * HD), bf16), gbuf=((n_b, n_u, 8, LANES), f32),
        gain=((8, width), f32), normed=(block, bf16), wq=((n_u, n_b * rows, columns), bf16),
        gog=(block, bf16), wg=((n_u, n_b * rows, 2 * ff), bf16), wdg=((ff, width), bf16),
        wo=((n_b * rows, width), bf16), stage=((n_b, tb + tb // 2, LANES), bf16),
        units=((n_b, tb + tb // 2, LANES), bf16), keys=((seq, LANES), bf16), key_t=((HD, seq), bf16),
        query=((seq, LANES), bf16), query_t=((LANES, seq), bf16), value=((seq, LANES), bf16),
        value_t=((HD, seq), bf16), acc=((HD, QB), f32), heads_t=((HD, seq), f32), lse=((8, seq), f32),
        ostage=((n_b, tb // 2, LANES), bf16), parts=((n_b, tb // 2, LANES), bf16),
        mix=((seqs, tb, heads * HD), bf16), branch=(block, bf16), landed=((n_u,) + own, bf16),
        sums=((8, width), f32), totals=((8, width), f32), hat=(block, bf16), hidden=(own, f32), nf_own=(own, bf16), nf=(block, bf16),
        act=((seqs, tb, ff), bf16), dgu=((seqs, tb, 2 * ff), bf16), d_low=(block, bf16),
        ghid=(own, f32), gb_own=(own, bf16),
        f_low=(block, bf16), landed_f=((n_u,) + own, bf16),
        wd_buf=((n_z, 2, ff_pad, width), bf16), wd_pair=((n_z, ff_pad, width), bf16),
        wd_sum=((n_z, ff_pad, width), bf16), wd_land=((n_z, ff_pad, width), bf16),
        wg_buf=((n_z, 2, n_u, rows, 2 * ff), bf16), wg_pair=((n_z, n_u, rows, 2 * ff), bf16),
        wg_sum=((n_z, n_u, rows, 2 * ff), bf16), wg_land=((n_z, n_u, rows, 2 * ff), bf16),
        wg_low=((n_u, rows, 2 * ff), bf16),
        ostage2=((n_b, tb // 2, LANES), bf16), grads=((n_b, tb // 2, LANES), bf16),
        wo_buf=((n_z, 2, rows, width), bf16), wo_pair=((n_z, rows, width), bf16),
        wo_sum=((n_z, rows, width), bf16), wo_land=((n_z, rows, width), bf16),
        grad=((seq, LANES), bf16), grad_t=((LANES, seq), bf16), row_dot=((8, seq), f32),
        dq_t=((HD, seq), f32), dk=((seq, LANES), f32), dv=((seq, LANES), f32),
        returned=((n_b, tb + tb // 2, LANES), bf16), raw=((seqs, tb, columns), bf16),
        gin_low=(block, bf16), gv=((n_u, seqs, td, heads * HD), bf16),
        wq_buf=((n_z, 2, n_u, rows, columns), bf16), wq_pair=((n_z, n_u, rows, columns), bf16),
        wq_sum=((n_z, n_u, rows, columns), bf16), wq_land=((n_z, n_u, rows, columns), bf16),
        wq_low=((n_u, rows, columns), bf16), sums_u=((n_u, 8, width), f32), sums_b=((n_b, 8, width), f32),
    )
    names = [*inputs_of, *outs, *scratch, "send_sems", "recv_sems"]
    vmem = pl.BlockSpec(memory_space=pltpu.VMEM)
    results = pl.pallas_call(
        functools.partial(layer_kernel, dims, names),
        out_shape=[jax.ShapeDtypeStruct(shape, dtype) for shape, dtype in outs.values()],
        in_specs=[vmem] * len(inputs_of),
        out_specs=[vmem] * len(outs),
        scratch_shapes=[pltpu.VMEM(shape, dtype) for shape, dtype in scratch.values()]
        + [pltpu.SemaphoreType.DMA((SEMAPHORES,))] * 2,
        compiler_params=pltpu.CompilerParams(
            collective_id=1, has_side_effects=True, vmem_limit_bytes=VMEM_BYTES
        ),
        name="layer",
    )(*inputs_of.values())
    return pl.pallas_call(
        functools.partial(hand_out_kernel, len(outs)),
        out_shape=[jax.ShapeDtypeStruct(shape, dtype) for shape, dtype in outs.values()],
        in_specs=[vmem] * len(outs),
        out_specs=[vmem] * len(outs),
        name="hand_out",
    )(*results)


SEMAPHORES = 224


def fits_units(mesh):
    return mesh.shape["ulysses"] == 4 and mesh.shape["blk"] == 8


def solution(mesh):
    in_specs = (
        P(None, ("blk", "ulysses"), None),
        P(None, ("blk", "ulysses"), None),
        P(None, ("blk", "ulysses"), None),
        P(None, ("blk", "ulysses")),
        P(),
        P(("ulysses", "blk"), None),
        P(("ulysses", "blk"), None),
        P(("ulysses", "blk"), None),
        P(("ulysses", "blk"), None),
        P(("ulysses", "blk"), None),
        P(("ulysses", "blk"), None),
        P(("ulysses", "blk"), None),
        P(("ulysses", "blk")),
        P(("ulysses", "blk")),
    )
    out_specs = (
        P(None, ("blk", "ulysses"), None),
        P(None, ("blk", "ulysses"), None),
        P(None, ("blk", "ulysses"), None),
        P(("ulysses", "blk"), None),
        P(("ulysses", "blk"), None),
        P(("ulysses", "blk"), None),
        P(("ulysses", "blk"), None),
        P(("ulysses", "blk"), None),
        P(("ulysses", "blk"), None),
        P(("ulysses", "blk"), None),
        P(("ulysses", "blk")),
        P(("ulysses", "blk")),
        P(),
    )
    path = local_units if fits_units(mesh) else local
    return jax.shard_map(path, mesh=mesh, in_specs=in_specs, out_specs=out_specs, check_vma=False)
```

```python
import functools
import types

import jax
import jax.numpy as jnp
import numpy as np
from jax import lax
from jax.experimental import pallas as pl
from jax.experimental.pallas import tpu as pltpu
from jax.sharding import PartitionSpec as P

HEADS = 16
HD = 64


epsilon = 1e-06
rope_base = 10000.0
neg_big = -1e30


def norm_rows(values, gain):
    factor = lax.rsqrt(jnp.mean(values * values, axis=-1, keepdims=True) + epsilon)
    hatted = values * factor
    return (hatted * gain, hatted, factor)


def norm_back(grad_normed, hatted, factor, gain):
    scaled = grad_normed * gain
    inner = jnp.mean(scaled * hatted, axis=-1, keepdims=True)
    return (factor * (scaled - hatted * inner), jnp.sum(grad_normed * hatted, axis=(0, 1)))


def rope_tables(positions):
    half_dim = HD // 2
    inverse = rope_base ** (-2.0 * jnp.arange(half_dim, dtype=jnp.float32) / HD)
    angles = positions.astype(jnp.float32)[:, :, None] * inverse
    return (jnp.cos(angles)[:, :, None, :], jnp.sin(angles)[:, :, None, :])


def rotate(values, cosine, sine, forward_turn):
    shaped = values.reshape(values.shape[0], values.shape[1], HEADS, HD)
    half_dim = HD // 2
    first = shaped[..., :half_dim]
    second = shaped[..., half_dim:]
    if forward_turn:
        turned = jnp.concatenate(
            [first * cosine - second * sine, second * cosine + first * sine], axis=-1
        )
    else:
        turned = jnp.concatenate(
            [first * cosine + second * sine, second * cosine - first * sine], axis=-1
        )
    return turned.reshape(values.shape)


def project(activations, weight):
    return jnp.einsum("std,de->ste", activations, weight, preferred_element_type=jnp.float32)


def project_back(gradient, weight):
    return jnp.einsum("ste,de->std", gradient, weight, preferred_element_type=jnp.float32)


def weight_grad(activations, gradient):
    return jnp.einsum("std,ste->de", activations, gradient, preferred_element_type=jnp.float32)


def allowed_mask(segments, query_first, query_count, key_first, key_count):
    seg_query = lax.dynamic_slice_in_dim(segments, query_first, query_count, 1)
    seg_key = lax.dynamic_slice_in_dim(segments, key_first, key_count, 1)
    query_place = query_first + jnp.arange(query_count, dtype=jnp.int32)
    key_place = key_first + jnp.arange(key_count, dtype=jnp.int32)
    causal = key_place[None, :] <= query_place[:, None]
    same_doc = seg_query[:, :, None] == seg_key[:, None, :]
    return (causal[None] & same_doc)[:, :, None, :]


def over_blocks(step_fn, running, pieces, block_rows):
    row_count = pieces[0].shape[1]
    block_count = row_count // block_rows
    stacked = tuple(
        (
            jnp.moveaxis(
                member.reshape((member.shape[0], block_count, block_rows) + member.shape[2:]), 1, 0
            )
            for member in pieces
        )
    )
    offsets = block_rows * jnp.arange(block_count, dtype=jnp.int32)

    def advance(current, scan_entry):
        return (step_fn(current, scan_entry[:-1], scan_entry[-1]), None)

    running, unused = lax.scan(advance, running, stacked + (offsets,))
    return running


def add_rows(buffer, update, first_row):
    current = lax.dynamic_slice_in_dim(buffer, first_row, update.shape[1], 1)
    return lax.dynamic_update_slice_in_dim(buffer, current + update, first_row, 1)


def unchanged(running):
    return running


def local(
    inputs,
    v_first,
    grad_out,
    positions,
    segments,
    w_query,
    w_key,
    w_value,
    w_out,
    w_gate,
    w_up,
    w_down,
    gain_attn,
    gain_ffn,
):
    gathered = (
        lax.all_gather(w_query, ("ulysses", "blk"), axis=0, tiled=True),
        lax.all_gather(w_key, ("ulysses", "blk"), axis=0, tiled=True),
        lax.all_gather(w_value, ("ulysses", "blk"), axis=0, tiled=True),
        lax.all_gather(w_out, ("ulysses", "blk"), axis=0, tiled=True),
        lax.all_gather(w_gate, ("ulysses", "blk"), axis=0, tiled=True),
        lax.all_gather(w_up, ("ulysses", "blk"), axis=0, tiled=True),
        lax.all_gather(w_down, ("ulysses", "blk"), axis=0, tiled=True),
        lax.all_gather(gain_attn, ("ulysses", "blk"), axis=0, tiled=True),
        lax.all_gather(gain_ffn, ("ulysses", "blk"), axis=0, tiled=True),
    )
    (
        full_query,
        full_key,
        full_value,
        full_out,
        full_gate,
        full_up,
        full_down,
        full_gain_attn,
        full_gain_ffn,
    ) = gathered
    score_scale = HD ** (-0.5)
    residual = inputs.astype(jnp.float32)
    normed_f, hatted_attn, factor_attn = norm_rows(residual, full_gain_attn.astype(jnp.float32))
    normed = normed_f.astype(jnp.bfloat16)
    cosine, sine = rope_tables(positions)
    query_tok = rotate(project(normed, full_query), cosine, sine, True).astype(jnp.bfloat16)
    key_tok = rotate(project(normed, full_key), cosine, sine, True).astype(jnp.bfloat16)
    value_tok = (0.5 * project(normed, full_value) + 0.5 * v_first.astype(jnp.float32)).astype(
        jnp.bfloat16
    )
    query_head, key_head, value_head = (
        lax.all_to_all(query_tok, "ulysses", split_axis=2, concat_axis=1, tiled=True),
        lax.all_to_all(key_tok, "ulysses", split_axis=2, concat_axis=1, tiled=True),
        lax.all_to_all(value_tok, "ulysses", split_axis=2, concat_axis=1, tiled=True),
    )
    seq_count, block_rows, width = query_head.shape
    heads_local = width // HD
    query_start = lax.axis_index("blk") * block_rows
    full_rows = block_rows * lax.axis_size("blk")

    def split_heads(values):
        return values.reshape(values.shape[0], values.shape[1], heads_local, HD)

    query_four = split_heads(query_head)

    def attend_rows(running, pieces, first_row):
        key_rows, value_rows = pieces
        key_count = key_rows.shape[1]

        def attend_compute(current):
            best, total, accum = current
            allowed = allowed_mask(segments, query_start, block_rows, first_row, key_count)
            scores = (
                jnp.einsum(
                    "sqhd,skhd->sqhk",
                    query_four,
                    split_heads(key_rows),
                    preferred_element_type=jnp.float32,
                )
                * score_scale
            )
            masked = jnp.where(allowed, scores, neg_big)
            new_best = jnp.maximum(best, jnp.max(masked, axis=-1))
            weights = jnp.where(allowed, jnp.exp(masked - new_best[..., None]), 0.0)
            rescale = jnp.exp(best - new_best)
            total = total * rescale + jnp.sum(weights, axis=-1)
            accum = accum * rescale[..., None] + jnp.einsum(
                "sqhk,skhd->sqhd",
                weights.astype(jnp.bfloat16),
                split_heads(value_rows),
                preferred_element_type=jnp.float32,
            )
            return (new_best, total, accum)

        return lax.cond(
            first_row <= query_start + block_rows - 1, attend_compute, unchanged, running
        )

    stat_zeros = jnp.zeros((seq_count, block_rows, heads_local), jnp.float32)
    head_zeros = jnp.zeros((seq_count, block_rows, heads_local, HD), jnp.float32)
    initial = (
        jnp.full((seq_count, block_rows, heads_local), neg_big, jnp.float32),
        stat_zeros,
        head_zeros,
    )
    best, total, accum = over_blocks(
        attend_rows,
        initial,
        (
            lax.all_gather(key_head, "blk", axis=1, tiled=True),
            lax.all_gather(value_head, "blk", axis=1, tiled=True),
        ),
        block_rows,
    )
    log_total = best + jnp.log(total)
    attn_heads = accum / total[..., None]
    attn_low = attn_heads.reshape(seq_count, block_rows, width).astype(jnp.bfloat16)
    mixed = lax.all_to_all(attn_low, "ulysses", split_axis=1, concat_axis=2, tiled=True)
    attn_branch = project(mixed, full_out)
    hidden = residual + attn_branch
    normed_ffn_f, hatted_ffn, factor_ffn = norm_rows(hidden, full_gain_ffn.astype(jnp.float32))
    normed_ffn = normed_ffn_f.astype(jnp.bfloat16)
    gate = project(normed_ffn, full_gate)
    up_proj = project(normed_ffn, full_up)
    sigmoid_gate = jax.nn.sigmoid(gate)
    silu_gate = gate * sigmoid_gate
    act = (silu_gate * up_proj).astype(jnp.bfloat16)
    ffn_branch = project(act, full_down)
    output_f = hidden + ffn_branch
    output = output_f.astype(jnp.bfloat16)
    squares = lax.psum(
        (
            jnp.sum(residual * residual),
            jnp.sum(attn_branch * attn_branch),
            jnp.sum(output_f * output_f),
        ),
        ("ulysses", "blk"),
    )
    entry_count = residual.size * lax.axis_size("ulysses") * lax.axis_size("blk")
    statistics = jnp.sqrt(jnp.stack(squares) / entry_count)
    again = (
        lax.all_gather(w_query, ("ulysses", "blk"), axis=0, tiled=True),
        lax.all_gather(w_key, ("ulysses", "blk"), axis=0, tiled=True),
        lax.all_gather(w_value, ("ulysses", "blk"), axis=0, tiled=True),
        lax.all_gather(w_out, ("ulysses", "blk"), axis=0, tiled=True),
        lax.all_gather(w_gate, ("ulysses", "blk"), axis=0, tiled=True),
        lax.all_gather(w_up, ("ulysses", "blk"), axis=0, tiled=True),
        lax.all_gather(w_down, ("ulysses", "blk"), axis=0, tiled=True),
        lax.all_gather(gain_attn, ("ulysses", "blk"), axis=0, tiled=True),
        lax.all_gather(gain_ffn, ("ulysses", "blk"), axis=0, tiled=True),
    )
    (
        back_query,
        back_key,
        back_value,
        back_out,
        back_gate,
        back_up,
        back_down,
        back_gain_attn,
        back_gain_ffn,
    ) = again
    grad_act = project_back(grad_out, back_down)
    grad_gate = (grad_act * up_proj * sigmoid_gate * (1.0 + gate * (1.0 - sigmoid_gate))).astype(
        jnp.bfloat16
    )
    grad_up = (grad_act * silu_gate).astype(jnp.bfloat16)
    grad_normed_ffn = project_back(grad_gate, back_gate) + project_back(grad_up, back_up)
    grad_ffn_norm, grad_gain_ffn = norm_back(
        grad_normed_ffn, hatted_ffn, factor_ffn, back_gain_ffn.astype(jnp.float32)
    )
    grad_hidden = grad_out.astype(jnp.float32) + grad_ffn_norm
    grad_branch = grad_hidden.astype(jnp.bfloat16)
    grad_mixed = project_back(grad_branch, back_out).astype(jnp.bfloat16)
    dout_head = lax.all_to_all(grad_mixed, "ulysses", split_axis=2, concat_axis=1, tiled=True)
    dout_four = split_heads(dout_head)
    row_dot = jnp.sum(dout_four.astype(jnp.float32) * attn_heads, axis=-1)

    def grad_rows(running, pieces, first_row):
        key_rows, value_rows = pieces
        key_count = key_rows.shape[1]

        def grad_compute(current):
            grad_query, grad_keys, grad_values = current
            key_part = split_heads(key_rows)
            allowed = allowed_mask(segments, query_start, block_rows, first_row, key_count)
            scores = (
                jnp.einsum(
                    "sqhd,skhd->sqhk", query_four, key_part, preferred_element_type=jnp.float32
                )
                * score_scale
            )
            probs = jnp.where(allowed, jnp.exp(scores - log_total[..., None]), 0.0)
            prob_grad = jnp.einsum(
                "sqhd,skhd->sqhk",
                dout_four,
                split_heads(value_rows),
                preferred_element_type=jnp.float32,
            )
            score_grad = (probs * (prob_grad - row_dot[..., None])).astype(jnp.bfloat16)
            grad_query = (
                grad_query
                + jnp.einsum(
                    "sqhk,skhd->sqhd", score_grad, key_part, preferred_element_type=jnp.float32
                )
                * score_scale
            )
            key_term = (
                jnp.einsum(
                    "sqhk,sqhd->skhd", score_grad, query_four, preferred_element_type=jnp.float32
                )
                * score_scale
            )
            value_term = jnp.einsum(
                "sqhk,sqhd->skhd",
                probs.astype(jnp.bfloat16),
                dout_four,
                preferred_element_type=jnp.float32,
            )
            return (
                grad_query,
                add_rows(grad_keys, key_term, first_row),
                add_rows(grad_values, value_term, first_row),
            )

        return lax.cond(first_row <= query_start + block_rows - 1, grad_compute, unchanged, running)

    full_zeros = jnp.zeros((seq_count, full_rows, heads_local, HD), jnp.float32)
    grad_query_own, grad_keys_all, grad_values_all = over_blocks(
        grad_rows,
        (head_zeros, full_zeros, full_zeros),
        (
            lax.all_gather(key_head, "blk", axis=1, tiled=True),
            lax.all_gather(value_head, "blk", axis=1, tiled=True),
        ),
        block_rows,
    )
    grad_key_own, grad_value_own = (
        lax.psum_scatter(
            grad_keys_all.reshape(seq_count, full_rows, width).astype(jnp.bfloat16),
            "blk",
            scatter_dimension=1,
            tiled=True,
        ).astype(jnp.float32),
        lax.psum_scatter(
            grad_values_all.reshape(seq_count, full_rows, width).astype(jnp.bfloat16),
            "blk",
            scatter_dimension=1,
            tiled=True,
        ).astype(jnp.float32),
    )
    grad_query_own = grad_query_own.reshape(seq_count, block_rows, width)
    grad_query_tok, grad_key_tok, grad_value_tok = (
        lax.all_to_all(
            grad_query_own.astype(jnp.bfloat16), "ulysses", split_axis=1, concat_axis=2, tiled=True
        ),
        lax.all_to_all(
            grad_key_own.astype(jnp.bfloat16), "ulysses", split_axis=1, concat_axis=2, tiled=True
        ),
        lax.all_to_all(
            grad_value_own.astype(jnp.bfloat16), "ulysses", split_axis=1, concat_axis=2, tiled=True
        ),
    )
    grad_query_raw = rotate(grad_query_tok.astype(jnp.float32), cosine, sine, False).astype(
        jnp.bfloat16
    )
    grad_key_raw = rotate(grad_key_tok.astype(jnp.float32), cosine, sine, False).astype(
        jnp.bfloat16
    )
    grad_v_first = grad_value_tok * 0.5
    grad_normed = (
        project_back(grad_query_raw, back_query)
        + project_back(grad_key_raw, back_key)
        + project_back(grad_v_first, back_value)
    )
    grad_attn_norm, grad_gain_attn = norm_back(
        grad_normed, hatted_attn, factor_attn, back_gain_attn.astype(jnp.float32)
    )
    grad_inputs = (grad_hidden + grad_attn_norm).astype(jnp.bfloat16)
    model_width = w_query.shape[1]
    hidden_width = w_gate.shape[1]
    owned = lax.psum_scatter(
        jnp.concatenate(
            [
                weight_grad(normed, grad_query_raw),
                weight_grad(normed, grad_key_raw),
                weight_grad(normed, grad_v_first),
                weight_grad(mixed, grad_branch),
                weight_grad(normed_ffn, grad_gate),
                weight_grad(normed_ffn, grad_up),
                grad_gain_attn[:, None],
                grad_gain_ffn[:, None],
            ],
            axis=1,
        ),
        ("ulysses", "blk"),
        scatter_dimension=0,
        tiled=True,
    )
    grad_w_down = lax.psum_scatter(
        weight_grad(act, grad_out), ("ulysses", "blk"), scatter_dimension=0, tiled=True
    )
    column = 0
    pieces = []
    for span in (model_width, model_width, model_width, model_width, hidden_width, hidden_width):
        pieces.append(owned[:, column : column + span])
        column = column + span
    grad_gain_attn_own = owned[:, column]
    grad_gain_ffn_own = owned[:, column + 1]
    return (
        output,
        grad_inputs,
        grad_v_first,
        pieces[0],
        pieces[1],
        pieces[2],
        pieces[3],
        pieces[4],
        pieces[5],
        grad_w_down,
        grad_gain_attn_own,
        grad_gain_ffn_own,
        statistics,
    )


MESH = pl.DeviceIdType.MESH
LANES = 128
VMEM_BYTES = 61 << 20
f32 = jnp.float32
bf16 = jnp.bfloat16
QB, KB = 512, 256


class Copy:
    def __init__(self, copy, send_at, recv_at, when):
        self.copy, self.at, self.recv_at, self.when = copy, send_at, recv_at, when

    def wait_recv(self):
        self.copy.wait_recv()

    def wait_send(self):
        if self.when is None:
            self.copy.wait_send()
        else:
            pl.when(self.when)(self.copy.wait_send)


class Net:
    def __init__(self, send_sems, recv_sems):
        self.send_sems, self.recv_sems = send_sems, recv_sems
        self.count, self.open = 0, []

    def push(self, src, dst, u, b, when=None, recv_at=None, at=None):
        if at is None:
            at = self.count
            self.count += 1
        recv_at = at if recv_at is None else recv_at
        copy = pltpu.make_async_remote_copy(
            src_ref=src,
            dst_ref=dst,
            send_sem=self.send_sems.at[at],
            recv_sem=self.recv_sems.at[recv_at],
            device_id=(u, b),
            device_id_type=MESH,
        )
        if when is None:
            copy.start()
        else:
            pl.when(when)(copy.start)
        made = Copy(copy, at, recv_at, when)
        self.open.append(made)
        return made

    def sent(self, copies):
        for copy in copies:
            copy.wait_send()
        self.open = [copy for copy in self.open if copy not in copies]

    def drain(self):
        for copy in self.open:
            copy.wait_send()
        self.open = []


def arrive(copies):
    for copy in copies:
        copy.wait_recv()


def here():
    return lax.axis_index("ulysses"), lax.axis_index("blk")


def greet(u, b, n_u, n_b):
    barrier = pltpu.get_barrier_semaphore()
    for off in range(1, n_u):
        pl.semaphore_signal(barrier, inc=1, device_id=(u ^ off, b), device_id_type=MESH)
    for off in range(1, n_b):
        pl.semaphore_signal(barrier, inc=1, device_id=(u, b ^ off), device_id_type=MESH)
    pl.semaphore_wait(barrier, n_u - 1 + n_b - 1)


def dot(left, right):
    return jnp.dot(left, right, preferred_element_type=f32)


def dot_nt(left, right):
    return lax.dot_general(left, right, (((1,), (1,)), ((), ())), preferred_element_type=f32)


def dot_tn(left, right):
    return lax.dot_general(left, right, (((0,), (0,)), ((), ())), preferred_element_type=f32)


def at_block(index, size):
    return pl.ds(pl.multiple_of(index * size, size), size)


def lane_of(shape):
    return lax.broadcasted_iota(jnp.int32, shape, len(shape) - 1)


def swap_halves(tile):
    return pltpu.roll(tile, HD, tile.ndim - 1)


def partner(tile):
    low = lane_of(tile.shape) % HD < HD // 2
    return jnp.where(low, pltpu.roll(tile, LANES - HD // 2, 1), pltpu.roll(tile, HD // 2, 1))


def pack_rows(rows):
    half = rows.shape[0] // 2
    low = lane_of((half, LANES)) < HD
    return jnp.where(low, rows[:half], swap_halves(rows[half:]))


def unpack_rows(packed):
    return jnp.concatenate([packed, swap_halves(packed)], axis=0)


class Exchange:
    def __init__(self, net, staged, landed, u, b, n_b):
        self.net, self.staged, self.landed, self.u, self.b, self.n_b = net, staged, landed, u, b, n_b
        self.at = net.count
        net.count += n_b

    def copy(self, to, slot_from):
        return pltpu.make_async_remote_copy(
            src_ref=self.staged.at[to],
            dst_ref=self.landed.at[slot_from],
            send_sem=self.net.send_sems.at[self.at + to],
            recv_sem=self.net.recv_sems.at[self.at + slot_from],
            device_id=(self.u, to),
            device_id_type=MESH,
        )

    def give(self, to):
        @pl.when(to != self.b)
        def _():
            self.copy(to, self.b).start()

    def take(self):
        for off in range(1, self.n_b):
            self.copy(self.b ^ off, self.b ^ off).wait_recv()

    def sent(self):
        for off in range(1, self.n_b):
            self.copy(self.b ^ off, self.b).wait_send()


class Gather:
    def __init__(self, net, slot, u, b):
        self.net, self.slot, self.u, self.b = net, slot, u, b
        self.inner = ((b // 2) == 1) | ((b // 2) == 2)
        mine = slot(b)
        self.two = net.push(mine, mine, u, b ^ 4)
        self.one = net.push(mine, mine, u, b ^ 2)
        self.three = net.push(mine, mine, u, b ^ 6, when=self.inner)
        self.side = [net.push(mine, mine, u, b ^ 1)]

    def beside(self, owner):
        got = self.slot(owner)
        self.side.append(self.net.push(got, got, self.u, self.b ^ 1))

    def forward(self):
        self.two.wait_recv()
        got = self.slot(self.b ^ 4)
        self.net.push(got, got, self.u, self.b ^ 2, when=self.inner, recv_at=self.three.at)
        self.beside(self.b ^ 4)

    def relay(self):
        self.one.wait_recv()
        self.beside(self.b ^ 2)
        self.three.wait_recv()
        self.beside(self.b ^ 6)

    def finish(self):
        arrive(self.side)


class Scatter:
    def __init__(self, net, u, b, mine, paired, summed, landed):
        self.net, self.u, self.b = net, u, b
        self.mine, self.paired, self.summed, self.landed = mine, paired, summed, landed
        self.z = b // 2
        self.inner = (self.z == 1) | (self.z == 2)
        self.swap = [net.push(mine(z, 1 - b % 2), paired.at[z], u, b ^ 1) for z in range(4)]

    def add(self, z):
        self.summed[z] = (self.mine(z, self.b % 2)[...].astype(f32) + self.paired[z].astype(f32)).astype(bf16)

    def middle(self):
        net, u, b, z, inner = self.net, self.u, self.b, self.z, self.inner
        outer = jnp.logical_not(inner)
        arrive(self.swap)
        self.add(z ^ 3)
        far = self.summed.at[z ^ 3]
        self.extra = net.push(far, self.landed.at[3], u, b ^ 2, when=outer)
        self.three = net.push(far, self.landed.at[2], u, b ^ 6, when=inner)
        self.add(z ^ 2)
        self.two = net.push(self.summed.at[z ^ 2], self.landed.at[1], u, b ^ 4, when=outer)
        self.add(z ^ 1)
        self.one = net.push(self.summed.at[z ^ 1], self.landed.at[0], u, b ^ 2)
        self.add(z)

    def merge(self):
        net, u, b, z = self.net, self.u, self.b, self.z

        @pl.when(self.inner)
        def _():
            self.extra.wait_recv()
            self.summed[z ^ 2] = (self.summed[z ^ 2].astype(f32) + self.landed[3].astype(f32)).astype(bf16)

        net.push(self.summed.at[z ^ 2], self.landed.at[1], u, b ^ 4, when=self.inner, at=self.two.at)

    def finish(self, total):
        self.one.wait_recv()
        self.two.wait_recv()
        total[...] = (
            self.summed[self.z].astype(f32) + self.landed[0].astype(f32) + self.landed[1].astype(f32)
        ).astype(total.dtype)

        @pl.when(self.inner)
        def _():
            self.three.wait_recv()
            total[...] = (total[...].astype(f32) + self.landed[2].astype(f32)).astype(total.dtype)


def fill_units(units, tb, store):
    def one(block, carry):
        low = lane_of((tb, LANES)) < HD
        tile = units[block, 0:tb].astype(f32)
        query = jnp.where(low, tile * HD ** (-0.5), 0.0)
        key = jnp.where(low, swap_halves(tile), 0.0)
        value = jnp.where(low, unpack_rows(units[block, tb:].astype(f32)), 0.0)
        store(block, query, key, value)
        return carry

    lax.fori_loop(0, units.shape[0], one, 0)


def allowed_block(first_key, first_query, low_row, keys=KB, queries=QB):
    key_place = first_key + lax.broadcasted_iota(jnp.int32, (keys, queries), 0)
    query_place = first_query + lax.broadcasted_iota(jnp.int32, (keys, queries), 1)
    return (key_place <= query_place) & (key_place >= low_row)


def widen(rows, size, padded):
    zeros = jnp.zeros((rows.shape[0], padded - size), rows.dtype)
    pieces = []
    for at in range(0, rows.shape[1], size):
        pieces += [rows[:, at : at + size], zeros]
    return jnp.concatenate(pieces, axis=1)


def rope_rows(base, cut, count):
    place = base + lax.broadcasted_iota(jnp.int32, (count, LANES), 0)
    place = place.astype(f32)
    local_place = jnp.where(place >= cut, place - cut, place)
    pair = lane_of((count, LANES)) % (HD // 2)
    inverse = jnp.zeros((1, LANES), f32)
    for i in range(HD // 2):
        inverse = jnp.where(pair[0:1] == i, float(np.float32(rope_base ** (-2.0 * i / HD))), inverse)
    angles = local_place * inverse
    sign = jnp.where(lane_of((count, LANES)) % HD < HD // 2, -1.0, 1.0)
    return jnp.cos(angles), sign * jnp.sin(angles)


def layer_kernel(dims, names, *refs):
    n_u, n_b, seqs, td, rows, heads = dims
    r = types.SimpleNamespace(**dict(zip(names, refs)))
    tb = n_u * td
    tokens = seqs * tb
    seq = n_b * tb
    n_z = n_b // 2
    width = r.x.shape[2]
    u, b = here()
    net = Net(r.send_sems, r.recv_sems)
    others = [u ^ off for off in range(1, n_u)]
    slab = at_block(u, td)
    mine = at_block(b, rows)
    ff = r.wdg.shape[0]
    ff_rows = ff // n_b
    chunks = ff // 256

    def part(v):
        return at_block(v, td)

    share = heads * HD
    ff_own = r.wd.shape[0]
    thirds = (r.wq_in, r.wk_in, r.wv_in)
    r.gains[...] = jnp.zeros_like(r.gains)
    for row, gain in enumerate((r.ga, r.gf)):
        r.gains[row : row + 1, 0:rows] = gain[...].astype(f32).reshape(1, rows)
    lane_place = (b % (LANES // rows)) * rows
    r.gains[...] = pltpu.roll(r.gains[...], lane_place, 1)
    greet(u, b, n_u, n_b)
    got_g = [net.push(r.gains, r.gbuf.at[b, u], v, b) for v in others]
    got_w = [
        net.push(w.at[:, at_block(v, share)], r.wq.at[u, mine, pl.ds(i * share, share)], v, b)
        for i, w in enumerate(thirds)
        for v in others
    ]
    r.wo[mine] = r.wout[...]
    g_out = Gather(net, lambda c: r.wo.at[at_block(c, rows)], u, b)
    got_x = [[net.push(r.x.at[s], r.xg.at[s, slab], v, b) for v in others] for s in range(seqs)]
    for i, w in enumerate(thirds):
        r.wq[u, mine, i * share : (i + 1) * share] = w[:, at_block(u, share)]
    r.xg[:, slab] = r.x[...]
    r.vfg[:, slab] = r.vf[:, :, at_block(u, share)]
    r.gog[:, slab] = r.go[...]
    r.gbuf[b, u] = r.gains[...]
    arrive(got_g)
    got_g = [net.push(r.gbuf.at[b], r.gbuf.at[b], u, b ^ off) for off in range(1, n_b)]
    arrive(got_w)
    g_qk = Gather(net, lambda c: r.wq.at[:, at_block(c, rows), pl.ds(0, 2 * share)], u, b)
    g_v = Gather(net, lambda c: r.wq.at[:, at_block(c, rows), pl.ds(2 * share, share)], u, b)
    got_v = [net.push(r.vf.at[:, :, at_block(v, share)], r.vfg.at[:, slab], v, b) for v in others]
    seq_of_unit = b // heads
    for s in range(seqs):
        cut = jnp.sum((1 - r.segments[s : s + 1, :]).astype(f32), axis=1, keepdims=True)
        r.cosr[s], r.sinr[s] = rope_rows(b * tb, cut, tb)

        @pl.when(seq_of_unit == s)
        def _():
            key_place = lane_of((8, seq)).astype(f32)
            r.low[...] = jnp.where(key_place >= cut, cut, 0.0).astype(jnp.int32)

    arrive(got_g)
    per_tile = LANES // rows
    for tile in range(n_u * n_b // per_tile):
        total = None
        for index in range(tile * per_tile, (tile + 1) * per_tile):
            term = r.gbuf[index % n_b, index // n_b]
            total = term if total is None else total + term
        r.gain[:, tile * LANES : (tile + 1) * LANES] = total
    for s in range(seqs):
        arrive(got_x[s])

        def norm(step, carry, s=s):
            place = at_block(step, tb // 2)
            values = r.xg[s, place].astype(f32)
            factor = lax.rsqrt(jnp.mean(values * values, axis=-1, keepdims=True) + epsilon)
            hat = values * factor
            r.hat[s, place] = hat.astype(bf16)
            r.normed[s, place] = (hat * r.gain[0:1, :]).astype(bf16)
            return carry

        lax.fori_loop(0, 2, norm, 0)
    got_go = [net.push(r.go, r.gog.at[:, slab], v, b) for v in others]
    g_qk.forward()
    g_qk.relay()
    g_v.forward()
    g_qk.finish()

    x_qk = Exchange(net, r.stage.at[:, pl.ds(0, tb)], r.units.at[:, pl.ds(0, tb)], u, b, n_b)
    x_v = Exchange(net, r.stage.at[:, pl.ds(tb, tb // 2)], r.units.at[:, pl.ds(tb, tb // 2)], u, b, n_b)
    for s in range(seqs):
        left = r.normed[s]
        for n in range(heads // 4):
            spans = [slice(i * share + n * 256, i * share + (n + 1) * 256) for i in range(2)]
            pair_of = [dot(left, r.wq[:, :, span].reshape(width, 256)) for span in spans]
            for i in range(2):
                lanes = slice(i * LANES, (i + 1) * LANES)
                query, key = [f[:, lanes] * r.cosr[s] + partner(f[:, lanes]) * r.sinr[s] for f in pair_of]
                low_lane = lane_of(query.shape) < HD
                unit = s * heads + 4 * n + 2 * i
                r.stage[unit, 0:tb] = jnp.where(low_lane, query, swap_halves(key)).astype(bf16)
                r.stage[unit + 1, 0:tb] = jnp.where(low_lane, swap_halves(query), key).astype(bf16)
        for unit in range(s * heads, (s + 1) * heads):
            x_qk.give(unit)
    arrive(got_v)
    g_v.relay()
    g_v.finish()
    for s in range(seqs):
        left = r.normed[s]
        for n in range(heads // 4):
            first_lane = 2 * share + n * 256
            found = dot(left, r.wq[:, :, first_lane : first_lane + 256].reshape(width, 256))
            for i in range(2):
                first = r.vfg[s, :, n * 256 + i * LANES : n * 256 + (i + 1) * LANES].astype(f32)
                value = 0.5 * found[:, i * LANES : (i + 1) * LANES] + 0.5 * first
                unit = s * heads + 4 * n + 2 * i
                r.stage[unit, tb:] = pack_rows(value).astype(bf16)
                r.stage[unit + 1, tb:] = pack_rows(swap_halves(value)).astype(bf16)
        for unit in range(s * heads, (s + 1) * heads):
            x_v.give(unit)
    for i, w in enumerate((r.wg_in, r.wu_in)):
        wide_rows = widen(w[...], ff_own, ff_rows)
        for v in range(n_u):
            for n in range(chunks):
                at = (2 * n + i) * 256
                r.wgu[v, :, at : at + 256] = wide_rows[:, v * ff + n * 256 : v * ff + (n + 1) * 256]
    r.wg[u, mine] = r.wgu[u]
    got_o = [net.push(r.wgu.at[v], r.wg.at[u, mine], v, b) for v in others]
    r.units[b] = r.stage[b]
    for slot in range(n_b):
        r.wdg[slot * ff_rows + ff_own : (slot + 1) * ff_rows] = jnp.zeros((ff_rows - ff_own, width), bf16)
    r.wdg[pl.ds(pl.multiple_of(b * ff_rows, ff_rows), ff_own)] = r.wd[...]
    g_out.forward()
    g_out.relay()
    x_qk.take()
    x_v.take()
    g_out.finish()

    g_down = Gather(net, lambda c: r.wdg.at[pl.ds(pl.multiple_of(c * ff_rows, ff_rows), ff_own)], u, b)
    x_out = Exchange(net, r.ostage, r.parts, u, b, n_b)

    def store(block, query, key, value):
        place = at_block(block, tb)
        r.keys[place] = key.astype(bf16)
        r.key_t[:, place] = jnp.transpose(key)[:HD].astype(bf16)
        r.query[place] = query.astype(bf16)
        r.query_t[:, place] = jnp.transpose(query).astype(bf16)
        r.value[place] = value.astype(bf16)
        r.value_t[:, place] = jnp.transpose(value)[:HD].astype(bf16)

    fill_units(r.units, tb, store)

    def attend(step, carry):
        qb = seq // QB - 1 - step
        q_at = at_block(qb, QB)
        query = r.query_t[:, q_at]
        low_row = r.low[0:1, q_at]
        r.acc[...] = jnp.zeros_like(r.acc)

        def inner(kb, state):
            best, total = state
            k_at = at_block(kb, KB)
            scores = dot(r.keys[k_at], query)
            scores = jnp.where(allowed_block(kb * KB, qb * QB, low_row), scores, neg_big)
            new_best = jnp.maximum(best, jnp.max(scores, axis=0, keepdims=True))
            weights = jnp.exp(scores - new_best)
            rescale = jnp.exp(best - new_best)
            total = total * rescale + jnp.sum(weights, axis=0, keepdims=True)
            r.acc[...] = r.acc[...] * rescale + dot(r.value_t[:, k_at], weights.astype(bf16))
            return new_best, total

        start = (jnp.full((1, QB), neg_big, f32), jnp.zeros((1, QB), f32))
        best, total = lax.fori_loop(0, (qb + 1) * (QB // KB), inner, start)
        out = r.acc[...] / total
        r.heads_t[:, q_at] = out
        r.lse[:, q_at] = jnp.broadcast_to(best + jnp.log(total), (8, QB))
        turned = jnp.transpose(jnp.concatenate([out, jnp.zeros_like(out)], axis=0))
        for i in range(QB // tb):
            to = qb * (QB // tb) + i
            r.ostage[to] = pack_rows(turned[i * tb : (i + 1) * tb]).astype(bf16)
            x_out.give(to)
        return carry

    lax.fori_loop(0, seq // QB, attend, 0)
    r.parts[b] = r.ostage[b]
    g_down.forward()
    arrive(got_o)
    x_out.take()
    def gate_slot(n):
        return lambda c: r.wg.at[:, at_block(c, rows), pl.ds(n * 512, 512)]

    g_gate = [Gather(net, gate_slot(n), u, b) for n in range(chunks)]

    half = tb // 2
    got_s = []
    for s in range(seqs):
        for pair in range(heads // 2):
            one = r.parts[s * heads + 2 * pair].astype(f32)
            two = r.parts[s * heads + 2 * pair + 1].astype(f32)
            low_lane = lane_of(one.shape) < HD
            lanes = slice(pair * LANES, (pair + 1) * LANES)
            r.mix[s, :half, lanes] = jnp.where(low_lane, one, swap_halves(two)).astype(bf16)
            r.mix[s, half:, lanes] = jnp.where(low_lane, swap_halves(one), two).astype(bf16)
        r.branch[s] = dot(r.mix[s], r.wo[...]).astype(bf16)
        got_s.append([net.push(r.branch.at[s, part(v)], r.landed.at[u, s], v, b) for v in others])
        r.landed[u, s] = r.branch[s, slab]
    g_down.relay()
    r.sums[...] = jnp.zeros_like(r.sums)
    got_n = []
    for s in range(seqs):
        arrive(got_s[s])
        total = sum(r.landed[v, s].astype(f32) for v in range(n_u))
        own = r.x[s].astype(f32)
        hid = own + total
        r.hidden[s] = hid
        factor = lax.rsqrt(jnp.mean(hid * hid, axis=-1, keepdims=True) + epsilon)
        r.nf_own[s] = (hid * factor * r.gain[1:2, :]).astype(bf16)
        got_n.append([net.push(r.nf_own.at[s], r.nf.at[s, slab], v, b) for v in others])
        r.nf[s, slab] = r.nf_own[s]
        r.sums[0:1] = r.sums[0:1] + jnp.sum(own * own, axis=0, keepdims=True)
        r.sums[1:2] = r.sums[1:2] + jnp.sum(total * total, axis=0, keepdims=True)
    arrive(got_go)
    g_down.finish()
    for n in range(2):
        g_gate[n].forward()
        g_gate[n].relay()

    def hidden_units(n, s):
        span, at = slice(n * 256, (n + 1) * 256), n * 512
        gate = dot(r.nf[s], r.wg[:, :, at : at + 256].reshape(width, 256))
        up = dot(r.nf[s], r.wg[:, :, at + 256 : at + 512].reshape(width, 256))
        grad_act = dot_nt(r.gog[s], r.wdg[span])
        sig = 1.0 / (1.0 + jnp.exp(-gate))
        silu = gate * sig
        r.act[s, :, span] = (silu * up).astype(bf16)
        r.dgu[s, :, at : at + 256] = (grad_act * up * sig * (1.0 + gate * (1.0 - sig))).astype(bf16)
        r.dgu[s, :, at + 256 : at + 512] = (grad_act * silu).astype(bf16)

    def grad_gate(n):
        right = r.dgu[:, :, n * 512 : (n + 1) * 512].reshape(tokens, 512)

        def some(v, carry):
            found = dot(r.nft[at_block(v, 256)], right)
            r.wg_buf[n, :, :, v] = found.astype(bf16).reshape(n_z, 2, rows, 512)
            return carry

        lax.fori_loop(0, n_u, some, 0)
        parts = r.wg_buf.at[n]
        return Scatter(
            net, u, b, lambda z, c: parts.at[z, c], r.wg_pair.at[n], r.wg_sum.at[n], r.wg_land.at[n]
        )

    def grad_down(n):
        half_units = ff // 2
        span = slice(n * half_units, (n + 1) * half_units)
        found = dot_tn(r.act[:, :, span].reshape(tokens, half_units), r.gog[...].reshape(tokens, width))
        r.wd_buf[n * (n_z // 2) : (n + 1) * (n_z // 2)] = found.astype(bf16).reshape(
            n_z // 2, 2, ff_rows, width
        )

    got_d, s_gate = [], []
    for n in range(chunks):
        g_gate[n].finish()
        for s in range(seqs):
            if n == 0:
                arrive(got_n[s])
            hidden_units(n, s)
            if n == 0:
                r.nft[:, s * tb : (s + 1) * tb] = jnp.transpose(r.nf[s])
        if n + 2 < chunks:
            g_gate[n + 2].forward()
            g_gate[n + 2].relay()
        if n > 0:
            s_gate[n - 1].middle()
        if n + 1 < chunks:
            s_gate.append(grad_gate(n))
    for s in range(seqs):
        left = r.dgu[s]
        for v in range(n_u):
            r.d_low[s, :, v * 256 : (v + 1) * 256] = dot_nt(left, r.wg[v]).astype(bf16)
        got_d.append([net.push(r.d_low.at[s, part(v)], r.landed.at[u, s], v, b) for v in others])
        r.landed[u, s] = r.d_low[s, slab]
    s_gate.append(grad_gate(chunks - 1))

    got_b = []

    def norm_back(s):
        arrive(got_d[s])
        grad_normed = sum(r.landed[v, s].astype(f32) for v in range(n_u))
        hid = r.hidden[s]
        factor = lax.rsqrt(jnp.mean(hid * hid, axis=-1, keepdims=True) + epsilon)
        hat = hid * factor
        scaled = grad_normed * r.gain[1:2, :]
        inner = jnp.mean(scaled * hat, axis=-1, keepdims=True)
        total = r.go[s].astype(f32) + factor * (scaled - hat * inner)
        r.ghid[s] = total
        r.gb_own[s] = total.astype(bf16)
        got_b.append([net.push(r.gb_own.at[s], r.xg.at[s, slab], v, b) for v in others])
        r.xg[s, slab] = r.gb_own[s]
        r.sums[4:5] = r.sums[4:5] + jnp.sum(grad_normed * hat, axis=0, keepdims=True)

    norm_back(0)
    grad_down(0)
    norm_back(1)
    grad_down(1)
    s_gate[0].merge()
    s_gate[chunks - 1].middle()
    ff_cut = pl.ds(0, ff_own)
    s_down = Scatter(
        net, u, b, lambda z, c: r.wd_buf.at[z, c, ff_cut], r.wd_pair.at[:, ff_cut],
        r.wd_sum.at[:, ff_cut], r.wd_land.at[:, ff_cut],
    )
    s_gate[1].merge()
    x_grad = Exchange(net, r.ostage2, r.grads, u, b, n_b)
    for s in range(seqs):
        arrive(got_b[s])
        for pair in range(heads // 2):
            found = dot_nt(r.xg[s], r.wo[pair * LANES : (pair + 1) * LANES])
            unit = s * heads + 2 * pair
            r.ostage2[unit] = pack_rows(found).astype(bf16)
            r.ostage2[unit + 1] = pack_rows(swap_halves(found)).astype(bf16)
            x_grad.give(unit)
            x_grad.give(unit + 1)
    r.grads[b] = r.ostage2[b]

    for copies in got_s:
        net.sent(copies)

    def forward(s, carry):
        r.branch[s] = dot(r.act[s], r.wdg[...]).astype(bf16)
        return carry

    lax.fori_loop(0, seqs, forward, 0)
    got_f = [net.push(r.branch.at[:, part(v)], r.landed_f.at[u], v, b) for v in others]
    r.landed_f[u] = r.branch[:, slab]
    found = dot_tn(r.mix[...].reshape(tokens, share), r.xg[...].reshape(tokens, width))
    r.wo_buf[...] = found.astype(bf16).reshape(n_z, 2, rows, width)
    s_out = Scatter(net, u, b, lambda z, c: r.wo_buf.at[z, c], r.wo_pair, r.wo_sum, r.wo_land)
    x_grad.take()
    s_gate[2].merge()
    s_out.middle()

    def more(block, carry):
        place = at_block(block, tb)
        g = unpack_rows(r.grads[block].astype(f32))
        g = jnp.where(lane_of(g.shape) < HD, g, 0.0)
        r.grad[place] = g.astype(bf16)
        turned = jnp.transpose(g)
        r.grad_t[:, place] = turned.astype(bf16)
        total = jnp.sum(turned[:HD] * r.heads_t[:, place], axis=0, keepdims=True)
        r.row_dot[:, place] = jnp.broadcast_to(total, (8, tb))
        return carry

    lax.fori_loop(0, n_b, more, 0)
    x_qk.sent()
    x_v.sent()
    x_back = Exchange(net, r.stage, r.returned, u, b, n_b)

    def backward(keys_at, first_key, queries_at, first_query):
        seen = allowed_block(first_key, first_query, r.low[0:1, queries_at], keys_at.size, queries_at.size)
        scores = dot(r.keys[keys_at], r.query_t[:, queries_at])
        probs = jnp.where(seen, jnp.exp(scores - r.lse[0:1, queries_at]), 0.0)
        prob_grad = dot(r.value[keys_at], r.grad_t[:, queries_at])
        score_grad = (probs * (prob_grad - r.row_dot[0:1, queries_at])).astype(bf16)
        r.dv[keys_at] += dot(probs.astype(bf16), r.grad[queries_at])
        r.dk[keys_at] += dot(score_grad, r.query[queries_at])
        r.dq_t[:, queries_at] += dot(r.key_t[:, keys_at], score_grad)

    def finished(block):
        place = at_block(block, tb)
        columns = r.dq_t[:, place] * HD ** (-0.5)
        turned = jnp.transpose(jnp.concatenate([columns, jnp.zeros_like(columns)], axis=0))
        low_lane = lane_of(turned.shape) < HD
        r.stage[block, 0:tb] = jnp.where(low_lane, turned, swap_halves(r.dk[place])).astype(bf16)
        r.stage[block, tb:] = pack_rows(r.dv[place]).astype(bf16)
        x_back.give(block)

    s_out.merge()
    for buffer in (r.dq_t, r.dk, r.dv):
        buffer[...] = jnp.zeros_like(buffer)
    ratio = QB // KB

    @pl.when(b >= n_b // 2)
    def _():
        def outer(kb, carry):
            def inner(qb, carry):
                backward(at_block(kb, KB), kb * KB, at_block(qb, QB), qb * QB)
                return carry

            lax.fori_loop(kb // ratio, seq // QB, inner, 0)
            finished(kb)
            return carry

        lax.fori_loop(0, n_b, outer, 0)

    @pl.when(b < n_b // 2)
    def _():
        def outer(step, carry):
            qb = n_b - 1 - step

            def inner(kb, carry):
                backward(at_block(kb, QB), kb * QB, at_block(qb, KB), qb * KB)
                return carry

            lax.fori_loop(0, qb // ratio + 1, inner, 0)
            finished(qb)
            return carry

        lax.fori_loop(0, n_b, outer, 0)

    s_down.middle()
    r.returned[b] = r.stage[b]
    arrive(got_f)
    for s in range(seqs):
        total = r.hidden[s] + sum(r.landed_f[v, s].astype(f32) for v in range(n_u))
        r.out[s] = total.astype(bf16)
        r.sums[2:3] = r.sums[2:3] + jnp.sum(total * total, axis=0, keepdims=True)
    x_back.take()

    for s in range(seqs):
        for pair in range(heads // 2):
            unit = s * heads + 2 * pair
            one, two = r.returned[unit, 0:tb].astype(f32), r.returned[unit + 1, 0:tb].astype(f32)
            low_lane = lane_of(one.shape) < HD
            grads = (
                jnp.where(low_lane, one, swap_halves(two)),
                jnp.where(low_lane, swap_halves(one), two),
            )
            for i, tile in enumerate(grads):
                turned = tile * r.cosr[s] - partner(tile) * r.sinr[s]
                at = i * share + pair * LANES
                r.raw[s, :, at : at + LANES] = turned.astype(bf16)
            one = unpack_rows(r.returned[unit, tb:].astype(f32))
            two = unpack_rows(r.returned[unit + 1, tb:].astype(f32))
            both = 0.5 * jnp.where(low_lane, one, swap_halves(two))
            at = 2 * share + pair * LANES
            r.raw[s, :, at : at + LANES] = both.astype(bf16)
    columns = r.raw.shape[2]
    for v in range(n_u):
        left = r.normed[:, :, v * 256 : (v + 1) * 256].reshape(tokens, 256)
        found = dot_tn(left, r.raw[...].reshape(tokens, columns))
        r.wq_buf[:, :, v] = found.astype(bf16).reshape(n_z, 2, rows, columns)
    s_qkv = Scatter(net, u, b, lambda z, c: r.wq_buf.at[z, c], r.wq_pair, r.wq_sum, r.wq_land)
    s_down.merge()

    for copies in got_d:
        net.sent(copies)
    got_g = []
    for s in range(seqs):
        left = r.raw[s]
        for v in range(n_u):
            lanes = slice(v * 256, (v + 1) * 256)
            found = dot_nt(left, r.wq[v])
            r.d_low[s, :, lanes] = found.astype(bf16)
            term = jnp.sum(found * r.hat[s, :, lanes].astype(f32), axis=0, keepdims=True)
            r.sums[3:4, lanes] = r.sums[3:4, lanes] + term
        got_g.append([net.push(r.d_low.at[s, part(v)], r.landed.at[u, s], v, b) for v in others])
        r.landed[u, s] = r.d_low[s, slab]
    got_s = [net.push(r.sums, r.sums_u.at[u], v, b) for v in others]
    r.sums_u[u] = r.sums[...]
    s_qkv.middle()
    got_v = [net.push(r.raw.at[:, part(v), pl.ds(2 * share, share)], r.gv.at[u], v, b) for v in others]
    r.gv[u] = r.raw[:, slab, 2 * share :]
    got_c = []
    for n in range(chunks):
        s_gate[n].finish(r.wg_low.at[n])
        got_c += [net.push(r.wg_low.at[n, v], r.dwgu.at[n, u], v, b) for v in others]
        r.dwgu[n, u] = r.wg_low[n, u]
    s_qkv.merge()
    s_out.finish(r.gwo)
    s_down.finish(r.gwd)
    arrive(got_s)
    r.sums_b[b] = sum(r.sums_u[v] for v in range(n_u))
    got_s = [net.push(r.sums_b.at[b], r.sums_b.at[b], u, b ^ off) for off in range(1, n_b)]
    for s in range(seqs):
        arrive(got_g[s])
        grad_normed = sum(r.landed[v, s].astype(f32) for v in range(n_u))
        own = r.x[s].astype(f32)
        factor = lax.rsqrt(jnp.mean(own * own, axis=-1, keepdims=True) + epsilon)
        hat = own * factor
        scaled = grad_normed * r.gain[0:1, :]
        inner = jnp.mean(scaled * hat, axis=-1, keepdims=True)
        r.gin[s] = (r.ghid[s] + factor * (scaled - hat * inner)).astype(bf16)
    arrive(got_v)
    for v in range(n_u):
        r.gvf[:, :, v * 256 : (v + 1) * 256] = r.gv[v]
    arrive(got_s)
    totals = sum(r.sums_b[c] for c in range(n_b))
    squares = jnp.sum(totals, axis=1, keepdims=True) / (seqs * seq * width)
    r.totals[...] = totals
    roots = jnp.sqrt(squares)
    lane = lane_of((1, LANES))
    r.stats[...] = jnp.where(lane == 0, roots[0:1], jnp.where(lane == 1, roots[1:2], roots[2:3]))[0, 0:3]
    per = LANES // rows
    tile = r.totals[:, at_block(u * (n_b // per) + b // per, LANES)]
    tile = pltpu.roll(tile, (LANES - lane_place) % LANES, 1)
    r.gga[...] = tile[3, 0:rows]
    r.ggf[...] = tile[4, 0:rows]
    s_qkv.finish(r.wq_low)
    got = [net.push(r.wq_low.at[v], r.dwq.at[u], v, b) for v in others]
    r.dwq[u] = r.wq_low[u]
    arrive(got_c)
    for i, to in enumerate((r.gwg, r.gwu)):
        pieces = []
        for v in range(n_u):
            row = jnp.concatenate(
                [r.dwgu[n, v, :, i * 256 : (i + 1) * 256] for n in range(chunks)], axis=1
            ).astype(f32)
            pieces += [row[:, j * ff_rows : j * ff_rows + ff_own] for j in range(n_b)]
        to[...] = jnp.concatenate(pieces, axis=1)
    arrive(got)
    for i, to in enumerate((r.gwq, r.gwk, r.gwv)):
        for v in range(n_u):
            to[:, v * share : (v + 1) * share] = r.dwq[v, :, i * share : (i + 1) * share].astype(f32)
    for exchange in (x_out, x_grad, x_back):
        exchange.sent()
    net.drain()


def hand_out_kernel(count, *refs):
    for given, taken in zip(refs[:count], refs[count:]):
        taken[...] = given[...]


def local_units(
    inputs, v_first, grad_out, positions, segments,
    w_query, w_key, w_value, w_out, w_gate, w_up, w_down, gain_attn, gain_ffn,
):
    n_u, n_b = lax.axis_size("ulysses"), lax.axis_size("blk")
    seqs, td, width = inputs.shape
    rows = w_query.shape[0]
    heads = HEADS // n_u
    tb = n_u * td
    seq = n_b * tb
    ff_own = w_down.shape[0]
    ff_pad = -(-ff_own // 32) * 32
    ff = ff_pad * n_b
    chunks = ff // 256
    dims = (n_u, n_b, seqs, td, rows, heads)

    columns = 3 * heads * HD
    n_z = n_b // 2
    own, block = (seqs, td, width), (seqs, tb, width)
    inputs_of = dict(
        x=inputs, vf=v_first, go=grad_out, segments=segments, wq_in=w_query, wk_in=w_key, wv_in=w_value,
        wout=w_out, wg_in=w_gate, wu_in=w_up, wd=w_down, ga=gain_attn, gf=gain_ffn,
    )
    outs = dict(
        out=(own, bf16), gin=(own, bf16), gvf=(own, bf16), gwq=((rows, width), f32), gwk=((rows, width), f32),
        gwv=((rows, width), f32), gwo=((rows, width), f32), gwg=(w_gate.shape, f32), gwu=(w_gate.shape, f32),
        gwd=((ff_own, width), f32), gga=((rows,), f32), ggf=((rows,), f32), stats=((3,), f32),
    )
    scratch = dict(
        gains=((8, LANES), f32), wgu=((n_u, rows, 2 * ff), bf16), cosr=((seqs, tb, LANES), f32),
        sinr=((seqs, tb, LANES), f32), low=((8, seq), jnp.int32),
        dwq=((n_u, rows, columns), bf16), dwgu=((chunks, n_u, rows, 512), bf16), nft=((width, seqs * tb), bf16),
        xg=(block, bf16), vfg=((seqs, tb, heads * HD), bf16), gbuf=((n_b, n_u, 8, LANES), f32),
        gain=((8, width), f32), normed=(block, bf16), wq=((n_u, n_b * rows, columns), bf16),
        gog=(block, bf16), wg=((n_u, n_b * rows, 2 * ff), bf16), wdg=((ff, width), bf16),
        wo=((n_b * rows, width), bf16), stage=((n_b, tb + tb // 2, LANES), bf16),
        units=((n_b, tb + tb // 2, LANES), bf16), keys=((seq, LANES), bf16), key_t=((HD, seq), bf16),
        query=((seq, LANES), bf16), query_t=((LANES, seq), bf16), value=((seq, LANES), bf16),
        value_t=((HD, seq), bf16), acc=((HD, QB), f32), heads_t=((HD, seq), f32), lse=((8, seq), f32),
        ostage=((n_b, tb // 2, LANES), bf16), parts=((n_b, tb // 2, LANES), bf16),
        mix=((seqs, tb, heads * HD), bf16), branch=(block, bf16), landed=((n_u,) + own, bf16),
        sums=((8, width), f32), totals=((8, width), f32), hat=(block, bf16), hidden=(own, f32), nf_own=(own, bf16), nf=(block, bf16),
        act=((seqs, tb, ff), bf16), dgu=((seqs, tb, 2 * ff), bf16), d_low=(block, bf16),
        ghid=(own, f32), gb_own=(own, bf16),
        landed_f=((n_u,) + own, bf16),
        wd_buf=((n_z, 2, ff_pad, width), bf16), wd_pair=((n_z, ff_pad, width), bf16),
        wd_sum=((n_z, ff_pad, width), bf16), wd_land=((n_z, ff_pad, width), bf16),
        wg_buf=((chunks, n_z, 2, n_u, rows, 512), bf16), wg_pair=((chunks, n_z, n_u, rows, 512), bf16),
        wg_sum=((chunks, n_z, n_u, rows, 512), bf16), wg_land=((chunks, n_z, n_u, rows, 512), bf16),
        wg_low=((chunks, n_u, rows, 512), bf16),
        ostage2=((n_b, tb // 2, LANES), bf16), grads=((n_b, tb // 2, LANES), bf16),
        wo_buf=((n_z, 2, rows, width), bf16), wo_pair=((n_z, rows, width), bf16),
        wo_sum=((n_z, rows, width), bf16), wo_land=((n_z, rows, width), bf16),
        grad=((seq, LANES), bf16), grad_t=((LANES, seq), bf16), row_dot=((8, seq), f32),
        dq_t=((HD, seq), f32), dk=((seq, LANES), f32), dv=((seq, LANES), f32),
        returned=((n_b, tb + tb // 2, LANES), bf16), raw=((seqs, tb, columns), bf16),
        gv=((n_u, seqs, td, heads * HD), bf16),
        wq_buf=((n_z, 2, n_u, rows, columns), bf16), wq_pair=((n_z, n_u, rows, columns), bf16),
        wq_sum=((n_z, n_u, rows, columns), bf16), wq_land=((n_z, n_u, rows, columns), bf16),
        wq_low=((n_u, rows, columns), bf16), sums_u=((n_u, 8, width), f32), sums_b=((n_b, 8, width), f32),
    )
    names = [*inputs_of, *outs, *scratch, "send_sems", "recv_sems"]
    vmem = pl.BlockSpec(memory_space=pltpu.VMEM)
    results = pl.pallas_call(
        functools.partial(layer_kernel, dims, names),
        out_shape=[jax.ShapeDtypeStruct(shape, dtype) for shape, dtype in outs.values()],
        in_specs=[vmem] * len(inputs_of),
        out_specs=[vmem] * len(outs),
        scratch_shapes=[pltpu.VMEM(shape, dtype) for shape, dtype in scratch.values()]
        + [pltpu.SemaphoreType.DMA((SEMAPHORES,))] * 2,
        compiler_params=pltpu.CompilerParams(
            collective_id=1, has_side_effects=True, vmem_limit_bytes=VMEM_BYTES
        ),
        name="layer",
    )(*inputs_of.values())
    return pl.pallas_call(
        functools.partial(hand_out_kernel, len(outs)),
        out_shape=[jax.ShapeDtypeStruct(shape, dtype) for shape, dtype in outs.values()],
        in_specs=[vmem] * len(outs),
        out_specs=[vmem] * len(outs),
        name="hand_out",
    )(*results)


SEMAPHORES = 288


def fits_units(mesh):
    return mesh.shape["ulysses"] == 4 and mesh.shape["blk"] == 8


def solution(mesh):
    in_specs = (
        P(None, ("blk", "ulysses"), None),
        P(None, ("blk", "ulysses"), None),
        P(None, ("blk", "ulysses"), None),
        P(None, ("blk", "ulysses")),
        P(),
        P(("ulysses", "blk"), None),
        P(("ulysses", "blk"), None),
        P(("ulysses", "blk"), None),
        P(("ulysses", "blk"), None),
        P(("ulysses", "blk"), None),
        P(("ulysses", "blk"), None),
        P(("ulysses", "blk"), None),
        P(("ulysses", "blk")),
        P(("ulysses", "blk")),
    )
    out_specs = (
        P(None, ("blk", "ulysses"), None),
        P(None, ("blk", "ulysses"), None),
        P(None, ("blk", "ulysses"), None),
        P(("ulysses", "blk"), None),
        P(("ulysses", "blk"), None),
        P(("ulysses", "blk"), None),
        P(("ulysses", "blk"), None),
        P(("ulysses", "blk"), None),
        P(("ulysses", "blk"), None),
        P(("ulysses", "blk"), None),
        P(("ulysses", "blk")),
        P(("ulysses", "blk")),
        P(),
    )
    path = local_units if fits_units(mesh) else local
    return jax.shard_map(path, mesh=mesh, in_specs=in_specs, out_specs=out_specs, check_vma=False)
```

```python
import functools
import types

import jax
import jax.numpy as jnp
import numpy as np
from jax import lax
from jax.experimental import pallas as pl
from jax.experimental.pallas import tpu as pltpu
from jax.sharding import PartitionSpec as P

HEADS = 16
HD = 64


epsilon = 1e-06
rope_base = 10000.0
neg_big = -1e30


def norm_rows(values, gain):
    factor = lax.rsqrt(jnp.mean(values * values, axis=-1, keepdims=True) + epsilon)
    hatted = values * factor
    return (hatted * gain, hatted, factor)


def norm_back(grad_normed, hatted, factor, gain):
    scaled = grad_normed * gain
    inner = jnp.mean(scaled * hatted, axis=-1, keepdims=True)
    return (factor * (scaled - hatted * inner), jnp.sum(grad_normed * hatted, axis=(0, 1)))


def rope_tables(positions):
    half_dim = HD // 2
    inverse = rope_base ** (-2.0 * jnp.arange(half_dim, dtype=jnp.float32) / HD)
    angles = positions.astype(jnp.float32)[:, :, None] * inverse
    return (jnp.cos(angles)[:, :, None, :], jnp.sin(angles)[:, :, None, :])


def rotate(values, cosine, sine, forward_turn):
    shaped = values.reshape(values.shape[0], values.shape[1], HEADS, HD)
    half_dim = HD // 2
    first = shaped[..., :half_dim]
    second = shaped[..., half_dim:]
    if forward_turn:
        turned = jnp.concatenate(
            [first * cosine - second * sine, second * cosine + first * sine], axis=-1
        )
    else:
        turned = jnp.concatenate(
            [first * cosine + second * sine, second * cosine - first * sine], axis=-1
        )
    return turned.reshape(values.shape)


def project(activations, weight):
    return jnp.einsum("std,de->ste", activations, weight, preferred_element_type=jnp.float32)


def project_back(gradient, weight):
    return jnp.einsum("ste,de->std", gradient, weight, preferred_element_type=jnp.float32)


def weight_grad(activations, gradient):
    return jnp.einsum("std,ste->de", activations, gradient, preferred_element_type=jnp.float32)


def allowed_mask(segments, query_first, query_count, key_first, key_count):
    seg_query = lax.dynamic_slice_in_dim(segments, query_first, query_count, 1)
    seg_key = lax.dynamic_slice_in_dim(segments, key_first, key_count, 1)
    query_place = query_first + jnp.arange(query_count, dtype=jnp.int32)
    key_place = key_first + jnp.arange(key_count, dtype=jnp.int32)
    causal = key_place[None, :] <= query_place[:, None]
    same_doc = seg_query[:, :, None] == seg_key[:, None, :]
    return (causal[None] & same_doc)[:, :, None, :]


def over_blocks(step_fn, running, pieces, block_rows):
    row_count = pieces[0].shape[1]
    block_count = row_count // block_rows
    stacked = tuple(
        (
            jnp.moveaxis(
                member.reshape((member.shape[0], block_count, block_rows) + member.shape[2:]), 1, 0
            )
            for member in pieces
        )
    )
    offsets = block_rows * jnp.arange(block_count, dtype=jnp.int32)

    def advance(current, scan_entry):
        return (step_fn(current, scan_entry[:-1], scan_entry[-1]), None)

    running, unused = lax.scan(advance, running, stacked + (offsets,))
    return running


def add_rows(buffer, update, first_row):
    current = lax.dynamic_slice_in_dim(buffer, first_row, update.shape[1], 1)
    return lax.dynamic_update_slice_in_dim(buffer, current + update, first_row, 1)


def unchanged(running):
    return running


def local(
    inputs,
    v_first,
    grad_out,
    positions,
    segments,
    w_query,
    w_key,
    w_value,
    w_out,
    w_gate,
    w_up,
    w_down,
    gain_attn,
    gain_ffn,
):
    gathered = (
        lax.all_gather(w_query, ("ulysses", "blk"), axis=0, tiled=True),
        lax.all_gather(w_key, ("ulysses", "blk"), axis=0, tiled=True),
        lax.all_gather(w_value, ("ulysses", "blk"), axis=0, tiled=True),
        lax.all_gather(w_out, ("ulysses", "blk"), axis=0, tiled=True),
        lax.all_gather(w_gate, ("ulysses", "blk"), axis=0, tiled=True),
        lax.all_gather(w_up, ("ulysses", "blk"), axis=0, tiled=True),
        lax.all_gather(w_down, ("ulysses", "blk"), axis=0, tiled=True),
        lax.all_gather(gain_attn, ("ulysses", "blk"), axis=0, tiled=True),
        lax.all_gather(gain_ffn, ("ulysses", "blk"), axis=0, tiled=True),
    )
    (
        full_query,
        full_key,
        full_value,
        full_out,
        full_gate,
        full_up,
        full_down,
        full_gain_attn,
        full_gain_ffn,
    ) = gathered
    score_scale = HD ** (-0.5)
    residual = inputs.astype(jnp.float32)
    normed_f, hatted_attn, factor_attn = norm_rows(residual, full_gain_attn.astype(jnp.float32))
    normed = normed_f.astype(jnp.bfloat16)
    cosine, sine = rope_tables(positions)
    query_tok = rotate(project(normed, full_query), cosine, sine, True).astype(jnp.bfloat16)
    key_tok = rotate(project(normed, full_key), cosine, sine, True).astype(jnp.bfloat16)
    value_tok = (0.5 * project(normed, full_value) + 0.5 * v_first.astype(jnp.float32)).astype(
        jnp.bfloat16
    )
    query_head, key_head, value_head = (
        lax.all_to_all(query_tok, "ulysses", split_axis=2, concat_axis=1, tiled=True),
        lax.all_to_all(key_tok, "ulysses", split_axis=2, concat_axis=1, tiled=True),
        lax.all_to_all(value_tok, "ulysses", split_axis=2, concat_axis=1, tiled=True),
    )
    seq_count, block_rows, width = query_head.shape
    heads_local = width // HD
    query_start = lax.axis_index("blk") * block_rows
    full_rows = block_rows * lax.axis_size("blk")

    def split_heads(values):
        return values.reshape(values.shape[0], values.shape[1], heads_local, HD)

    query_four = split_heads(query_head)

    def attend_rows(running, pieces, first_row):
        key_rows, value_rows = pieces
        key_count = key_rows.shape[1]

        def attend_compute(current):
            best, total, accum = current
            allowed = allowed_mask(segments, query_start, block_rows, first_row, key_count)
            scores = (
                jnp.einsum(
                    "sqhd,skhd->sqhk",
                    query_four,
                    split_heads(key_rows),
                    preferred_element_type=jnp.float32,
                )
                * score_scale
            )
            masked = jnp.where(allowed, scores, neg_big)
            new_best = jnp.maximum(best, jnp.max(masked, axis=-1))
            weights = jnp.where(allowed, jnp.exp(masked - new_best[..., None]), 0.0)
            rescale = jnp.exp(best - new_best)
            total = total * rescale + jnp.sum(weights, axis=-1)
            accum = accum * rescale[..., None] + jnp.einsum(
                "sqhk,skhd->sqhd",
                weights.astype(jnp.bfloat16),
                split_heads(value_rows),
                preferred_element_type=jnp.float32,
            )
            return (new_best, total, accum)

        return lax.cond(
            first_row <= query_start + block_rows - 1, attend_compute, unchanged, running
        )

    stat_zeros = jnp.zeros((seq_count, block_rows, heads_local), jnp.float32)
    head_zeros = jnp.zeros((seq_count, block_rows, heads_local, HD), jnp.float32)
    initial = (
        jnp.full((seq_count, block_rows, heads_local), neg_big, jnp.float32),
        stat_zeros,
        head_zeros,
    )
    best, total, accum = over_blocks(
        attend_rows,
        initial,
        (
            lax.all_gather(key_head, "blk", axis=1, tiled=True),
            lax.all_gather(value_head, "blk", axis=1, tiled=True),
        ),
        block_rows,
    )
    log_total = best + jnp.log(total)
    attn_heads = accum / total[..., None]
    attn_low = attn_heads.reshape(seq_count, block_rows, width).astype(jnp.bfloat16)
    mixed = lax.all_to_all(attn_low, "ulysses", split_axis=1, concat_axis=2, tiled=True)
    attn_branch = project(mixed, full_out)
    hidden = residual + attn_branch
    normed_ffn_f, hatted_ffn, factor_ffn = norm_rows(hidden, full_gain_ffn.astype(jnp.float32))
    normed_ffn = normed_ffn_f.astype(jnp.bfloat16)
    gate = project(normed_ffn, full_gate)
    up_proj = project(normed_ffn, full_up)
    sigmoid_gate = jax.nn.sigmoid(gate)
    silu_gate = gate * sigmoid_gate
    act = (silu_gate * up_proj).astype(jnp.bfloat16)
    ffn_branch = project(act, full_down)
    output_f = hidden + ffn_branch
    output = output_f.astype(jnp.bfloat16)
    squares = lax.psum(
        (
            jnp.sum(residual * residual),
            jnp.sum(attn_branch * attn_branch),
            jnp.sum(output_f * output_f),
        ),
        ("ulysses", "blk"),
    )
    entry_count = residual.size * lax.axis_size("ulysses") * lax.axis_size("blk")
    statistics = jnp.sqrt(jnp.stack(squares) / entry_count)
    again = (
        lax.all_gather(w_query, ("ulysses", "blk"), axis=0, tiled=True),
        lax.all_gather(w_key, ("ulysses", "blk"), axis=0, tiled=True),
        lax.all_gather(w_value, ("ulysses", "blk"), axis=0, tiled=True),
        lax.all_gather(w_out, ("ulysses", "blk"), axis=0, tiled=True),
        lax.all_gather(w_gate, ("ulysses", "blk"), axis=0, tiled=True),
        lax.all_gather(w_up, ("ulysses", "blk"), axis=0, tiled=True),
        lax.all_gather(w_down, ("ulysses", "blk"), axis=0, tiled=True),
        lax.all_gather(gain_attn, ("ulysses", "blk"), axis=0, tiled=True),
        lax.all_gather(gain_ffn, ("ulysses", "blk"), axis=0, tiled=True),
    )
    (
        back_query,
        back_key,
        back_value,
        back_out,
        back_gate,
        back_up,
        back_down,
        back_gain_attn,
        back_gain_ffn,
    ) = again
    grad_act = project_back(grad_out, back_down)
    grad_gate = (grad_act * up_proj * sigmoid_gate * (1.0 + gate * (1.0 - sigmoid_gate))).astype(
        jnp.bfloat16
    )
    grad_up = (grad_act * silu_gate).astype(jnp.bfloat16)
    grad_normed_ffn = project_back(grad_gate, back_gate) + project_back(grad_up, back_up)
    grad_ffn_norm, grad_gain_ffn = norm_back(
        grad_normed_ffn, hatted_ffn, factor_ffn, back_gain_ffn.astype(jnp.float32)
    )
    grad_hidden = grad_out.astype(jnp.float32) + grad_ffn_norm
    grad_branch = grad_hidden.astype(jnp.bfloat16)
    grad_mixed = project_back(grad_branch, back_out).astype(jnp.bfloat16)
    dout_head = lax.all_to_all(grad_mixed, "ulysses", split_axis=2, concat_axis=1, tiled=True)
    dout_four = split_heads(dout_head)
    row_dot = jnp.sum(dout_four.astype(jnp.float32) * attn_heads, axis=-1)

    def grad_rows(running, pieces, first_row):
        key_rows, value_rows = pieces
        key_count = key_rows.shape[1]

        def grad_compute(current):
            grad_query, grad_keys, grad_values = current
            key_part = split_heads(key_rows)
            allowed = allowed_mask(segments, query_start, block_rows, first_row, key_count)
            scores = (
                jnp.einsum(
                    "sqhd,skhd->sqhk", query_four, key_part, preferred_element_type=jnp.float32
                )
                * score_scale
            )
            probs = jnp.where(allowed, jnp.exp(scores - log_total[..., None]), 0.0)
            prob_grad = jnp.einsum(
                "sqhd,skhd->sqhk",
                dout_four,
                split_heads(value_rows),
                preferred_element_type=jnp.float32,
            )
            score_grad = (probs * (prob_grad - row_dot[..., None])).astype(jnp.bfloat16)
            grad_query = (
                grad_query
                + jnp.einsum(
                    "sqhk,skhd->sqhd", score_grad, key_part, preferred_element_type=jnp.float32
                )
                * score_scale
            )
            key_term = (
                jnp.einsum(
                    "sqhk,sqhd->skhd", score_grad, query_four, preferred_element_type=jnp.float32
                )
                * score_scale
            )
            value_term = jnp.einsum(
                "sqhk,sqhd->skhd",
                probs.astype(jnp.bfloat16),
                dout_four,
                preferred_element_type=jnp.float32,
            )
            return (
                grad_query,
                add_rows(grad_keys, key_term, first_row),
                add_rows(grad_values, value_term, first_row),
            )

        return lax.cond(first_row <= query_start + block_rows - 1, grad_compute, unchanged, running)

    full_zeros = jnp.zeros((seq_count, full_rows, heads_local, HD), jnp.float32)
    grad_query_own, grad_keys_all, grad_values_all = over_blocks(
        grad_rows,
        (head_zeros, full_zeros, full_zeros),
        (
            lax.all_gather(key_head, "blk", axis=1, tiled=True),
            lax.all_gather(value_head, "blk", axis=1, tiled=True),
        ),
        block_rows,
    )
    grad_key_own, grad_value_own = (
        lax.psum_scatter(
            grad_keys_all.reshape(seq_count, full_rows, width).astype(jnp.bfloat16),
            "blk",
            scatter_dimension=1,
            tiled=True,
        ).astype(jnp.float32),
        lax.psum_scatter(
            grad_values_all.reshape(seq_count, full_rows, width).astype(jnp.bfloat16),
            "blk",
            scatter_dimension=1,
            tiled=True,
        ).astype(jnp.float32),
    )
    grad_query_own = grad_query_own.reshape(seq_count, block_rows, width)
    grad_query_tok, grad_key_tok, grad_value_tok = (
        lax.all_to_all(
            grad_query_own.astype(jnp.bfloat16), "ulysses", split_axis=1, concat_axis=2, tiled=True
        ),
        lax.all_to_all(
            grad_key_own.astype(jnp.bfloat16), "ulysses", split_axis=1, concat_axis=2, tiled=True
        ),
        lax.all_to_all(
            grad_value_own.astype(jnp.bfloat16), "ulysses", split_axis=1, concat_axis=2, tiled=True
        ),
    )
    grad_query_raw = rotate(grad_query_tok.astype(jnp.float32), cosine, sine, False).astype(
        jnp.bfloat16
    )
    grad_key_raw = rotate(grad_key_tok.astype(jnp.float32), cosine, sine, False).astype(
        jnp.bfloat16
    )
    grad_v_first = grad_value_tok * 0.5
    grad_normed = (
        project_back(grad_query_raw, back_query)
        + project_back(grad_key_raw, back_key)
        + project_back(grad_v_first, back_value)
    )
    grad_attn_norm, grad_gain_attn = norm_back(
        grad_normed, hatted_attn, factor_attn, back_gain_attn.astype(jnp.float32)
    )
    grad_inputs = (grad_hidden + grad_attn_norm).astype(jnp.bfloat16)
    model_width = w_query.shape[1]
    hidden_width = w_gate.shape[1]
    owned = lax.psum_scatter(
        jnp.concatenate(
            [
                weight_grad(normed, grad_query_raw),
                weight_grad(normed, grad_key_raw),
                weight_grad(normed, grad_v_first),
                weight_grad(mixed, grad_branch),
                weight_grad(normed_ffn, grad_gate),
                weight_grad(normed_ffn, grad_up),
                grad_gain_attn[:, None],
                grad_gain_ffn[:, None],
            ],
            axis=1,
        ),
        ("ulysses", "blk"),
        scatter_dimension=0,
        tiled=True,
    )
    grad_w_down = lax.psum_scatter(
        weight_grad(act, grad_out), ("ulysses", "blk"), scatter_dimension=0, tiled=True
    )
    column = 0
    pieces = []
    for span in (model_width, model_width, model_width, model_width, hidden_width, hidden_width):
        pieces.append(owned[:, column : column + span])
        column = column + span
    grad_gain_attn_own = owned[:, column]
    grad_gain_ffn_own = owned[:, column + 1]
    return (
        output,
        grad_inputs,
        grad_v_first,
        pieces[0],
        pieces[1],
        pieces[2],
        pieces[3],
        pieces[4],
        pieces[5],
        grad_w_down,
        grad_gain_attn_own,
        grad_gain_ffn_own,
        statistics,
    )


MESH = pl.DeviceIdType.MESH
LANES = 128
VMEM_BYTES = 61 << 20
f32 = jnp.float32
bf16 = jnp.bfloat16
QB, KB = 512, 256


class Copy:
    def __init__(self, copy, send_at, recv_at, when):
        self.copy, self.at, self.recv_at, self.when = copy, send_at, recv_at, when

    def wait_recv(self):
        self.copy.wait_recv()

    def wait_send(self):
        if self.when is None:
            self.copy.wait_send()
        else:
            pl.when(self.when)(self.copy.wait_send)


class Net:
    def __init__(self, send_sems, recv_sems):
        self.send_sems, self.recv_sems = send_sems, recv_sems
        self.count, self.open = 0, []

    def push(self, src, dst, u, b, when=None, recv_at=None, at=None):
        if at is None:
            at = self.count
            self.count += 1
        recv_at = at if recv_at is None else recv_at
        copy = pltpu.make_async_remote_copy(
            src_ref=src,
            dst_ref=dst,
            send_sem=self.send_sems.at[at],
            recv_sem=self.recv_sems.at[recv_at],
            device_id=(u, b),
            device_id_type=MESH,
        )
        if when is None:
            copy.start()
        else:
            pl.when(when)(copy.start)
        made = Copy(copy, at, recv_at, when)
        self.open.append(made)
        return made

    def sent(self, copies):
        for copy in copies:
            copy.wait_send()
        self.open = [copy for copy in self.open if copy not in copies]

    def drain(self):
        for copy in self.open:
            copy.wait_send()
        self.open = []


def arrive(copies):
    for copy in copies:
        copy.wait_recv()


def here():
    return lax.axis_index("ulysses"), lax.axis_index("blk")


def greet(u, b, n_u, n_b):
    barrier = pltpu.get_barrier_semaphore()
    for off in range(1, n_u):
        pl.semaphore_signal(barrier, inc=1, device_id=(u ^ off, b), device_id_type=MESH)
    for off in range(1, n_b):
        pl.semaphore_signal(barrier, inc=1, device_id=(u, b ^ off), device_id_type=MESH)
    pl.semaphore_wait(barrier, n_u - 1 + n_b - 1)


def dot(left, right):
    return jnp.dot(left, right, preferred_element_type=f32)


def dot_nt(left, right):
    return lax.dot_general(left, right, (((1,), (1,)), ((), ())), preferred_element_type=f32)


def dot_tn(left, right):
    return lax.dot_general(left, right, (((0,), (0,)), ((), ())), preferred_element_type=f32)


def at_block(index, size):
    return pl.ds(pl.multiple_of(index * size, size), size)


def lane_of(shape):
    return lax.broadcasted_iota(jnp.int32, shape, len(shape) - 1)


def swap_halves(tile):
    return pltpu.roll(tile, HD, tile.ndim - 1)


def partner(tile):
    low = lane_of(tile.shape) % HD < HD // 2
    return jnp.where(low, pltpu.roll(tile, LANES - HD // 2, 1), pltpu.roll(tile, HD // 2, 1))


def pack_rows(rows):
    half = rows.shape[0] // 2
    low = lane_of((half, LANES)) < HD
    return jnp.where(low, rows[:half], swap_halves(rows[half:]))


def unpack_rows(packed):
    return jnp.concatenate([packed, swap_halves(packed)], axis=0)


class Exchange:
    def __init__(self, net, staged, landed, u, b, n_b):
        self.net, self.staged, self.landed, self.u, self.b, self.n_b = net, staged, landed, u, b, n_b
        self.at = net.count
        net.count += n_b

    def copy(self, to, slot_from):
        return pltpu.make_async_remote_copy(
            src_ref=self.staged.at[to],
            dst_ref=self.landed.at[slot_from],
            send_sem=self.net.send_sems.at[self.at + to],
            recv_sem=self.net.recv_sems.at[self.at + slot_from],
            device_id=(self.u, to),
            device_id_type=MESH,
        )

    def give(self, to):
        @pl.when(to != self.b)
        def _():
            self.copy(to, self.b).start()

    def take(self):
        for off in range(1, self.n_b):
            self.copy(self.b ^ off, self.b ^ off).wait_recv()

    def sent(self):
        for off in range(1, self.n_b):
            self.copy(self.b ^ off, self.b).wait_send()


class Gather:
    def __init__(self, net, slot, u, b):
        self.net, self.slot, self.u, self.b = net, slot, u, b
        self.inner = ((b // 2) == 1) | ((b // 2) == 2)
        mine = slot(b)
        self.two = net.push(mine, mine, u, b ^ 4)
        self.one = net.push(mine, mine, u, b ^ 2)
        self.three = net.push(mine, mine, u, b ^ 6, when=self.inner)
        self.side = [net.push(mine, mine, u, b ^ 1)]

    def beside(self, owner):
        got = self.slot(owner)
        self.side.append(self.net.push(got, got, self.u, self.b ^ 1))

    def forward(self):
        self.two.wait_recv()
        got = self.slot(self.b ^ 4)
        self.net.push(got, got, self.u, self.b ^ 2, when=self.inner, recv_at=self.three.at)
        self.beside(self.b ^ 4)

    def relay(self):
        self.one.wait_recv()
        self.beside(self.b ^ 2)
        self.three.wait_recv()
        self.beside(self.b ^ 6)

    def finish(self):
        arrive(self.side)


class Scatter:
    def __init__(self, net, u, b, mine, paired, summed, landed):
        self.net, self.u, self.b = net, u, b
        self.mine, self.paired, self.summed, self.landed = mine, paired, summed, landed
        self.z = b // 2
        self.inner = (self.z == 1) | (self.z == 2)
        self.swap = [net.push(mine(z, 1 - b % 2), paired.at[z], u, b ^ 1) for z in range(4)]

    def add(self, z):
        self.summed[z] = (self.mine(z, self.b % 2)[...].astype(f32) + self.paired[z].astype(f32)).astype(bf16)

    def middle(self):
        net, u, b, z, inner = self.net, self.u, self.b, self.z, self.inner
        outer = jnp.logical_not(inner)
        arrive(self.swap)
        self.add(z ^ 3)
        far = self.summed.at[z ^ 3]
        self.extra = net.push(far, self.landed.at[3], u, b ^ 2, when=outer)
        self.three = net.push(far, self.landed.at[2], u, b ^ 6, when=inner)
        self.add(z ^ 2)
        self.two = net.push(self.summed.at[z ^ 2], self.landed.at[1], u, b ^ 4, when=outer)
        self.add(z ^ 1)
        self.one = net.push(self.summed.at[z ^ 1], self.landed.at[0], u, b ^ 2)
        self.add(z)

    def merge(self):
        net, u, b, z = self.net, self.u, self.b, self.z

        @pl.when(self.inner)
        def _():
            self.extra.wait_recv()
            self.summed[z ^ 2] = (self.summed[z ^ 2].astype(f32) + self.landed[3].astype(f32)).astype(bf16)

        net.push(self.summed.at[z ^ 2], self.landed.at[1], u, b ^ 4, when=self.inner, at=self.two.at)

    def finish(self, total):
        self.one.wait_recv()
        self.two.wait_recv()
        total[...] = (
            self.summed[self.z].astype(f32) + self.landed[0].astype(f32) + self.landed[1].astype(f32)
        ).astype(total.dtype)

        @pl.when(self.inner)
        def _():
            self.three.wait_recv()
            total[...] = (total[...].astype(f32) + self.landed[2].astype(f32)).astype(total.dtype)


def allowed_block(first_key, first_query, low_row, keys=KB, queries=QB):
    key_place = first_key + lax.broadcasted_iota(jnp.int32, (keys, queries), 0)
    query_place = first_query + lax.broadcasted_iota(jnp.int32, (keys, queries), 1)
    return (key_place <= query_place) & (key_place >= low_row)


def widen(rows, size, padded):
    zeros = jnp.zeros((rows.shape[0], padded - size), rows.dtype)
    pieces = []
    for at in range(0, rows.shape[1], size):
        pieces += [rows[:, at : at + size], zeros]
    return jnp.concatenate(pieces, axis=1)


def rope_rows(base, cut, count):
    place = base + lax.broadcasted_iota(jnp.int32, (count, LANES), 0)
    place = place.astype(f32)
    local_place = jnp.where(place >= cut, place - cut, place)
    pair = lane_of((count, LANES)) % (HD // 2)
    inverse = jnp.zeros((1, LANES), f32)
    for i in range(HD // 2):
        inverse = jnp.where(pair[0:1] == i, float(np.float32(rope_base ** (-2.0 * i / HD))), inverse)
    angles = local_place * inverse
    sign = jnp.where(lane_of((count, LANES)) % HD < HD // 2, -1.0, 1.0)
    return jnp.cos(angles), sign * jnp.sin(angles)


def layer_kernel(dims, names, *refs):
    n_u, n_b, seqs, td, rows, heads = dims
    r = types.SimpleNamespace(**dict(zip(names, refs)))
    tb = n_u * td
    tokens = seqs * tb
    seq = n_b * tb
    n_z = n_b // 2
    width = r.x.shape[2]
    u, b = here()
    net = Net(r.send_sems, r.recv_sems)
    others = [u ^ off for off in range(n_u - 1, 0, -1)]
    slab = at_block(u, td)
    mine = at_block(b, rows)
    ff = r.wdg.shape[0]
    ff_rows = ff // n_b
    chunks = ff // 256

    def part(v):
        return at_block(v, td)

    share = heads * HD
    ff_own = r.wd.shape[0]
    thirds = (r.wq_in, r.wk_in, r.wv_in)
    r.gains[...] = jnp.zeros_like(r.gains)
    for row, gain in enumerate((r.ga, r.gf)):
        r.gains[row : row + 1, 0:rows] = gain[...].astype(f32).reshape(1, rows)
    lane_place = (b % (LANES // rows)) * rows
    r.gains[...] = pltpu.roll(r.gains[...], lane_place, 1)
    greet(u, b, n_u, n_b)
    got_g = [net.push(r.gains, r.gbuf.at[b, u], v, b) for v in others]
    got_w = [
        net.push(w.at[:, at_block(v, share)], r.wq.at[u, mine, pl.ds(i * share, share)], v, b)
        for i, w in enumerate(thirds)
        for v in others
    ]
    r.wo[mine] = r.wout[...]
    g_out = Gather(net, lambda c: r.wo.at[at_block(c, rows)], u, b)
    got_x = [[net.push(r.x.at[s], r.xg.at[s, slab], v, b) for v in others] for s in range(seqs)]
    for i, w in enumerate(thirds):
        r.wq[u, mine, i * share : (i + 1) * share] = w[:, at_block(u, share)]
    r.xg[:, slab] = r.x[...]
    r.vfg[:, slab] = r.vf[:, :, at_block(u, share)]
    r.gog[:, slab] = r.go[...]
    r.gbuf[b, u] = r.gains[...]
    arrive(got_g)
    got_g = [net.push(r.gbuf.at[b], r.gbuf.at[b], u, b ^ off) for off in range(1, n_b)]
    arrive(got_w)
    g_qk = Gather(net, lambda c: r.wq.at[:, at_block(c, rows), pl.ds(0, 2 * share)], u, b)
    g_v = Gather(net, lambda c: r.wq.at[:, at_block(c, rows), pl.ds(2 * share, share)], u, b)
    got_v = [net.push(r.vf.at[:, :, at_block(v, share)], r.vfg.at[:, slab], v, b) for v in others]
    seq_of_unit = b // heads
    for s in range(seqs):
        cut = jnp.sum((1 - r.segments[s : s + 1, :]).astype(f32), axis=1, keepdims=True)
        r.cosr[s], r.sinr[s] = rope_rows(b * tb, cut, tb)

        @pl.when(seq_of_unit == s)
        def _():
            key_place = lane_of((8, seq)).astype(f32)
            r.low[...] = jnp.where(key_place >= cut, cut, 0.0).astype(jnp.int32)

    arrive(got_g)
    per_tile = LANES // rows
    for tile in range(n_u * n_b // per_tile):
        total = None
        for index in range(tile * per_tile, (tile + 1) * per_tile):
            term = r.gbuf[index % n_b, index // n_b]
            total = term if total is None else total + term
        r.gain[:, tile * LANES : (tile + 1) * LANES] = total
    for s in range(seqs):
        arrive(got_x[s])

        def norm(step, carry, s=s):
            place = at_block(step, tb // 2)
            values = r.xg[s, place].astype(f32)
            factor = lax.rsqrt(jnp.mean(values * values, axis=-1, keepdims=True) + epsilon)
            hat = values * factor
            r.hat[s, place] = hat.astype(bf16)
            r.normed[s, place] = (hat * r.gain[0:1, :]).astype(bf16)
            return carry

        lax.fori_loop(0, 2, norm, 0)
    got_go = [net.push(r.go, r.gog.at[:, slab], v, b) for v in others]
    g_qk.forward()
    g_qk.relay()
    g_v.forward()
    g_qk.finish()

    x_qk = Exchange(net, r.stage.at[:, pl.ds(0, tb)], r.units.at[:, pl.ds(0, tb)], u, b, n_b)
    x_v = Exchange(net, r.stage.at[:, pl.ds(tb, tb // 2)], r.units.at[:, pl.ds(tb, tb // 2)], u, b, n_b)
    for s in range(seqs):
        left = r.normed[s]
        for n in range(heads // 4):
            spans = [slice(i * share + n * 256, i * share + (n + 1) * 256) for i in range(2)]
            pair_of = [dot(left, r.wq[:, :, span].reshape(width, 256)) for span in spans]
            for i in range(2):
                lanes = slice(i * LANES, (i + 1) * LANES)
                query, key = [f[:, lanes] * r.cosr[s] + partner(f[:, lanes]) * r.sinr[s] for f in pair_of]
                low_lane = lane_of(query.shape) < HD
                unit = s * heads + 4 * n + 2 * i
                r.stage[unit, 0:tb] = jnp.where(low_lane, query, swap_halves(key)).astype(bf16)
                r.stage[unit + 1, 0:tb] = jnp.where(low_lane, swap_halves(query), key).astype(bf16)
        for unit in range(s * heads, (s + 1) * heads):
            x_qk.give(unit)
    arrive(got_v)
    g_v.relay()
    g_v.finish()
    for s in range(seqs):
        left = r.normed[s]
        for n in range(heads // 4):
            first_lane = 2 * share + n * 256
            found = dot(left, r.wq[:, :, first_lane : first_lane + 256].reshape(width, 256))
            for i in range(2):
                first = r.vfg[s, :, n * 256 + i * LANES : n * 256 + (i + 1) * LANES].astype(f32)
                value = 0.5 * found[:, i * LANES : (i + 1) * LANES] + 0.5 * first
                unit = s * heads + 4 * n + 2 * i
                r.stage[unit, tb:] = pack_rows(value).astype(bf16)
                r.stage[unit + 1, tb:] = pack_rows(swap_halves(value)).astype(bf16)
        for unit in range(s * heads, (s + 1) * heads):
            x_v.give(unit)
    for i, w in enumerate((r.wg_in, r.wu_in)):
        wide_rows = widen(w[...], ff_own, ff_rows)
        for v in range(n_u):
            for n in range(chunks):
                at = (2 * n + i) * 256
                r.wgu[v, :, at : at + 256] = wide_rows[:, v * ff + n * 256 : v * ff + (n + 1) * 256]
    r.wg[u, mine] = r.wgu[u]
    got_o = [net.push(r.wgu.at[v], r.wg.at[u, mine], v, b) for v in others]
    r.units[b] = r.stage[b]
    for slot in range(n_b):
        r.wdg[slot * ff_rows + ff_own : (slot + 1) * ff_rows] = jnp.zeros((ff_rows - ff_own, width), bf16)
    r.wdg[pl.ds(pl.multiple_of(b * ff_rows, ff_rows), ff_own)] = r.wd[...]
    g_out.forward()
    g_out.relay()
    x_qk.take()
    g_out.finish()


    def fill_keys(block, carry):
        place = at_block(block, tb)
        low = lane_of((tb, LANES)) < HD
        tile = r.units[block, 0:tb].astype(f32)
        query = jnp.where(low, tile * HD ** (-0.5), 0.0)
        key = jnp.where(low, swap_halves(tile), 0.0)
        r.keys[place] = key.astype(bf16)
        r.key_t[:, place] = jnp.transpose(key)[:HD].astype(bf16)
        r.query[place] = query.astype(bf16)
        r.query_t[:, place] = jnp.transpose(query).astype(bf16)
        return carry

    def fill_values(block, carry):
        place = at_block(block, tb)
        low = lane_of((tb, LANES)) < HD
        value = jnp.where(low, unpack_rows(r.units[block, tb:].astype(f32)), 0.0)
        r.value[place] = value.astype(bf16)
        r.value_t[:, place] = jnp.transpose(value)[:HD].astype(bf16)
        return carry

    lax.fori_loop(0, n_b, fill_keys, 0)
    x_v.take()
    arrive(got_o)

    def gate_slot(n):
        return lambda c: r.wg.at[:, at_block(c, rows), pl.ds(n * 512, 512)]

    g_gate = [Gather(net, gate_slot(0), u, b)]
    x_out = Exchange(net, r.ostage, r.parts, u, b, n_b)
    lax.fori_loop(0, n_b, fill_values, 0)

    def attend(step, carry):
        qb = seq // QB - 1 - step
        q_at = at_block(qb, QB)
        query = r.query_t[:, q_at]
        low_row = r.low[0:1, q_at]
        r.acc[...] = jnp.zeros_like(r.acc)

        def inner(kb, state):
            best, total = state
            k_at = at_block(kb, QB)
            scores = dot(r.keys[k_at], query)
            scores = jnp.where(allowed_block(kb * QB, qb * QB, low_row, QB, QB), scores, neg_big)
            new_best = jnp.maximum(best, jnp.max(scores, axis=0, keepdims=True))
            weights = jnp.exp(scores - new_best)
            rescale = jnp.exp(best - new_best)
            total = total * rescale + jnp.sum(weights, axis=0, keepdims=True)
            r.acc[...] = r.acc[...] * rescale + dot(r.value_t[:, k_at], weights.astype(bf16))
            return new_best, total

        start = (jnp.full((1, QB), neg_big, f32), jnp.zeros((1, QB), f32))
        best, total = lax.fori_loop(0, qb + 1, inner, start)
        out = r.acc[...] / total
        r.heads_t[:, q_at] = out
        r.lse[:, q_at] = jnp.broadcast_to(best + jnp.log(total), (8, QB))
        turned = jnp.transpose(jnp.concatenate([out, jnp.zeros_like(out)], axis=0))
        for i in range(QB // tb):
            to = qb * (QB // tb) + i
            r.ostage[to] = pack_rows(turned[i * tb : (i + 1) * tb]).astype(bf16)
            x_out.give(to)
        return carry

    lax.fori_loop(0, seq // QB, attend, 0)
    r.parts[b] = r.ostage[b]
    g_gate[0].forward()
    x_out.take()
    g_down = Gather(net, lambda c: r.wdg.at[pl.ds(pl.multiple_of(c * ff_rows, ff_rows), ff_own)], u, b)
    g_gate += [Gather(net, gate_slot(n), u, b) for n in range(1, chunks)]

    half = tb // 2
    got_s = []
    for s in range(seqs):
        for pair in range(heads // 2):
            one = r.parts[s * heads + 2 * pair].astype(f32)
            two = r.parts[s * heads + 2 * pair + 1].astype(f32)
            low_lane = lane_of(one.shape) < HD
            lanes = slice(pair * LANES, (pair + 1) * LANES)
            r.mix[s, :half, lanes] = jnp.where(low_lane, one, swap_halves(two)).astype(bf16)
            r.mix[s, half:, lanes] = jnp.where(low_lane, swap_halves(one), two).astype(bf16)
        r.branch[s] = dot(r.mix[s], r.wo[...]).astype(bf16)
        got_s.append([net.push(r.branch.at[s, part(v)], r.landed.at[u, s], v, b) for v in others])
        r.landed[u, s] = r.branch[s, slab]
    g_gate[0].relay()
    g_down.forward()
    r.sums[...] = jnp.zeros_like(r.sums)
    got_n = []
    for s in range(seqs):
        arrive(got_s[s])
        total = sum(r.landed[v, s].astype(f32) for v in range(n_u))
        own = r.x[s].astype(f32)
        hid = own + total
        r.hidden[s] = hid
        factor = lax.rsqrt(jnp.mean(hid * hid, axis=-1, keepdims=True) + epsilon)
        r.nf_own[s] = (hid * factor * r.gain[1:2, :]).astype(bf16)
        got_n.append([net.push(r.nf_own.at[s], r.nf.at[s, slab], v, b) for v in others])
        r.nf[s, slab] = r.nf_own[s]
        r.sums[0:1] = r.sums[0:1] + jnp.sum(own * own, axis=0, keepdims=True)
        r.sums[1:2] = r.sums[1:2] + jnp.sum(total * total, axis=0, keepdims=True)
    arrive(got_go)
    g_down.relay()
    g_down.finish()
    g_gate[1].forward()

    def hidden_units(n, s):
        span, at = slice(n * 256, (n + 1) * 256), n * 512
        gate = dot(r.nf[s], r.wg[:, :, at : at + 256].reshape(width, 256))
        up = dot(r.nf[s], r.wg[:, :, at + 256 : at + 512].reshape(width, 256))
        grad_act = dot_nt(r.gog[s], r.wdg[span])
        sig = 1.0 / (1.0 + jnp.exp(-gate))
        silu = gate * sig
        r.act[s, :, span] = (silu * up).astype(bf16)
        r.dgu[s, :, at : at + 256] = (grad_act * up * sig * (1.0 + gate * (1.0 - sig))).astype(bf16)
        r.dgu[s, :, at + 256 : at + 512] = (grad_act * silu).astype(bf16)

    def grad_gate(n):
        right = r.dgu[:, :, n * 512 : (n + 1) * 512].reshape(tokens, 512)

        def some(v, carry):
            found = dot(r.nft[at_block(v, 256)], right)
            r.wg_buf[n, :, :, v] = found.astype(bf16).reshape(n_z, 2, rows, 512)
            return carry

        lax.fori_loop(0, n_u, some, 0)
        parts = r.wg_buf.at[n]
        return Scatter(
            net, u, b, lambda z, c: parts.at[z, c], r.wg_pair.at[n], r.wg_sum.at[n], r.wg_land.at[n]
        )

    def grad_down(n):
        half_units = ff // 2
        span = slice(n * half_units, (n + 1) * half_units)
        found = dot_tn(r.act[:, :, span].reshape(tokens, half_units), r.gog[...].reshape(tokens, width))
        r.wd_buf[n * (n_z // 2) : (n + 1) * (n_z // 2)] = found.astype(bf16).reshape(
            n_z // 2, 2, ff_rows, width
        )

    got_d, s_gate = [], []
    for n in range(chunks):
        g_gate[n].finish()
        for s in range(seqs):
            if n == 0:
                arrive(got_n[s])
            hidden_units(n, s)
            if n == 0:
                r.nft[:, s * tb : (s + 1) * tb] = jnp.transpose(r.nf[s])
            if s == 0 and n + 1 < chunks:
                g_gate[n + 1].relay()
        if n + 2 < chunks:
            g_gate[n + 2].forward()
        if n > 0:
            s_gate[n - 1].middle()
        if n + 1 < chunks:
            s_gate.append(grad_gate(n))
    for s in range(seqs):
        left = r.dgu[s]
        for v in range(n_u):
            r.d_low[s, :, v * 256 : (v + 1) * 256] = dot_nt(left, r.wg[v]).astype(bf16)
        got_d.append([net.push(r.d_low.at[s, part(v)], r.landed.at[u, s], v, b) for v in others])
        r.landed[u, s] = r.d_low[s, slab]
    s_gate.append(grad_gate(chunks - 1))

    got_b = []

    def norm_back(s):
        arrive(got_d[s])
        grad_normed = sum(r.landed[v, s].astype(f32) for v in range(n_u))
        hid = r.hidden[s]
        factor = lax.rsqrt(jnp.mean(hid * hid, axis=-1, keepdims=True) + epsilon)
        hat = hid * factor
        scaled = grad_normed * r.gain[1:2, :]
        inner = jnp.mean(scaled * hat, axis=-1, keepdims=True)
        total = r.go[s].astype(f32) + factor * (scaled - hat * inner)
        r.ghid[s] = total
        r.gb_own[s] = total.astype(bf16)
        got_b.append([net.push(r.gb_own.at[s], r.xg.at[s, slab], v, b) for v in others])
        r.xg[s, slab] = r.gb_own[s]
        r.sums[4:5] = r.sums[4:5] + jnp.sum(grad_normed * hat, axis=0, keepdims=True)

    norm_back(0)
    grad_down(0)
    norm_back(1)
    grad_down(1)
    s_gate[0].merge()
    s_gate[chunks - 1].middle()
    ff_cut = pl.ds(0, ff_own)
    s_down = Scatter(
        net, u, b, lambda z, c: r.wd_buf.at[z, c, ff_cut], r.wd_pair.at[:, ff_cut],
        r.wd_sum.at[:, ff_cut], r.wd_land.at[:, ff_cut],
    )
    s_gate[1].merge()
    x_grad = Exchange(net, r.ostage2, r.grads, u, b, n_b)
    for s in range(seqs):
        arrive(got_b[s])
        for pair in range(heads // 2):
            found = dot_nt(r.xg[s], r.wo[pair * LANES : (pair + 1) * LANES])
            unit = s * heads + 2 * pair
            r.ostage2[unit] = pack_rows(found).astype(bf16)
            r.ostage2[unit + 1] = pack_rows(swap_halves(found)).astype(bf16)
            x_grad.give(unit)
            x_grad.give(unit + 1)
    r.grads[b] = r.ostage2[b]

    for copies in got_s:
        net.sent(copies)

    def forward(s, carry):
        r.branch[s] = dot(r.act[s], r.wdg[...]).astype(bf16)
        return carry

    lax.fori_loop(0, seqs, forward, 0)
    got_f = [net.push(r.branch.at[:, part(v)], r.landed_f.at[u], v, b) for v in others]
    r.landed_f[u] = r.branch[:, slab]
    found = dot_tn(r.mix[...].reshape(tokens, share), r.xg[...].reshape(tokens, width))
    r.wo_buf[...] = found.astype(bf16).reshape(n_z, 2, rows, width)
    s_out = Scatter(net, u, b, lambda z, c: r.wo_buf.at[z, c], r.wo_pair, r.wo_sum, r.wo_land)
    x_grad.take()
    s_gate[2].merge()
    s_out.middle()

    def more(block, carry):
        place = at_block(block, tb)
        g = unpack_rows(r.grads[block].astype(f32))
        g = jnp.where(lane_of(g.shape) < HD, g, 0.0)
        r.grad[place] = g.astype(bf16)
        turned = jnp.transpose(g)
        r.grad_t[:, place] = turned.astype(bf16)
        total = jnp.sum(turned[:HD] * r.heads_t[:, place], axis=0, keepdims=True)
        r.row_dot[:, place] = jnp.broadcast_to(total, (8, tb))
        return carry

    lax.fori_loop(0, n_b, more, 0)
    x_qk.sent()
    x_v.sent()
    x_back = Exchange(net, r.stage, r.returned, u, b, n_b)

    def backward(keys_at, first_key, queries_at, first_query):
        seen = allowed_block(first_key, first_query, r.low[0:1, queries_at], keys_at.size, queries_at.size)
        scores = dot(r.keys[keys_at], r.query_t[:, queries_at])
        probs = jnp.where(seen, jnp.exp(scores - r.lse[0:1, queries_at]), 0.0)
        prob_grad = dot(r.value[keys_at], r.grad_t[:, queries_at])
        score_grad = (probs * (prob_grad - r.row_dot[0:1, queries_at])).astype(bf16)
        r.dv[keys_at] += dot(probs.astype(bf16), r.grad[queries_at])
        r.dk[keys_at] += dot(score_grad, r.query[queries_at])
        r.dq_t[:, queries_at] += dot(r.key_t[:, keys_at], score_grad)

    def finished(block):
        place = at_block(block, tb)
        columns = r.dq_t[:, place] * HD ** (-0.5)
        turned = jnp.transpose(jnp.concatenate([columns, jnp.zeros_like(columns)], axis=0))
        low_lane = lane_of(turned.shape) < HD
        r.stage[block, 0:tb] = jnp.where(low_lane, turned, swap_halves(r.dk[place])).astype(bf16)
        r.stage[block, tb:] = pack_rows(r.dv[place]).astype(bf16)
        x_back.give(block)

    s_out.merge()
    for buffer in (r.dq_t, r.dk, r.dv):
        buffer[...] = jnp.zeros_like(buffer)
    ratio = QB // KB

    @pl.when(b >= n_b // 2)
    def _():
        def outer(kb, carry):
            def inner(qb, carry):
                backward(at_block(kb, KB), kb * KB, at_block(qb, QB), qb * QB)
                return carry

            lax.fori_loop(kb // ratio, seq // QB, inner, 0)
            finished(kb)
            return carry

        lax.fori_loop(0, n_b, outer, 0)

    @pl.when(b < n_b // 2)
    def _():
        def outer(step, carry):
            qb = n_b - 1 - step

            def inner(kb, carry):
                backward(at_block(kb, QB), kb * QB, at_block(qb, KB), qb * KB)
                return carry

            lax.fori_loop(0, qb // ratio + 1, inner, 0)
            finished(qb)
            return carry

        lax.fori_loop(0, n_b, outer, 0)

    s_down.middle()
    r.returned[b] = r.stage[b]
    arrive(got_f)
    for s in range(seqs):
        total = r.hidden[s] + sum(r.landed_f[v, s].astype(f32) for v in range(n_u))
        r.out[s] = total.astype(bf16)
        r.sums[2:3] = r.sums[2:3] + jnp.sum(total * total, axis=0, keepdims=True)
    x_back.take()

    for s in range(seqs):
        for pair in range(heads // 2):
            unit = s * heads + 2 * pair
            one, two = r.returned[unit, 0:tb].astype(f32), r.returned[unit + 1, 0:tb].astype(f32)
            low_lane = lane_of(one.shape) < HD
            grads = (
                jnp.where(low_lane, one, swap_halves(two)),
                jnp.where(low_lane, swap_halves(one), two),
            )
            for i, tile in enumerate(grads):
                turned = tile * r.cosr[s] - partner(tile) * r.sinr[s]
                at = i * share + pair * LANES
                r.raw[s, :, at : at + LANES] = turned.astype(bf16)
            one = unpack_rows(r.returned[unit, tb:].astype(f32))
            two = unpack_rows(r.returned[unit + 1, tb:].astype(f32))
            both = 0.5 * jnp.where(low_lane, one, swap_halves(two))
            at = 2 * share + pair * LANES
            r.raw[s, :, at : at + LANES] = both.astype(bf16)
    columns = r.raw.shape[2]
    for v in range(n_u):
        left = r.normed[:, :, v * 256 : (v + 1) * 256].reshape(tokens, 256)
        found = dot_tn(left, r.raw[...].reshape(tokens, columns))
        r.wq_buf[:, :, v] = found.astype(bf16).reshape(n_z, 2, rows, columns)
    s_qkv = Scatter(net, u, b, lambda z, c: r.wq_buf.at[z, c], r.wq_pair, r.wq_sum, r.wq_land)
    s_down.merge()

    for copies in got_d:
        net.sent(copies)
    got_g = []
    for s in range(seqs):
        left = r.raw[s]
        for v in range(n_u):
            lanes = slice(v * 256, (v + 1) * 256)
            found = dot_nt(left, r.wq[v])
            r.d_low[s, :, lanes] = found.astype(bf16)
            term = jnp.sum(found * r.hat[s, :, lanes].astype(f32), axis=0, keepdims=True)
            r.sums[3:4, lanes] = r.sums[3:4, lanes] + term
        got_g.append([net.push(r.d_low.at[s, part(v)], r.landed.at[u, s], v, b) for v in others])
        r.landed[u, s] = r.d_low[s, slab]
    got_s = [net.push(r.sums, r.sums_u.at[u], v, b) for v in others]
    r.sums_u[u] = r.sums[...]
    s_qkv.middle()
    got_v = [net.push(r.raw.at[:, part(v), pl.ds(2 * share, share)], r.gv.at[u], v, b) for v in others]
    r.gv[u] = r.raw[:, slab, 2 * share :]
    got_c = []
    for n in range(chunks):
        s_gate[n].finish(r.wg_low.at[n])
        got_c += [net.push(r.wg_low.at[n, v], r.dwgu.at[n, u], v, b) for v in others]
        r.dwgu[n, u] = r.wg_low[n, u]
    s_qkv.merge()
    s_out.finish(r.gwo)
    s_down.finish(r.gwd)
    arrive(got_s)
    r.sums_b[b] = sum(r.sums_u[v] for v in range(n_u))
    got_s = [net.push(r.sums_b.at[b], r.sums_b.at[b], u, b ^ off) for off in range(1, n_b)]
    for s in range(seqs):
        arrive(got_g[s])
        grad_normed = sum(r.landed[v, s].astype(f32) for v in range(n_u))
        own = r.x[s].astype(f32)
        factor = lax.rsqrt(jnp.mean(own * own, axis=-1, keepdims=True) + epsilon)
        hat = own * factor
        scaled = grad_normed * r.gain[0:1, :]
        inner = jnp.mean(scaled * hat, axis=-1, keepdims=True)
        r.gin[s] = (r.ghid[s] + factor * (scaled - hat * inner)).astype(bf16)
    arrive(got_v)
    for v in range(n_u):
        r.gvf[:, :, v * 256 : (v + 1) * 256] = r.gv[v]
    arrive(got_s)
    totals = sum(r.sums_b[c] for c in range(n_b))
    squares = jnp.sum(totals, axis=1, keepdims=True) / (seqs * seq * width)
    r.totals[...] = totals
    roots = jnp.sqrt(squares)
    lane = lane_of((1, LANES))
    r.stats[...] = jnp.where(lane == 0, roots[0:1], jnp.where(lane == 1, roots[1:2], roots[2:3]))[0, 0:3]
    per = LANES // rows
    tile = r.totals[:, at_block(u * (n_b // per) + b // per, LANES)]
    tile = pltpu.roll(tile, (LANES - lane_place) % LANES, 1)
    r.gga[...] = tile[3, 0:rows]
    r.ggf[...] = tile[4, 0:rows]
    s_qkv.finish(r.wq_low)
    got = [net.push(r.wq_low.at[v], r.dwq.at[u], v, b) for v in others]
    r.dwq[u] = r.wq_low[u]
    arrive(got_c)
    for i, to in enumerate((r.gwg, r.gwu)):
        pieces = []
        for v in range(n_u):
            row = jnp.concatenate(
                [r.dwgu[n, v, :, i * 256 : (i + 1) * 256] for n in range(chunks)], axis=1
            ).astype(f32)
            pieces += [row[:, j * ff_rows : j * ff_rows + ff_own] for j in range(n_b)]
        to[...] = jnp.concatenate(pieces, axis=1)
    arrive(got)
    for i, to in enumerate((r.gwq, r.gwk, r.gwv)):
        for v in range(n_u):
            to[:, v * share : (v + 1) * share] = r.dwq[v, :, i * share : (i + 1) * share].astype(f32)
    for exchange in (x_out, x_grad, x_back):
        exchange.sent()
    net.drain()


def hand_out_kernel(count, *refs):
    for given, taken in zip(refs[:count], refs[count:]):
        taken[...] = given[...]


def local_units(
    inputs, v_first, grad_out, positions, segments,
    w_query, w_key, w_value, w_out, w_gate, w_up, w_down, gain_attn, gain_ffn,
):
    n_u, n_b = lax.axis_size("ulysses"), lax.axis_size("blk")
    seqs, td, width = inputs.shape
    rows = w_query.shape[0]
    heads = HEADS // n_u
    tb = n_u * td
    seq = n_b * tb
    ff_own = w_down.shape[0]
    ff_pad = -(-ff_own // 32) * 32
    ff = ff_pad * n_b
    chunks = ff // 256
    dims = (n_u, n_b, seqs, td, rows, heads)

    columns = 3 * heads * HD
    n_z = n_b // 2
    own, block = (seqs, td, width), (seqs, tb, width)
    inputs_of = dict(
        x=inputs, vf=v_first, go=grad_out, segments=segments, wq_in=w_query, wk_in=w_key, wv_in=w_value,
        wout=w_out, wg_in=w_gate, wu_in=w_up, wd=w_down, ga=gain_attn, gf=gain_ffn,
    )
    outs = dict(
        out=(own, bf16), gin=(own, bf16), gvf=(own, bf16), gwq=((rows, width), f32), gwk=((rows, width), f32),
        gwv=((rows, width), f32), gwo=((rows, width), f32), gwg=(w_gate.shape, f32), gwu=(w_gate.shape, f32),
        gwd=((ff_own, width), f32), gga=((rows,), f32), ggf=((rows,), f32), stats=((3,), f32),
    )
    scratch = dict(
        gains=((8, LANES), f32), wgu=((n_u, rows, 2 * ff), bf16), cosr=((seqs, tb, LANES), f32),
        sinr=((seqs, tb, LANES), f32), low=((8, seq), jnp.int32),
        dwq=((n_u, rows, columns), bf16), dwgu=((chunks, n_u, rows, 512), bf16), nft=((width, seqs * tb), bf16),
        xg=(block, bf16), vfg=((seqs, tb, heads * HD), bf16), gbuf=((n_b, n_u, 8, LANES), f32),
        gain=((8, width), f32), normed=(block, bf16), wq=((n_u, n_b * rows, columns), bf16),
        gog=(block, bf16), wg=((n_u, n_b * rows, 2 * ff), bf16), wdg=((ff, width), bf16),
        wo=((n_b * rows, width), bf16), stage=((n_b, tb + tb // 2, LANES), bf16),
        units=((n_b, tb + tb // 2, LANES), bf16), keys=((seq, LANES), bf16), key_t=((HD, seq), bf16),
        query=((seq, LANES), bf16), query_t=((LANES, seq), bf16), value=((seq, LANES), bf16),
        value_t=((HD, seq), bf16), acc=((HD, QB), f32), heads_t=((HD, seq), f32), lse=((8, seq), f32),
        ostage=((n_b, tb // 2, LANES), bf16), parts=((n_b, tb // 2, LANES), bf16),
        mix=((seqs, tb, heads * HD), bf16), branch=(block, bf16), landed=((n_u,) + own, bf16),
        sums=((8, width), f32), totals=((8, width), f32), hat=(block, bf16), hidden=(own, f32), nf_own=(own, bf16), nf=(block, bf16),
        act=((seqs, tb, ff), bf16), dgu=((seqs, tb, 2 * ff), bf16), d_low=(block, bf16),
        ghid=(own, f32), gb_own=(own, bf16),
        landed_f=((n_u,) + own, bf16),
        wd_buf=((n_z, 2, ff_pad, width), bf16), wd_pair=((n_z, ff_pad, width), bf16),
        wd_sum=((n_z, ff_pad, width), bf16), wd_land=((n_z, ff_pad, width), bf16),
        wg_buf=((chunks, n_z, 2, n_u, rows, 512), bf16), wg_pair=((chunks, n_z, n_u, rows, 512), bf16),
        wg_sum=((chunks, n_z, n_u, rows, 512), bf16), wg_land=((chunks, n_z, n_u, rows, 512), bf16),
        wg_low=((chunks, n_u, rows, 512), bf16),
        ostage2=((n_b, tb // 2, LANES), bf16), grads=((n_b, tb // 2, LANES), bf16),
        wo_buf=((n_z, 2, rows, width), bf16), wo_pair=((n_z, rows, width), bf16),
        wo_sum=((n_z, rows, width), bf16), wo_land=((n_z, rows, width), bf16),
        grad=((seq, LANES), bf16), grad_t=((LANES, seq), bf16), row_dot=((8, seq), f32),
        dq_t=((HD, seq), f32), dk=((seq, LANES), f32), dv=((seq, LANES), f32),
        returned=((n_b, tb + tb // 2, LANES), bf16), raw=((seqs, tb, columns), bf16),
        gv=((n_u, seqs, td, heads * HD), bf16),
        wq_buf=((n_z, 2, n_u, rows, columns), bf16), wq_pair=((n_z, n_u, rows, columns), bf16),
        wq_sum=((n_z, n_u, rows, columns), bf16), wq_land=((n_z, n_u, rows, columns), bf16),
        wq_low=((n_u, rows, columns), bf16), sums_u=((n_u, 8, width), f32), sums_b=((n_b, 8, width), f32),
    )
    names = [*inputs_of, *outs, *scratch, "send_sems", "recv_sems"]
    vmem = pl.BlockSpec(memory_space=pltpu.VMEM)
    results = pl.pallas_call(
        functools.partial(layer_kernel, dims, names),
        out_shape=[jax.ShapeDtypeStruct(shape, dtype) for shape, dtype in outs.values()],
        in_specs=[vmem] * len(inputs_of),
        out_specs=[vmem] * len(outs),
        scratch_shapes=[pltpu.VMEM(shape, dtype) for shape, dtype in scratch.values()]
        + [pltpu.SemaphoreType.DMA((SEMAPHORES,))] * 2,
        compiler_params=pltpu.CompilerParams(
            collective_id=1, has_side_effects=True, vmem_limit_bytes=VMEM_BYTES
        ),
        name="layer",
    )(*inputs_of.values())
    return pl.pallas_call(
        functools.partial(hand_out_kernel, len(outs)),
        out_shape=[jax.ShapeDtypeStruct(shape, dtype) for shape, dtype in outs.values()],
        in_specs=[vmem] * len(outs),
        out_specs=[vmem] * len(outs),
        name="hand_out",
    )(*results)


SEMAPHORES = 288


def fits_units(mesh):
    return mesh.shape["ulysses"] == 4 and mesh.shape["blk"] == 8


def solution(mesh):
    in_specs = (
        P(None, ("blk", "ulysses"), None),
        P(None, ("blk", "ulysses"), None),
        P(None, ("blk", "ulysses"), None),
        P(None, ("blk", "ulysses")),
        P(),
        P(("ulysses", "blk"), None),
        P(("ulysses", "blk"), None),
        P(("ulysses", "blk"), None),
        P(("ulysses", "blk"), None),
        P(("ulysses", "blk"), None),
        P(("ulysses", "blk"), None),
        P(("ulysses", "blk"), None),
        P(("ulysses", "blk")),
        P(("ulysses", "blk")),
    )
    out_specs = (
        P(None, ("blk", "ulysses"), None),
        P(None, ("blk", "ulysses"), None),
        P(None, ("blk", "ulysses"), None),
        P(("ulysses", "blk"), None),
        P(("ulysses", "blk"), None),
        P(("ulysses", "blk"), None),
        P(("ulysses", "blk"), None),
        P(("ulysses", "blk"), None),
        P(("ulysses", "blk"), None),
        P(("ulysses", "blk"), None),
        P(("ulysses", "blk")),
        P(("ulysses", "blk")),
        P(),
    )
    path = local_units if fits_units(mesh) else local
    return jax.shard_map(path, mesh=mesh, in_specs=in_specs, out_specs=out_specs, check_vma=False)
```

```python
import functools
import types

import jax
import jax.numpy as jnp
import numpy as np
from jax import lax
from jax.experimental import pallas as pl
from jax.experimental.pallas import tpu as pltpu
from jax.sharding import PartitionSpec as P

HEADS = 16
HD = 64


epsilon = 1e-06
rope_base = 10000.0
neg_big = -1e30


def norm_rows(values, gain):
    factor = lax.rsqrt(jnp.mean(values * values, axis=-1, keepdims=True) + epsilon)
    hatted = values * factor
    return (hatted * gain, hatted, factor)


def norm_back(grad_normed, hatted, factor, gain):
    scaled = grad_normed * gain
    inner = jnp.mean(scaled * hatted, axis=-1, keepdims=True)
    return (factor * (scaled - hatted * inner), jnp.sum(grad_normed * hatted, axis=(0, 1)))


def rope_tables(positions):
    half_dim = HD // 2
    inverse = rope_base ** (-2.0 * jnp.arange(half_dim, dtype=jnp.float32) / HD)
    angles = positions.astype(jnp.float32)[:, :, None] * inverse
    return (jnp.cos(angles)[:, :, None, :], jnp.sin(angles)[:, :, None, :])


def rotate(values, cosine, sine, forward_turn):
    shaped = values.reshape(values.shape[0], values.shape[1], HEADS, HD)
    half_dim = HD // 2
    first = shaped[..., :half_dim]
    second = shaped[..., half_dim:]
    if forward_turn:
        turned = jnp.concatenate(
            [first * cosine - second * sine, second * cosine + first * sine], axis=-1
        )
    else:
        turned = jnp.concatenate(
            [first * cosine + second * sine, second * cosine - first * sine], axis=-1
        )
    return turned.reshape(values.shape)


def project(activations, weight):
    return jnp.einsum("std,de->ste", activations, weight, preferred_element_type=jnp.float32)


def project_back(gradient, weight):
    return jnp.einsum("ste,de->std", gradient, weight, preferred_element_type=jnp.float32)


def weight_grad(activations, gradient):
    return jnp.einsum("std,ste->de", activations, gradient, preferred_element_type=jnp.float32)


def allowed_mask(segments, query_first, query_count, key_first, key_count):
    seg_query = lax.dynamic_slice_in_dim(segments, query_first, query_count, 1)
    seg_key = lax.dynamic_slice_in_dim(segments, key_first, key_count, 1)
    query_place = query_first + jnp.arange(query_count, dtype=jnp.int32)
    key_place = key_first + jnp.arange(key_count, dtype=jnp.int32)
    causal = key_place[None, :] <= query_place[:, None]
    same_doc = seg_query[:, :, None] == seg_key[:, None, :]
    return (causal[None] & same_doc)[:, :, None, :]


def over_blocks(step_fn, running, pieces, block_rows):
    row_count = pieces[0].shape[1]
    block_count = row_count // block_rows
    stacked = tuple(
        (
            jnp.moveaxis(
                member.reshape((member.shape[0], block_count, block_rows) + member.shape[2:]), 1, 0
            )
            for member in pieces
        )
    )
    offsets = block_rows * jnp.arange(block_count, dtype=jnp.int32)

    def advance(current, scan_entry):
        return (step_fn(current, scan_entry[:-1], scan_entry[-1]), None)

    running, unused = lax.scan(advance, running, stacked + (offsets,))
    return running


def add_rows(buffer, update, first_row):
    current = lax.dynamic_slice_in_dim(buffer, first_row, update.shape[1], 1)
    return lax.dynamic_update_slice_in_dim(buffer, current + update, first_row, 1)


def unchanged(running):
    return running


def local(
    inputs,
    v_first,
    grad_out,
    positions,
    segments,
    w_query,
    w_key,
    w_value,
    w_out,
    w_gate,
    w_up,
    w_down,
    gain_attn,
    gain_ffn,
):
    gathered = (
        lax.all_gather(w_query, ("ulysses", "blk"), axis=0, tiled=True),
        lax.all_gather(w_key, ("ulysses", "blk"), axis=0, tiled=True),
        lax.all_gather(w_value, ("ulysses", "blk"), axis=0, tiled=True),
        lax.all_gather(w_out, ("ulysses", "blk"), axis=0, tiled=True),
        lax.all_gather(w_gate, ("ulysses", "blk"), axis=0, tiled=True),
        lax.all_gather(w_up, ("ulysses", "blk"), axis=0, tiled=True),
        lax.all_gather(w_down, ("ulysses", "blk"), axis=0, tiled=True),
        lax.all_gather(gain_attn, ("ulysses", "blk"), axis=0, tiled=True),
        lax.all_gather(gain_ffn, ("ulysses", "blk"), axis=0, tiled=True),
    )
    (
        full_query,
        full_key,
        full_value,
        full_out,
        full_gate,
        full_up,
        full_down,
        full_gain_attn,
        full_gain_ffn,
    ) = gathered
    score_scale = HD ** (-0.5)
    residual = inputs.astype(jnp.float32)
    normed_f, hatted_attn, factor_attn = norm_rows(residual, full_gain_attn.astype(jnp.float32))
    normed = normed_f.astype(jnp.bfloat16)
    cosine, sine = rope_tables(positions)
    query_tok = rotate(project(normed, full_query), cosine, sine, True).astype(jnp.bfloat16)
    key_tok = rotate(project(normed, full_key), cosine, sine, True).astype(jnp.bfloat16)
    value_tok = (0.5 * project(normed, full_value) + 0.5 * v_first.astype(jnp.float32)).astype(
        jnp.bfloat16
    )
    query_head, key_head, value_head = (
        lax.all_to_all(query_tok, "ulysses", split_axis=2, concat_axis=1, tiled=True),
        lax.all_to_all(key_tok, "ulysses", split_axis=2, concat_axis=1, tiled=True),
        lax.all_to_all(value_tok, "ulysses", split_axis=2, concat_axis=1, tiled=True),
    )
    seq_count, block_rows, width = query_head.shape
    heads_local = width // HD
    query_start = lax.axis_index("blk") * block_rows
    full_rows = block_rows * lax.axis_size("blk")

    def split_heads(values):
        return values.reshape(values.shape[0], values.shape[1], heads_local, HD)

    query_four = split_heads(query_head)

    def attend_rows(running, pieces, first_row):
        key_rows, value_rows = pieces
        key_count = key_rows.shape[1]

        def attend_compute(current):
            best, total, accum = current
            allowed = allowed_mask(segments, query_start, block_rows, first_row, key_count)
            scores = (
                jnp.einsum(
                    "sqhd,skhd->sqhk",
                    query_four,
                    split_heads(key_rows),
                    preferred_element_type=jnp.float32,
                )
                * score_scale
            )
            masked = jnp.where(allowed, scores, neg_big)
            new_best = jnp.maximum(best, jnp.max(masked, axis=-1))
            weights = jnp.where(allowed, jnp.exp(masked - new_best[..., None]), 0.0)
            rescale = jnp.exp(best - new_best)
            total = total * rescale + jnp.sum(weights, axis=-1)
            accum = accum * rescale[..., None] + jnp.einsum(
                "sqhk,skhd->sqhd",
                weights.astype(jnp.bfloat16),
                split_heads(value_rows),
                preferred_element_type=jnp.float32,
            )
            return (new_best, total, accum)

        return lax.cond(
            first_row <= query_start + block_rows - 1, attend_compute, unchanged, running
        )

    stat_zeros = jnp.zeros((seq_count, block_rows, heads_local), jnp.float32)
    head_zeros = jnp.zeros((seq_count, block_rows, heads_local, HD), jnp.float32)
    initial = (
        jnp.full((seq_count, block_rows, heads_local), neg_big, jnp.float32),
        stat_zeros,
        head_zeros,
    )
    best, total, accum = over_blocks(
        attend_rows,
        initial,
        (
            lax.all_gather(key_head, "blk", axis=1, tiled=True),
            lax.all_gather(value_head, "blk", axis=1, tiled=True),
        ),
        block_rows,
    )
    log_total = best + jnp.log(total)
    attn_heads = accum / total[..., None]
    attn_low = attn_heads.reshape(seq_count, block_rows, width).astype(jnp.bfloat16)
    mixed = lax.all_to_all(attn_low, "ulysses", split_axis=1, concat_axis=2, tiled=True)
    attn_branch = project(mixed, full_out)
    hidden = residual + attn_branch
    normed_ffn_f, hatted_ffn, factor_ffn = norm_rows(hidden, full_gain_ffn.astype(jnp.float32))
    normed_ffn = normed_ffn_f.astype(jnp.bfloat16)
    gate = project(normed_ffn, full_gate)
    up_proj = project(normed_ffn, full_up)
    sigmoid_gate = jax.nn.sigmoid(gate)
    silu_gate = gate * sigmoid_gate
    act = (silu_gate * up_proj).astype(jnp.bfloat16)
    ffn_branch = project(act, full_down)
    output_f = hidden + ffn_branch
    output = output_f.astype(jnp.bfloat16)
    squares = lax.psum(
        (
            jnp.sum(residual * residual),
            jnp.sum(attn_branch * attn_branch),
            jnp.sum(output_f * output_f),
        ),
        ("ulysses", "blk"),
    )
    entry_count = residual.size * lax.axis_size("ulysses") * lax.axis_size("blk")
    statistics = jnp.sqrt(jnp.stack(squares) / entry_count)
    again = (
        lax.all_gather(w_query, ("ulysses", "blk"), axis=0, tiled=True),
        lax.all_gather(w_key, ("ulysses", "blk"), axis=0, tiled=True),
        lax.all_gather(w_value, ("ulysses", "blk"), axis=0, tiled=True),
        lax.all_gather(w_out, ("ulysses", "blk"), axis=0, tiled=True),
        lax.all_gather(w_gate, ("ulysses", "blk"), axis=0, tiled=True),
        lax.all_gather(w_up, ("ulysses", "blk"), axis=0, tiled=True),
        lax.all_gather(w_down, ("ulysses", "blk"), axis=0, tiled=True),
        lax.all_gather(gain_attn, ("ulysses", "blk"), axis=0, tiled=True),
        lax.all_gather(gain_ffn, ("ulysses", "blk"), axis=0, tiled=True),
    )
    (
        back_query,
        back_key,
        back_value,
        back_out,
        back_gate,
        back_up,
        back_down,
        back_gain_attn,
        back_gain_ffn,
    ) = again
    grad_act = project_back(grad_out, back_down)
    grad_gate = (grad_act * up_proj * sigmoid_gate * (1.0 + gate * (1.0 - sigmoid_gate))).astype(
        jnp.bfloat16
    )
    grad_up = (grad_act * silu_gate).astype(jnp.bfloat16)
    grad_normed_ffn = project_back(grad_gate, back_gate) + project_back(grad_up, back_up)
    grad_ffn_norm, grad_gain_ffn = norm_back(
        grad_normed_ffn, hatted_ffn, factor_ffn, back_gain_ffn.astype(jnp.float32)
    )
    grad_hidden = grad_out.astype(jnp.float32) + grad_ffn_norm
    grad_branch = grad_hidden.astype(jnp.bfloat16)
    grad_mixed = project_back(grad_branch, back_out).astype(jnp.bfloat16)
    dout_head = lax.all_to_all(grad_mixed, "ulysses", split_axis=2, concat_axis=1, tiled=True)
    dout_four = split_heads(dout_head)
    row_dot = jnp.sum(dout_four.astype(jnp.float32) * attn_heads, axis=-1)

    def grad_rows(running, pieces, first_row):
        key_rows, value_rows = pieces
        key_count = key_rows.shape[1]

        def grad_compute(current):
            grad_query, grad_keys, grad_values = current
            key_part = split_heads(key_rows)
            allowed = allowed_mask(segments, query_start, block_rows, first_row, key_count)
            scores = (
                jnp.einsum(
                    "sqhd,skhd->sqhk", query_four, key_part, preferred_element_type=jnp.float32
                )
                * score_scale
            )
            probs = jnp.where(allowed, jnp.exp(scores - log_total[..., None]), 0.0)
            prob_grad = jnp.einsum(
                "sqhd,skhd->sqhk",
                dout_four,
                split_heads(value_rows),
                preferred_element_type=jnp.float32,
            )
            score_grad = (probs * (prob_grad - row_dot[..., None])).astype(jnp.bfloat16)
            grad_query = (
                grad_query
                + jnp.einsum(
                    "sqhk,skhd->sqhd", score_grad, key_part, preferred_element_type=jnp.float32
                )
                * score_scale
            )
            key_term = (
                jnp.einsum(
                    "sqhk,sqhd->skhd", score_grad, query_four, preferred_element_type=jnp.float32
                )
                * score_scale
            )
            value_term = jnp.einsum(
                "sqhk,sqhd->skhd",
                probs.astype(jnp.bfloat16),
                dout_four,
                preferred_element_type=jnp.float32,
            )
            return (
                grad_query,
                add_rows(grad_keys, key_term, first_row),
                add_rows(grad_values, value_term, first_row),
            )

        return lax.cond(first_row <= query_start + block_rows - 1, grad_compute, unchanged, running)

    full_zeros = jnp.zeros((seq_count, full_rows, heads_local, HD), jnp.float32)
    grad_query_own, grad_keys_all, grad_values_all = over_blocks(
        grad_rows,
        (head_zeros, full_zeros, full_zeros),
        (
            lax.all_gather(key_head, "blk", axis=1, tiled=True),
            lax.all_gather(value_head, "blk", axis=1, tiled=True),
        ),
        block_rows,
    )
    grad_key_own, grad_value_own = (
        lax.psum_scatter(
            grad_keys_all.reshape(seq_count, full_rows, width).astype(jnp.bfloat16),
            "blk",
            scatter_dimension=1,
            tiled=True,
        ).astype(jnp.float32),
        lax.psum_scatter(
            grad_values_all.reshape(seq_count, full_rows, width).astype(jnp.bfloat16),
            "blk",
            scatter_dimension=1,
            tiled=True,
        ).astype(jnp.float32),
    )
    grad_query_own = grad_query_own.reshape(seq_count, block_rows, width)
    grad_query_tok, grad_key_tok, grad_value_tok = (
        lax.all_to_all(
            grad_query_own.astype(jnp.bfloat16), "ulysses", split_axis=1, concat_axis=2, tiled=True
        ),
        lax.all_to_all(
            grad_key_own.astype(jnp.bfloat16), "ulysses", split_axis=1, concat_axis=2, tiled=True
        ),
        lax.all_to_all(
            grad_value_own.astype(jnp.bfloat16), "ulysses", split_axis=1, concat_axis=2, tiled=True
        ),
    )
    grad_query_raw = rotate(grad_query_tok.astype(jnp.float32), cosine, sine, False).astype(
        jnp.bfloat16
    )
    grad_key_raw = rotate(grad_key_tok.astype(jnp.float32), cosine, sine, False).astype(
        jnp.bfloat16
    )
    grad_v_first = grad_value_tok * 0.5
    grad_normed = (
        project_back(grad_query_raw, back_query)
        + project_back(grad_key_raw, back_key)
        + project_back(grad_v_first, back_value)
    )
    grad_attn_norm, grad_gain_attn = norm_back(
        grad_normed, hatted_attn, factor_attn, back_gain_attn.astype(jnp.float32)
    )
    grad_inputs = (grad_hidden + grad_attn_norm).astype(jnp.bfloat16)
    model_width = w_query.shape[1]
    hidden_width = w_gate.shape[1]
    owned = lax.psum_scatter(
        jnp.concatenate(
            [
                weight_grad(normed, grad_query_raw),
                weight_grad(normed, grad_key_raw),
                weight_grad(normed, grad_v_first),
                weight_grad(mixed, grad_branch),
                weight_grad(normed_ffn, grad_gate),
                weight_grad(normed_ffn, grad_up),
                grad_gain_attn[:, None],
                grad_gain_ffn[:, None],
            ],
            axis=1,
        ),
        ("ulysses", "blk"),
        scatter_dimension=0,
        tiled=True,
    )
    grad_w_down = lax.psum_scatter(
        weight_grad(act, grad_out), ("ulysses", "blk"), scatter_dimension=0, tiled=True
    )
    column = 0
    pieces = []
    for span in (model_width, model_width, model_width, model_width, hidden_width, hidden_width):
        pieces.append(owned[:, column : column + span])
        column = column + span
    grad_gain_attn_own = owned[:, column]
    grad_gain_ffn_own = owned[:, column + 1]
    return (
        output,
        grad_inputs,
        grad_v_first,
        pieces[0],
        pieces[1],
        pieces[2],
        pieces[3],
        pieces[4],
        pieces[5],
        grad_w_down,
        grad_gain_attn_own,
        grad_gain_ffn_own,
        statistics,
    )


MESH = pl.DeviceIdType.MESH
LANES = 128
VMEM_BYTES = 61 << 20
f32 = jnp.float32
bf16 = jnp.bfloat16
QB, KB = 512, 256


class Copy:
    def __init__(self, copy, send_at, recv_at, when):
        self.copy, self.at, self.recv_at, self.when = copy, send_at, recv_at, when

    def wait_recv(self):
        self.copy.wait_recv()

    def wait_send(self):
        if self.when is None:
            self.copy.wait_send()
        else:
            pl.when(self.when)(self.copy.wait_send)


class Net:
    def __init__(self, send_sems, recv_sems):
        self.send_sems, self.recv_sems = send_sems, recv_sems
        self.count, self.open = 0, []

    def push(self, src, dst, u, b, when=None, recv_at=None, at=None):
        if at is None:
            at = self.count
            self.count += 1
        recv_at = at if recv_at is None else recv_at
        copy = pltpu.make_async_remote_copy(
            src_ref=src,
            dst_ref=dst,
            send_sem=self.send_sems.at[at],
            recv_sem=self.recv_sems.at[recv_at],
            device_id=(u, b),
            device_id_type=MESH,
        )
        if when is None:
            copy.start()
        else:
            pl.when(when)(copy.start)
        made = Copy(copy, at, recv_at, when)
        self.open.append(made)
        return made

    def sent(self, copies):
        for copy in copies:
            copy.wait_send()
        self.open = [copy for copy in self.open if copy not in copies]

    def drain(self):
        for copy in self.open:
            copy.wait_send()
        self.open = []


def arrive(copies):
    for copy in copies:
        copy.wait_recv()


def here():
    return lax.axis_index("ulysses"), lax.axis_index("blk")


def greet(u, b, n_u, n_b):
    barrier = pltpu.get_barrier_semaphore()
    for off in range(1, n_u):
        pl.semaphore_signal(barrier, inc=1, device_id=(u ^ off, b), device_id_type=MESH)
    for off in range(1, n_b):
        pl.semaphore_signal(barrier, inc=1, device_id=(u, b ^ off), device_id_type=MESH)
    pl.semaphore_wait(barrier, n_u - 1 + n_b - 1)


def dot(left, right):
    return jnp.dot(left, right, preferred_element_type=f32)


def dot_nt(left, right):
    return lax.dot_general(left, right, (((1,), (1,)), ((), ())), preferred_element_type=f32)


def dot_tn(left, right):
    return lax.dot_general(left, right, (((0,), (0,)), ((), ())), preferred_element_type=f32)


def at_block(index, size):
    return pl.ds(pl.multiple_of(index * size, size), size)


def lane_of(shape):
    return lax.broadcasted_iota(jnp.int32, shape, len(shape) - 1)


def swap_halves(tile):
    return pltpu.roll(tile, HD, tile.ndim - 1)


def partner(tile):
    low = lane_of(tile.shape) % HD < HD // 2
    return jnp.where(low, pltpu.roll(tile, LANES - HD // 2, 1), pltpu.roll(tile, HD // 2, 1))


def pack_rows(rows):
    half = rows.shape[0] // 2
    low = lane_of((half, LANES)) < HD
    return jnp.where(low, rows[:half], swap_halves(rows[half:]))


def unpack_rows(packed):
    return jnp.concatenate([packed, swap_halves(packed)], axis=0)


class Exchange:
    def __init__(self, net, staged, landed, u, b, n_b):
        self.net, self.staged, self.landed, self.u, self.b, self.n_b = net, staged, landed, u, b, n_b
        self.at = net.count
        net.count += n_b

    def copy(self, to, slot_from):
        return pltpu.make_async_remote_copy(
            src_ref=self.staged.at[to],
            dst_ref=self.landed.at[slot_from],
            send_sem=self.net.send_sems.at[self.at + to],
            recv_sem=self.net.recv_sems.at[self.at + slot_from],
            device_id=(self.u, to),
            device_id_type=MESH,
        )

    def give(self, to):
        @pl.when(to != self.b)
        def _():
            self.copy(to, self.b).start()

    def take(self):
        for off in range(1, self.n_b):
            self.copy(self.b ^ off, self.b ^ off).wait_recv()

    def sent(self):
        for off in range(1, self.n_b):
            self.copy(self.b ^ off, self.b).wait_send()


class Gather:
    def __init__(self, net, slot, u, b):
        self.net, self.slot, self.u, self.b = net, slot, u, b
        self.inner = ((b // 2) == 1) | ((b // 2) == 2)
        mine = slot(b)
        self.two = net.push(mine, mine, u, b ^ 4)
        self.one = net.push(mine, mine, u, b ^ 2)
        self.three = net.push(mine, mine, u, b ^ 6, when=self.inner)
        self.side = [net.push(mine, mine, u, b ^ 1)]

    def beside(self, owner):
        got = self.slot(owner)
        self.side.append(self.net.push(got, got, self.u, self.b ^ 1))

    def forward(self):
        self.two.wait_recv()
        got = self.slot(self.b ^ 4)
        self.net.push(got, got, self.u, self.b ^ 2, when=self.inner, recv_at=self.three.at)
        self.beside(self.b ^ 4)

    def relay(self):
        self.one.wait_recv()
        self.beside(self.b ^ 2)
        self.three.wait_recv()
        self.beside(self.b ^ 6)

    def finish(self):
        arrive(self.side)


class Scatter:
    def __init__(self, net, u, b, mine, paired, summed, landed):
        self.net, self.u, self.b = net, u, b
        self.mine, self.paired, self.summed, self.landed = mine, paired, summed, landed
        self.z = b // 2
        self.inner = (self.z == 1) | (self.z == 2)
        self.swap = [net.push(mine(z, 1 - b % 2), paired.at[z], u, b ^ 1) for z in range(4)]

    def add(self, z):
        self.summed[z] = (self.mine(z, self.b % 2)[...].astype(f32) + self.paired[z].astype(f32)).astype(bf16)

    def middle(self):
        net, u, b, z, inner = self.net, self.u, self.b, self.z, self.inner
        outer = jnp.logical_not(inner)
        arrive(self.swap)
        self.add(z ^ 3)
        far = self.summed.at[z ^ 3]
        self.extra = net.push(far, self.landed.at[3], u, b ^ 2, when=outer)
        self.three = net.push(far, self.landed.at[2], u, b ^ 6, when=inner)
        self.add(z ^ 2)
        self.two = net.push(self.summed.at[z ^ 2], self.landed.at[1], u, b ^ 4, when=outer)
        self.add(z ^ 1)
        self.one = net.push(self.summed.at[z ^ 1], self.landed.at[0], u, b ^ 2)
        self.add(z)

    def merge(self):
        net, u, b, z = self.net, self.u, self.b, self.z

        @pl.when(self.inner)
        def _():
            self.extra.wait_recv()
            self.summed[z ^ 2] = (self.summed[z ^ 2].astype(f32) + self.landed[3].astype(f32)).astype(bf16)

        net.push(self.summed.at[z ^ 2], self.landed.at[1], u, b ^ 4, when=self.inner, at=self.two.at)

    def finish(self, total):
        self.one.wait_recv()
        self.two.wait_recv()
        total[...] = (
            self.summed[self.z].astype(f32) + self.landed[0].astype(f32) + self.landed[1].astype(f32)
        ).astype(total.dtype)

        @pl.when(self.inner)
        def _():
            self.three.wait_recv()
            total[...] = (total[...].astype(f32) + self.landed[2].astype(f32)).astype(total.dtype)


def allowed_block(first_key, first_query, low_row, keys=KB, queries=QB):
    key_place = first_key + lax.broadcasted_iota(jnp.int32, (keys, queries), 0)
    query_place = first_query + lax.broadcasted_iota(jnp.int32, (keys, queries), 1)
    return (key_place <= query_place) & (key_place >= low_row)


def widen(rows, size, padded):
    zeros = jnp.zeros((rows.shape[0], padded - size), rows.dtype)
    pieces = []
    for at in range(0, rows.shape[1], size):
        pieces += [rows[:, at : at + size], zeros]
    return jnp.concatenate(pieces, axis=1)


def rope_rows(base, cut, count):
    place = base + lax.broadcasted_iota(jnp.int32, (count, LANES), 0)
    place = place.astype(f32)
    local_place = jnp.where(place >= cut, place - cut, place)
    pair = lane_of((count, LANES)) % (HD // 2)
    inverse = jnp.zeros((1, LANES), f32)
    for i in range(HD // 2):
        inverse = jnp.where(pair[0:1] == i, float(np.float32(rope_base ** (-2.0 * i / HD))), inverse)
    angles = local_place * inverse
    sign = jnp.where(lane_of((count, LANES)) % HD < HD // 2, -1.0, 1.0)
    return jnp.cos(angles), sign * jnp.sin(angles)


def layer_kernel(dims, names, *refs):
    n_u, n_b, seqs, td, rows, heads = dims
    r = types.SimpleNamespace(**dict(zip(names, refs)))
    tb = n_u * td
    tokens = seqs * tb
    seq = n_b * tb
    n_z = n_b // 2
    width = r.x.shape[2]
    u, b = here()
    net = Net(r.send_sems, r.recv_sems)
    others = [u ^ off for off in range(n_u - 1, 0, -1)]
    slab = at_block(u, td)
    mine = at_block(b, rows)
    ff = r.wdg.shape[0]
    ff_rows = ff // n_b
    chunks = ff // 256

    def part(v):
        return at_block(v, td)

    share = heads * HD
    ff_own = r.wd.shape[0]
    thirds = (r.wq_in, r.wk_in, r.wv_in)
    r.gains[...] = jnp.zeros_like(r.gains)
    for row, gain in enumerate((r.ga, r.gf)):
        r.gains[row : row + 1, 0:rows] = gain[...].astype(f32).reshape(1, rows)
    lane_place = (b % (LANES // rows)) * rows
    r.gains[...] = pltpu.roll(r.gains[...], lane_place, 1)
    greet(u, b, n_u, n_b)
    got_g = [net.push(r.gains, r.gbuf.at[b, u], v, b) for v in others]
    got_w = [
        net.push(w.at[:, at_block(v, share)], r.wq.at[u, mine, pl.ds(i * share, share)], v, b)
        for i, w in enumerate(thirds)
        for v in others
    ]
    r.wo[mine] = r.wout[...]
    g_out = Gather(net, lambda c: r.wo.at[at_block(c, rows)], u, b)
    got_x = [[net.push(r.x.at[s], r.xg.at[s, slab], v, b) for v in others] for s in range(seqs)]
    for i, w in enumerate(thirds):
        r.wq[u, mine, i * share : (i + 1) * share] = w[:, at_block(u, share)]
    r.xg[:, slab] = r.x[...]
    r.vfg[:, slab] = r.vf[:, :, at_block(u, share)]
    r.gog[:, slab] = r.go[...]
    r.gbuf[b, u] = r.gains[...]
    arrive(got_g)
    got_g = [net.push(r.gbuf.at[b], r.gbuf.at[b], u, b ^ off) for off in range(1, n_b)]
    arrive(got_w)
    g_qk = Gather(net, lambda c: r.wq.at[:, at_block(c, rows), pl.ds(0, 2 * share)], u, b)
    g_v = Gather(net, lambda c: r.wq.at[:, at_block(c, rows), pl.ds(2 * share, share)], u, b)
    got_v = [net.push(r.vf.at[:, :, at_block(v, share)], r.vfg.at[:, slab], v, b) for v in others]
    seq_of_unit = b // heads
    for s in range(seqs):
        cut = jnp.sum((1 - r.segments[s : s + 1, :]).astype(f32), axis=1, keepdims=True)
        r.cosr[s], r.sinr[s] = rope_rows(b * tb, cut, tb)

        @pl.when(seq_of_unit == s)
        def _():
            key_place = lane_of((8, seq)).astype(f32)
            r.low[...] = jnp.where(key_place >= cut, cut, 0.0).astype(jnp.int32)

    arrive(got_g)
    per_tile = LANES // rows
    for tile in range(n_u * n_b // per_tile):
        total = None
        for index in range(tile * per_tile, (tile + 1) * per_tile):
            term = r.gbuf[index % n_b, index // n_b]
            total = term if total is None else total + term
        r.gain[:, tile * LANES : (tile + 1) * LANES] = total
    for s in range(seqs):
        arrive(got_x[s])

        def norm(step, carry, s=s):
            place = at_block(step, tb // 2)
            values = r.xg[s, place].astype(f32)
            factor = lax.rsqrt(jnp.mean(values * values, axis=-1, keepdims=True) + epsilon)
            hat = values * factor
            r.hat[s, place] = hat.astype(bf16)
            r.normed[s, place] = (hat * r.gain[0:1, :]).astype(bf16)
            return carry

        lax.fori_loop(0, 2, norm, 0)
    got_go = [net.push(r.go, r.gog.at[:, slab], v, b) for v in others]
    g_qk.forward()
    g_qk.relay()
    g_v.forward()
    g_qk.finish()

    x_qk = Exchange(net, r.stage.at[:, pl.ds(0, tb)], r.units.at[:, pl.ds(0, tb)], u, b, n_b)
    x_v = Exchange(net, r.stage.at[:, pl.ds(tb, tb // 2)], r.units.at[:, pl.ds(tb, tb // 2)], u, b, n_b)
    for s in range(seqs):
        left = r.normed[s]
        for n in range(heads // 4):
            spans = [slice(i * share + n * 256, i * share + (n + 1) * 256) for i in range(2)]
            pair_of = [dot(left, r.wq[:, :, span].reshape(width, 256)) for span in spans]
            for i in range(2):
                lanes = slice(i * LANES, (i + 1) * LANES)
                query, key = [f[:, lanes] * r.cosr[s] + partner(f[:, lanes]) * r.sinr[s] for f in pair_of]
                low_lane = lane_of(query.shape) < HD
                unit = s * heads + 4 * n + 2 * i
                r.stage[unit, 0:tb] = jnp.where(low_lane, query, swap_halves(key)).astype(bf16)
                r.stage[unit + 1, 0:tb] = jnp.where(low_lane, swap_halves(query), key).astype(bf16)
        for unit in range(s * heads, (s + 1) * heads):
            x_qk.give(unit)
    arrive(got_v)
    g_v.relay()
    g_v.finish()
    for s in range(seqs):
        left = r.normed[s]
        for n in range(heads // 4):
            first_lane = 2 * share + n * 256
            found = dot(left, r.wq[:, :, first_lane : first_lane + 256].reshape(width, 256))
            for i in range(2):
                first = r.vfg[s, :, n * 256 + i * LANES : n * 256 + (i + 1) * LANES].astype(f32)
                value = 0.5 * found[:, i * LANES : (i + 1) * LANES] + 0.5 * first
                unit = s * heads + 4 * n + 2 * i
                r.stage[unit, tb:] = pack_rows(value).astype(bf16)
                r.stage[unit + 1, tb:] = pack_rows(swap_halves(value)).astype(bf16)
        for unit in range(s * heads, (s + 1) * heads):
            x_v.give(unit)
    for i, w in enumerate((r.wg_in, r.wu_in)):
        wide_rows = widen(w[...], ff_own, ff_rows)
        for v in range(n_u):
            for n in range(chunks):
                at = (2 * n + i) * 256
                r.wgu[v, :, at : at + 256] = wide_rows[:, v * ff + n * 256 : v * ff + (n + 1) * 256]
    r.wg[u, mine] = r.wgu[u]
    got_o = [net.push(r.wgu.at[v], r.wg.at[u, mine], v, b) for v in others]
    r.units[b] = r.stage[b]
    for slot in range(n_b):
        r.wdg[slot * ff_rows + ff_own : (slot + 1) * ff_rows] = jnp.zeros((ff_rows - ff_own, width), bf16)
    r.wdg[pl.ds(pl.multiple_of(b * ff_rows, ff_rows), ff_own)] = r.wd[...]
    g_out.forward()
    g_out.relay()
    x_qk.take()
    g_out.finish()


    def fill_keys(block, carry):
        place = at_block(block, tb)
        low = lane_of((tb, LANES)) < HD
        tile = r.units[block, 0:tb].astype(f32)
        query = jnp.where(low, tile * HD ** (-0.5), 0.0)
        key = jnp.where(low, swap_halves(tile), 0.0)
        r.keys[place] = key.astype(bf16)
        r.key_t[:, place] = jnp.transpose(key)[:HD].astype(bf16)
        r.query[place] = query.astype(bf16)
        r.query_t[:, place] = jnp.transpose(query).astype(bf16)
        return carry

    def fill_values(block, carry):
        place = at_block(block, tb)
        low = lane_of((tb, LANES)) < HD
        value = jnp.where(low, unpack_rows(r.units[block, tb:].astype(f32)), 0.0)
        r.value[place] = value.astype(bf16)
        r.value_t[:, place] = jnp.transpose(value)[:HD].astype(bf16)
        return carry

    lax.fori_loop(0, n_b, fill_keys, 0)
    x_v.take()
    arrive(got_o)

    def gate_slot(n):
        return lambda c: r.wg.at[:, at_block(c, rows), pl.ds(n * 512, 512)]

    g_gate = [Gather(net, gate_slot(0), u, b)]
    x_out = Exchange(net, r.ostage, r.parts, u, b, n_b)
    lax.fori_loop(0, n_b, fill_values, 0)

    def attend(step, carry):
        qb = seq // QB - 1 - step
        q_at = at_block(qb, QB)
        query = r.query_t[:, q_at]
        low_row = r.low[0:1, q_at]
        r.acc[...] = jnp.zeros_like(r.acc)

        def inner(kb, state):
            best, total = state
            k_at = at_block(kb, QB)
            scores = dot(r.keys[k_at], query)
            scores = jnp.where(allowed_block(kb * QB, qb * QB, low_row, QB, QB), scores, neg_big)
            new_best = jnp.maximum(best, jnp.max(scores, axis=0, keepdims=True))
            weights = jnp.exp(scores - new_best)
            rescale = jnp.exp(best - new_best)
            total = total * rescale + jnp.sum(weights, axis=0, keepdims=True)
            r.acc[...] = r.acc[...] * rescale + dot(r.value_t[:, k_at], weights.astype(bf16))
            return new_best, total

        start = (jnp.full((1, QB), neg_big, f32), jnp.zeros((1, QB), f32))
        best, total = lax.fori_loop(0, qb + 1, inner, start)
        out = r.acc[...] / total
        r.heads_t[:, q_at] = out
        r.lse[:, q_at] = jnp.broadcast_to(best + jnp.log(total), (8, QB))
        turned = jnp.transpose(jnp.concatenate([out, jnp.zeros_like(out)], axis=0))
        for i in range(QB // tb):
            to = qb * (QB // tb) + i
            r.ostage[to] = pack_rows(turned[i * tb : (i + 1) * tb]).astype(bf16)
            x_out.give(to)
        return carry

    lax.fori_loop(0, seq // QB, attend, 0)
    r.parts[b] = r.ostage[b]
    g_gate[0].forward()
    x_out.take()
    g_down = Gather(net, lambda c: r.wdg.at[pl.ds(pl.multiple_of(c * ff_rows, ff_rows), ff_own)], u, b)
    g_gate += [Gather(net, gate_slot(n), u, b) for n in range(1, chunks)]

    half = tb // 2
    got_s = []
    for s in range(seqs):
        for pair in range(heads // 2):
            one = r.parts[s * heads + 2 * pair].astype(f32)
            two = r.parts[s * heads + 2 * pair + 1].astype(f32)
            low_lane = lane_of(one.shape) < HD
            lanes = slice(pair * LANES, (pair + 1) * LANES)
            r.mix[s, :half, lanes] = jnp.where(low_lane, one, swap_halves(two)).astype(bf16)
            r.mix[s, half:, lanes] = jnp.where(low_lane, swap_halves(one), two).astype(bf16)
        r.branch[s] = dot(r.mix[s], r.wo[...]).astype(bf16)
        got_s.append([net.push(r.branch.at[s, part(v)], r.landed.at[u, s], v, b) for v in others])
        r.landed[u, s] = r.branch[s, slab]
    g_gate[0].relay()
    g_down.forward()
    r.sums[...] = jnp.zeros_like(r.sums)
    got_n = []
    for s in range(seqs):
        arrive(got_s[s])
        total = sum(r.landed[v, s].astype(f32) for v in range(n_u))
        own = r.x[s].astype(f32)
        hid = own + total
        r.hidden[s] = hid
        factor = lax.rsqrt(jnp.mean(hid * hid, axis=-1, keepdims=True) + epsilon)
        r.nf_own[s] = (hid * factor * r.gain[1:2, :]).astype(bf16)
        got_n.append([net.push(r.nf_own.at[s], r.nf.at[s, slab], v, b) for v in others])
        r.nf[s, slab] = r.nf_own[s]
        r.sums[0:1] = r.sums[0:1] + jnp.sum(own * own, axis=0, keepdims=True)
        r.sums[1:2] = r.sums[1:2] + jnp.sum(total * total, axis=0, keepdims=True)
    arrive(got_go)
    g_down.relay()
    g_down.finish()

    def hidden_units(n, s):
        span, at = slice(n * 256, (n + 1) * 256), n * 512
        gate = dot(r.nf[s], r.wg[:, :, at : at + 256].reshape(width, 256))
        up = dot(r.nf[s], r.wg[:, :, at + 256 : at + 512].reshape(width, 256))
        grad_act = dot_nt(r.gog[s], r.wdg[span])
        sig = 1.0 / (1.0 + jnp.exp(-gate))
        silu = gate * sig
        r.act[s, :, span] = (silu * up).astype(bf16)
        r.dgu[s, :, at : at + 256] = (grad_act * up * sig * (1.0 + gate * (1.0 - sig))).astype(bf16)
        r.dgu[s, :, at + 256 : at + 512] = (grad_act * silu).astype(bf16)

    def grad_gate(n):
        right = r.dgu[:, :, n * 512 : (n + 1) * 512].reshape(tokens, 512)

        def some(v, carry):
            found = dot(r.nft[at_block(v, 256)], right)
            r.wg_buf[n, :, :, v] = found.astype(bf16).reshape(n_z, 2, rows, 512)
            return carry

        lax.fori_loop(0, n_u, some, 0)
        parts = r.wg_buf.at[n]
        return Scatter(
            net, u, b, lambda z, c: parts.at[z, c], r.wg_pair.at[n], r.wg_sum.at[n], r.wg_land.at[n]
        )

    def grad_down(n):
        half_units = ff // 2
        span = slice(n * half_units, (n + 1) * half_units)
        found = dot_tn(r.act[:, :, span].reshape(tokens, half_units), r.gog[...].reshape(tokens, width))
        r.wd_buf[n * (n_z // 2) : (n + 1) * (n_z // 2)] = found.astype(bf16).reshape(
            n_z // 2, 2, ff_rows, width
        )

    got_d, s_gate = [], []
    for n in range(chunks):
        g_gate[n].finish()
        for s in range(seqs):
            if n == 0:
                arrive(got_n[s])
            hidden_units(n, s)
            if n == 0:
                r.nft[:, s * tb : (s + 1) * tb] = jnp.transpose(r.nf[s])
            if s == 0 and n + 1 < chunks:
                g_gate[n + 1].forward()
        if n + 1 < chunks:
            g_gate[n + 1].relay()
        if n > 0:
            s_gate[n - 1].middle()
        if n + 1 < chunks:
            s_gate.append(grad_gate(n))
    for s in range(seqs):
        left = r.dgu[s]
        for v in range(n_u):
            r.d_low[s, :, v * 256 : (v + 1) * 256] = dot_nt(left, r.wg[v]).astype(bf16)
        got_d.append([net.push(r.d_low.at[s, part(v)], r.landed.at[u, s], v, b) for v in others])
        r.landed[u, s] = r.d_low[s, slab]
    s_gate.append(grad_gate(chunks - 1))

    got_b = []

    def norm_back(s):
        arrive(got_d[s])
        grad_normed = sum(r.landed[v, s].astype(f32) for v in range(n_u))
        hid = r.hidden[s]
        factor = lax.rsqrt(jnp.mean(hid * hid, axis=-1, keepdims=True) + epsilon)
        hat = hid * factor
        scaled = grad_normed * r.gain[1:2, :]
        inner = jnp.mean(scaled * hat, axis=-1, keepdims=True)
        total = r.go[s].astype(f32) + factor * (scaled - hat * inner)
        r.ghid[s] = total
        r.gb_own[s] = total.astype(bf16)
        got_b.append([net.push(r.gb_own.at[s], r.xg.at[s, slab], v, b) for v in others])
        r.xg[s, slab] = r.gb_own[s]
        r.sums[4:5] = r.sums[4:5] + jnp.sum(grad_normed * hat, axis=0, keepdims=True)

    norm_back(0)
    grad_down(0)
    norm_back(1)
    grad_down(1)
    s_gate[0].merge()
    s_gate[chunks - 1].middle()
    ff_cut = pl.ds(0, ff_own)
    s_down = Scatter(
        net, u, b, lambda z, c: r.wd_buf.at[z, c, ff_cut], r.wd_pair.at[:, ff_cut],
        r.wd_sum.at[:, ff_cut], r.wd_land.at[:, ff_cut],
    )
    s_gate[1].merge()
    x_grad = Exchange(net, r.ostage2, r.grads, u, b, n_b)
    for s in range(seqs):
        arrive(got_b[s])
        for pair in range(heads // 2):
            found = dot_nt(r.xg[s], r.wo[pair * LANES : (pair + 1) * LANES])
            unit = s * heads + 2 * pair
            r.ostage2[unit] = pack_rows(found).astype(bf16)
            r.ostage2[unit + 1] = pack_rows(swap_halves(found)).astype(bf16)
            x_grad.give(unit)
            x_grad.give(unit + 1)
    r.grads[b] = r.ostage2[b]

    for copies in got_s:
        net.sent(copies)

    def forward(s, carry):
        r.branch[s] = dot(r.act[s], r.wdg[...]).astype(bf16)
        return carry

    lax.fori_loop(0, seqs, forward, 0)
    got_f = [net.push(r.branch.at[:, part(v)], r.landed_f.at[u], v, b) for v in others]
    r.landed_f[u] = r.branch[:, slab]
    found = dot_tn(r.mix[...].reshape(tokens, share), r.xg[...].reshape(tokens, width))
    r.wo_buf[...] = found.astype(bf16).reshape(n_z, 2, rows, width)
    s_out = Scatter(net, u, b, lambda z, c: r.wo_buf.at[z, c], r.wo_pair, r.wo_sum, r.wo_land)
    x_grad.take()
    s_gate[2].merge()
    s_out.middle()

    def more(block, carry):
        place = at_block(block, tb)
        g = unpack_rows(r.grads[block].astype(f32))
        g = jnp.where(lane_of(g.shape) < HD, g, 0.0)
        r.grad[place] = g.astype(bf16)
        turned = jnp.transpose(g)
        r.grad_t[:, place] = turned.astype(bf16)
        total = jnp.sum(turned[:HD] * r.heads_t[:, place], axis=0, keepdims=True)
        r.row_dot[:, place] = jnp.broadcast_to(total, (8, tb))
        return carry

    lax.fori_loop(0, n_b, more, 0)
    x_qk.sent()
    x_v.sent()
    x_back = Exchange(net, r.stage, r.returned, u, b, n_b)

    def backward(keys_at, first_key, queries_at, first_query):
        seen = allowed_block(first_key, first_query, r.low[0:1, queries_at], keys_at.size, queries_at.size)
        scores = dot(r.keys[keys_at], r.query_t[:, queries_at])
        probs = jnp.where(seen, jnp.exp(scores - r.lse[0:1, queries_at]), 0.0)
        prob_grad = dot(r.value[keys_at], r.grad_t[:, queries_at])
        score_grad = (probs * (prob_grad - r.row_dot[0:1, queries_at])).astype(bf16)
        r.dv[keys_at] += dot(probs.astype(bf16), r.grad[queries_at])
        r.dk[keys_at] += dot(score_grad, r.query[queries_at])
        r.dq_t[:, queries_at] += dot(r.key_t[:, keys_at], score_grad)

    def finished(block):
        place = at_block(block, tb)
        columns = r.dq_t[:, place] * HD ** (-0.5)
        turned = jnp.transpose(jnp.concatenate([columns, jnp.zeros_like(columns)], axis=0))
        low_lane = lane_of(turned.shape) < HD
        r.stage[block, 0:tb] = jnp.where(low_lane, turned, swap_halves(r.dk[place])).astype(bf16)
        r.stage[block, tb:] = pack_rows(r.dv[place]).astype(bf16)
        x_back.give(block)

    s_out.merge()
    for buffer in (r.dq_t, r.dk, r.dv):
        buffer[...] = jnp.zeros_like(buffer)
    ratio = QB // KB

    @pl.when(b >= n_b // 2)
    def _():
        def outer(kb, carry):
            def inner(qb, carry):
                backward(at_block(kb, KB), kb * KB, at_block(qb, QB), qb * QB)
                return carry

            lax.fori_loop(kb // ratio, seq // QB, inner, 0)
            finished(kb)
            return carry

        lax.fori_loop(0, n_b, outer, 0)

    @pl.when(b < n_b // 2)
    def _():
        def outer(step, carry):
            qb = n_b - 1 - step

            def inner(kb, carry):
                backward(at_block(kb, QB), kb * QB, at_block(qb, KB), qb * KB)
                return carry

            lax.fori_loop(0, qb // ratio + 1, inner, 0)
            finished(qb)
            return carry

        lax.fori_loop(0, n_b, outer, 0)

    s_down.middle()
    r.returned[b] = r.stage[b]
    arrive(got_f)
    for s in range(seqs):
        total = r.hidden[s] + sum(r.landed_f[v, s].astype(f32) for v in range(n_u))
        r.out[s] = total.astype(bf16)
        r.sums[2:3] = r.sums[2:3] + jnp.sum(total * total, axis=0, keepdims=True)
    x_back.take()

    for s in range(seqs):
        for pair in range(heads // 2):
            unit = s * heads + 2 * pair
            one, two = r.returned[unit, 0:tb].astype(f32), r.returned[unit + 1, 0:tb].astype(f32)
            low_lane = lane_of(one.shape) < HD
            grads = (
                jnp.where(low_lane, one, swap_halves(two)),
                jnp.where(low_lane, swap_halves(one), two),
            )
            for i, tile in enumerate(grads):
                turned = tile * r.cosr[s] - partner(tile) * r.sinr[s]
                at = i * share + pair * LANES
                r.raw[s, :, at : at + LANES] = turned.astype(bf16)
            one = unpack_rows(r.returned[unit, tb:].astype(f32))
            two = unpack_rows(r.returned[unit + 1, tb:].astype(f32))
            both = 0.5 * jnp.where(low_lane, one, swap_halves(two))
            at = 2 * share + pair * LANES
            r.raw[s, :, at : at + LANES] = both.astype(bf16)
    columns = r.raw.shape[2]
    for v in range(n_u):
        left = r.normed[:, :, v * 256 : (v + 1) * 256].reshape(tokens, 256)
        found = dot_tn(left, r.raw[...].reshape(tokens, columns))
        r.wq_buf[:, :, v] = found.astype(bf16).reshape(n_z, 2, rows, columns)
    s_qkv = Scatter(net, u, b, lambda z, c: r.wq_buf.at[z, c], r.wq_pair, r.wq_sum, r.wq_land)
    s_down.merge()

    for copies in got_d:
        net.sent(copies)
    got_g = []
    for s in range(seqs):
        left = r.raw[s]
        for v in range(n_u):
            lanes = slice(v * 256, (v + 1) * 256)
            found = dot_nt(left, r.wq[v])
            r.d_low[s, :, lanes] = found.astype(bf16)
            term = jnp.sum(found * r.hat[s, :, lanes].astype(f32), axis=0, keepdims=True)
            r.sums[3:4, lanes] = r.sums[3:4, lanes] + term
        got_g.append([net.push(r.d_low.at[s, part(v)], r.landed.at[u, s], v, b) for v in others])
        r.landed[u, s] = r.d_low[s, slab]
    got_s = [net.push(r.sums, r.sums_u.at[u], v, b) for v in others]
    r.sums_u[u] = r.sums[...]
    s_qkv.middle()
    got_v = [net.push(r.raw.at[:, part(v), pl.ds(2 * share, share)], r.gv.at[u], v, b) for v in others]
    r.gv[u] = r.raw[:, slab, 2 * share :]
    got_c = []
    for n in range(chunks):
        s_gate[n].finish(r.wg_low.at[n])
        got_c += [net.push(r.wg_low.at[n, v], r.dwgu.at[n, u], v, b) for v in others]
        r.dwgu[n, u] = r.wg_low[n, u]
    s_qkv.merge()
    s_out.finish(r.gwo)
    s_down.finish(r.gwd)
    arrive(got_s)
    r.sums_b[b] = sum(r.sums_u[v] for v in range(n_u))
    got_s = [net.push(r.sums_b.at[b], r.sums_b.at[b], u, b ^ off) for off in range(1, n_b)]
    for s in range(seqs):
        arrive(got_g[s])
        grad_normed = sum(r.landed[v, s].astype(f32) for v in range(n_u))
        own = r.x[s].astype(f32)
        factor = lax.rsqrt(jnp.mean(own * own, axis=-1, keepdims=True) + epsilon)
        hat = own * factor
        scaled = grad_normed * r.gain[0:1, :]
        inner = jnp.mean(scaled * hat, axis=-1, keepdims=True)
        r.gin[s] = (r.ghid[s] + factor * (scaled - hat * inner)).astype(bf16)
    arrive(got_v)
    for v in range(n_u):
        r.gvf[:, :, v * 256 : (v + 1) * 256] = r.gv[v]
    arrive(got_s)
    totals = sum(r.sums_b[c] for c in range(n_b))
    squares = jnp.sum(totals, axis=1, keepdims=True) / (seqs * seq * width)
    r.totals[...] = totals
    roots = jnp.sqrt(squares)
    lane = lane_of((1, LANES))
    r.stats[...] = jnp.where(lane == 0, roots[0:1], jnp.where(lane == 1, roots[1:2], roots[2:3]))[0, 0:3]
    per = LANES // rows
    tile = r.totals[:, at_block(u * (n_b // per) + b // per, LANES)]
    tile = pltpu.roll(tile, (LANES - lane_place) % LANES, 1)
    r.gga[...] = tile[3, 0:rows]
    r.ggf[...] = tile[4, 0:rows]
    s_qkv.finish(r.wq_low)
    got = [net.push(r.wq_low.at[v], r.dwq.at[u], v, b) for v in others]
    r.dwq[u] = r.wq_low[u]
    arrive(got_c)
    for i, to in enumerate((r.gwg, r.gwu)):
        pieces = []
        for v in range(n_u):
            row = jnp.concatenate(
                [r.dwgu[n, v, :, i * 256 : (i + 1) * 256] for n in range(chunks)], axis=1
            ).astype(f32)
            pieces += [row[:, j * ff_rows : j * ff_rows + ff_own] for j in range(n_b)]
        to[...] = jnp.concatenate(pieces, axis=1)
    arrive(got)
    for i, to in enumerate((r.gwq, r.gwk, r.gwv)):
        for v in range(n_u):
            to[:, v * share : (v + 1) * share] = r.dwq[v, :, i * share : (i + 1) * share].astype(f32)
    for exchange in (x_out, x_grad, x_back):
        exchange.sent()
    net.drain()


def hand_out_kernel(count, *refs):
    for given, taken in zip(refs[:count], refs[count:]):
        taken[...] = given[...]


def local_units(
    inputs, v_first, grad_out, positions, segments,
    w_query, w_key, w_value, w_out, w_gate, w_up, w_down, gain_attn, gain_ffn,
):
    n_u, n_b = lax.axis_size("ulysses"), lax.axis_size("blk")
    seqs, td, width = inputs.shape
    rows = w_query.shape[0]
    heads = HEADS // n_u
    tb = n_u * td
    seq = n_b * tb
    ff_own = w_down.shape[0]
    ff_pad = -(-ff_own // 32) * 32
    ff = ff_pad * n_b
    chunks = ff // 256
    dims = (n_u, n_b, seqs, td, rows, heads)

    columns = 3 * heads * HD
    n_z = n_b // 2
    own, block = (seqs, td, width), (seqs, tb, width)
    inputs_of = dict(
        x=inputs, vf=v_first, go=grad_out, segments=segments, wq_in=w_query, wk_in=w_key, wv_in=w_value,
        wout=w_out, wg_in=w_gate, wu_in=w_up, wd=w_down, ga=gain_attn, gf=gain_ffn,
    )
    outs = dict(
        out=(own, bf16), gin=(own, bf16), gvf=(own, bf16), gwq=((rows, width), f32), gwk=((rows, width), f32),
        gwv=((rows, width), f32), gwo=((rows, width), f32), gwg=(w_gate.shape, f32), gwu=(w_gate.shape, f32),
        gwd=((ff_own, width), f32), gga=((rows,), f32), ggf=((rows,), f32), stats=((3,), f32),
    )
    scratch = dict(
        gains=((8, LANES), f32), wgu=((n_u, rows, 2 * ff), bf16), cosr=((seqs, tb, LANES), f32),
        sinr=((seqs, tb, LANES), f32), low=((8, seq), jnp.int32),
        dwq=((n_u, rows, columns), bf16), dwgu=((chunks, n_u, rows, 512), bf16), nft=((width, seqs * tb), bf16),
        xg=(block, bf16), vfg=((seqs, tb, heads * HD), bf16), gbuf=((n_b, n_u, 8, LANES), f32),
        gain=((8, width), f32), normed=(block, bf16), wq=((n_u, n_b * rows, columns), bf16),
        gog=(block, bf16), wg=((n_u, n_b * rows, 2 * ff), bf16), wdg=((ff, width), bf16),
        wo=((n_b * rows, width), bf16), stage=((n_b, tb + tb // 2, LANES), bf16),
        units=((n_b, tb + tb // 2, LANES), bf16), keys=((seq, LANES), bf16), key_t=((HD, seq), bf16),
        query=((seq, LANES), bf16), query_t=((LANES, seq), bf16), value=((seq, LANES), bf16),
        value_t=((HD, seq), bf16), acc=((HD, QB), f32), heads_t=((HD, seq), f32), lse=((8, seq), f32),
        ostage=((n_b, tb // 2, LANES), bf16), parts=((n_b, tb // 2, LANES), bf16),
        mix=((seqs, tb, heads * HD), bf16), branch=(block, bf16), landed=((n_u,) + own, bf16),
        sums=((8, width), f32), totals=((8, width), f32), hat=(block, bf16), hidden=(own, f32), nf_own=(own, bf16), nf=(block, bf16),
        act=((seqs, tb, ff), bf16), dgu=((seqs, tb, 2 * ff), bf16), d_low=(block, bf16),
        ghid=(own, f32), gb_own=(own, bf16),
        landed_f=((n_u,) + own, bf16),
        wd_buf=((n_z, 2, ff_pad, width), bf16), wd_pair=((n_z, ff_pad, width), bf16),
        wd_sum=((n_z, ff_pad, width), bf16), wd_land=((n_z, ff_pad, width), bf16),
        wg_buf=((chunks, n_z, 2, n_u, rows, 512), bf16), wg_pair=((chunks, n_z, n_u, rows, 512), bf16),
        wg_sum=((chunks, n_z, n_u, rows, 512), bf16), wg_land=((chunks, n_z, n_u, rows, 512), bf16),
        wg_low=((chunks, n_u, rows, 512), bf16),
        ostage2=((n_b, tb // 2, LANES), bf16), grads=((n_b, tb // 2, LANES), bf16),
        wo_buf=((n_z, 2, rows, width), bf16), wo_pair=((n_z, rows, width), bf16),
        wo_sum=((n_z, rows, width), bf16), wo_land=((n_z, rows, width), bf16),
        grad=((seq, LANES), bf16), grad_t=((LANES, seq), bf16), row_dot=((8, seq), f32),
        dq_t=((HD, seq), f32), dk=((seq, LANES), f32), dv=((seq, LANES), f32),
        returned=((n_b, tb + tb // 2, LANES), bf16), raw=((seqs, tb, columns), bf16),
        gv=((n_u, seqs, td, heads * HD), bf16),
        wq_buf=((n_z, 2, n_u, rows, columns), bf16), wq_pair=((n_z, n_u, rows, columns), bf16),
        wq_sum=((n_z, n_u, rows, columns), bf16), wq_land=((n_z, n_u, rows, columns), bf16),
        wq_low=((n_u, rows, columns), bf16), sums_u=((n_u, 8, width), f32), sums_b=((n_b, 8, width), f32),
    )
    names = [*inputs_of, *outs, *scratch, "send_sems", "recv_sems"]
    vmem = pl.BlockSpec(memory_space=pltpu.VMEM)
    results = pl.pallas_call(
        functools.partial(layer_kernel, dims, names),
        out_shape=[jax.ShapeDtypeStruct(shape, dtype) for shape, dtype in outs.values()],
        in_specs=[vmem] * len(inputs_of),
        out_specs=[vmem] * len(outs),
        scratch_shapes=[pltpu.VMEM(shape, dtype) for shape, dtype in scratch.values()]
        + [pltpu.SemaphoreType.DMA((SEMAPHORES,))] * 2,
        compiler_params=pltpu.CompilerParams(
            collective_id=1, has_side_effects=True, vmem_limit_bytes=VMEM_BYTES
        ),
        name="layer",
    )(*inputs_of.values())
    return pl.pallas_call(
        functools.partial(hand_out_kernel, len(outs)),
        out_shape=[jax.ShapeDtypeStruct(shape, dtype) for shape, dtype in outs.values()],
        in_specs=[vmem] * len(outs),
        out_specs=[vmem] * len(outs),
        name="hand_out",
    )(*results)


SEMAPHORES = 288


def fits_units(mesh):
    return mesh.shape["ulysses"] == 4 and mesh.shape["blk"] == 8


def solution(mesh):
    in_specs = (
        P(None, ("blk", "ulysses"), None),
        P(None, ("blk", "ulysses"), None),
        P(None, ("blk", "ulysses"), None),
        P(None, ("blk", "ulysses")),
        P(),
        P(("ulysses", "blk"), None),
        P(("ulysses", "blk"), None),
        P(("ulysses", "blk"), None),
        P(("ulysses", "blk"), None),
        P(("ulysses", "blk"), None),
        P(("ulysses", "blk"), None),
        P(("ulysses", "blk"), None),
        P(("ulysses", "blk")),
        P(("ulysses", "blk")),
    )
    out_specs = (
        P(None, ("blk", "ulysses"), None),
        P(None, ("blk", "ulysses"), None),
        P(None, ("blk", "ulysses"), None),
        P(("ulysses", "blk"), None),
        P(("ulysses", "blk"), None),
        P(("ulysses", "blk"), None),
        P(("ulysses", "blk"), None),
        P(("ulysses", "blk"), None),
        P(("ulysses", "blk"), None),
        P(("ulysses", "blk"), None),
        P(("ulysses", "blk")),
        P(("ulysses", "blk")),
        P(),
    )
    path = local_units if fits_units(mesh) else local
    return jax.shard_map(path, mesh=mesh, in_specs=in_specs, out_specs=out_specs, check_vma=False)
```
